32 devices in a mesh: dp: 8 (over z, y), tensor: 4 (over x, core).
Axes of the slice: x: 2, y: 2, z: 4, core: 2. Of those that a mesh axis runs over, the one named last changes fastest.
Arguments:
- tokens: bfloat16 [16384, 1280], P(('dp', 'tensor')), may hold values from -6 to 6
- cotangent: bfloat16 [16384, 1280], P(('dp', 'tensor')), may hold values from -6 to 6
- block_ids: int32 [8, 2048], P('dp'), may hold values from 0 to 15, never falling along the last dimension, each value on 1 to 256 neighbouring positions
- attn_gain: float32 [1280], replicated, may hold values from 0.5 to 1.5
- w_query: bfloat16 [1280, 1280], P('dp', 'tensor'), may hold values from -0.15625 to 0.15625
- w_key: bfloat16 [1280, 1280], P('dp', 'tensor'), may hold values from -0.15625 to 0.15625
- w_value: bfloat16 [1280, 1280], P('dp', 'tensor'), may hold values from -0.15625 to 0.15625
- query_scale: float32 [80], replicated, may hold values from 0.5 to 2.5
- w_out: bfloat16 [1280, 1280], P('tensor', 'dp'), may hold values from -0.5 to 0.5
- mlp_gain: float32 [1280], replicated, may hold values from 0.5 to 1.5
- w_up: bfloat16 [1280, 1280], P('dp', 'tensor'), may hold values from -0.15625 to 0.15625
- b_up: float32 [1280], replicated, may hold values from -3 to 3
- w_down: bfloat16 [1280, 1280], P('tensor', 'dp'), may hold values from -0.25 to 0.25
- b_down: float32 [1280], replicated, may hold values from -3 to 3
Outputs:
- output: bfloat16 [16384, 1280], P(('dp', 'tensor'))
- d_tokens: bfloat16 [16384, 1280], P(('dp', 'tensor'))
- d_attn_gain: float32 [1280], replicated
- d_w_query: float32 [1280, 1280], P('dp', 'tensor')
- d_w_key: float32 [1280, 1280], P('dp', 'tensor')
- d_w_value: float32 [1280, 1280], P('dp', 'tensor')
- d_query_scale: float32 [80], replicated
- d_w_out: float32 [1280, 1280], P('tensor', 'dp')
- d_mlp_gain: float32 [1280], replicated
- d_w_up: float32 [1280, 1280], P('dp', 'tensor')
- d_b_up: float32 [1280], replicated
- d_w_down: float32 [1280, 1280], P('tensor', 'dp')
- d_b_down: float32 [1280], replicated
The draws below stay inside these ranges and needn't reach their ends.
Inputs may be any that keep to these rules, and one draw needn't show every extreme that they name: `block_ids`: in each sequence the block numbers never fall along positions, each number from 0 to 15 appears, a block spans 1 to 256 positions, and one block spans exactly 256.
All inputs are finite; a program needn't handle non-finite values.
Results may differ from the reference program's by a relative error of at most 0.014.
The reference program's roundings to bfloat16 on the way count: a program that leaves them out, or rounds other values in their place, can miss the bound.
Values may be sent and summed in bfloat16 or wider, within the bound.
A program may use at most 192 MiB of HBM per device.

```python
import math
import jax
import jax.numpy as jnp
import numpy as np
from jax import lax

D = 1280
H = 16
HD = 80
FF = 1280
BLOCK_MOST = 256
SEQS = 8
SEQ_LEN = 2048
TOKENS = 16384
BLOCKS = 16


def block_scale(stream_key, shape, pieces, low, largest):
    level, own = 1.0, jax.random.fold_in(stream_key, 6)
    for axis_at, shards_of in pieces:
        draws = jnp.exp(jax.random.uniform(jax.random.fold_in(own, axis_at), (shards_of,), jnp.float32, low / len(pieces), largest / len(pieces)))
        level = level * jnp.repeat(draws, shape[axis_at] // shards_of).reshape([-1 if axis == axis_at else 1 for axis in range(len(shape))])
    return level


def length_profile(count, total, most, skew):
    loads = [(1 << 20) // math.isqrt(standing ** skew) + 1 for standing in range(2, count + 1)]
    spare, counts = total - most - (count - 1), [1] * (count - 1)
    while spare > 0:
        free = [i for i in range(count - 1) if counts[i] < most]
        mass, left = sum([loads[i] for i in free]), spare
        for i in free:
            more = min(most - counts[i], max(1, left * loads[i] // mass), spare)
            counts[i] = counts[i] + more
            spare = spare - more
    return np.array([most] + counts)


def ragged(rng, number_of, total, bound, lean):
    if number_of == 2:
        one = jax.random.randint(rng, (), max(1, total - bound), min(bound, total - 1) + 1)
        return jnp.stack([one, total - one])
    sizes = jnp.asarray(length_profile(number_of, total, bound, lean), jnp.int32)
    pairs = (number_of - 1) // 2
    donor, taker = sizes[1:1 + 2 * pairs:2], sizes[2:2 + 2 * pairs:2]
    margin = jnp.minimum(donor - 1, bound - taker)
    moved = jax.random.randint(jax.random.fold_in(rng, 1), (pairs,), 0, 1 << 20) % (margin + 1)
    sizes = sizes.at[1:1 + 2 * pairs:2].set(donor - moved).at[2:2 + 2 * pairs:2].set(taker + moved)
    return sizes[jax.random.permutation(jax.random.fold_in(rng, 2), number_of)]


def noise(own_key, extent, spread, limit, split=(), dtype=jnp.bfloat16):
    drawn = jax.random.normal(own_key, extent, jnp.float32) * spread
    if len(split) > 0:
        drawn = block_scale(own_key, extent, split, -0.22, 0.18) * drawn
    return jnp.clip(drawn, min=-limit, max=limit).astype(dtype)


def setup_inputs(seed: int = 0) -> dict:
    key_list = jax.random.split(jax.random.key(seed), 15)
    tokens = noise(key_list[0], (TOKENS, D), 1.0, 6.0, ((0, 32),))
    cotangent = noise(key_list[1], (TOKENS, D), 1.0, 6.0, ((0, 32),))
    block_ids = jax.vmap(lambda own: jnp.searchsorted(jnp.cumsum(ragged(own, BLOCKS, SEQ_LEN, BLOCK_MOST, 1)), jnp.arange(SEQ_LEN), side="right"))(jax.random.split(key_list[2], SEQS)).reshape((SEQS, SEQ_LEN)).astype(jnp.int32)
    attn_gain = jnp.clip(1.0 + 0.1 * jax.random.normal(key_list[3], (D,), jnp.float32), 0.5, 1.5)
    w_query = noise(key_list[4], (D, H * HD), D ** -0.5, 0.15625, ((0, 8), (1, 4)))
    w_key = noise(key_list[5], (D, H * HD), D ** -0.5, 0.15625, ((0, 8), (1, 4)))
    w_value = noise(key_list[6], (D, H * HD), D ** -0.5, 0.15625, ((0, 8), (1, 4)))
    query_scale = jnp.clip(jax.random.uniform(key_list[7], (HD,), jnp.float32, 0.5, 2.5), 0.5, 2.5)
    w_out = noise(key_list[8], (H * HD, D), (H * HD // 8) ** -0.5, 0.5, ((0, 4), (1, 8)))
    mlp_gain = jnp.clip(1.0 + 0.1 * jax.random.normal(key_list[9], (D,), jnp.float32), 0.5, 1.5)
    w_up = noise(key_list[10], (D, FF), D ** -0.5, 0.15625, ((0, 8), (1, 4)))
    b_up = noise(key_list[11], (FF,), 0.5, 3.0, (), jnp.float32)
    w_down = noise(key_list[12], (FF, D), (FF // 2) ** -0.5, 0.25, ((0, 4), (1, 8)))
    b_down = noise(key_list[13], (D,), 0.5, 3.0, (), jnp.float32)
    return dict(tokens=tokens, cotangent=cotangent, block_ids=block_ids, attn_gain=attn_gain, w_query=w_query, w_key=w_key, w_value=w_value, query_scale=query_scale, w_out=w_out, mlp_gain=mlp_gain, w_up=w_up, b_up=b_up, w_down=w_down, b_down=b_down)


@jax.custom_vjp
def low(v):
    return lax.optimization_barrier(v.astype(jnp.bfloat16)).astype(jnp.float32)

@jax.custom_vjp
def low_back(v):
    return v

def low_keep(v):
    return (low(v), None)

def low_pass(kept, grad):
    return (grad,)

def back_keep(v):
    return (v, None)

def back_low(kept, grad):
    return (low(grad),)
low.defvjp(low_keep, low_pass)
low_back.defvjp(back_keep, back_low)
HIGHEST = lax.Precision.HIGHEST
EPSILON = 1e-06
SCORE_BASE = 1.442695041
MASKED = -1e+30

def matmul(left_side, right_side):
    return jnp.dot(left_side, right_side, precision=HIGHEST)

def rms_norm(values_in, gain):
    return values_in * lax.rsqrt(lax.optimization_barrier(jnp.mean(values_in * values_in, axis=-1, keepdims=True)) + EPSILON) * gain

def softplus_of(values_in):
    return jnp.log1p(jnp.exp(values_in))

def attend_block(query_block, query_ids, key_all, value_all, key_ids):
    scores = jnp.einsum('qhd,khd->hqk', query_block, key_all, precision=HIGHEST)
    scores = low_back(scores)
    visible = query_ids[:, None] >= key_ids[None, :]
    scores = jnp.where(visible[None], scores, MASKED)
    highest = lax.optimization_barrier(jnp.max(scores, axis=-1, keepdims=True))
    weights = jnp.exp(scores - highest)
    probs = weights / lax.optimization_barrier(jnp.sum(weights, axis=-1, keepdims=True))
    return jnp.einsum('hqk,khd->qhd', low(probs), value_all, precision=HIGHEST)

def layer(params, sequence, seq_ids):
    attn_gain, w_query, w_key, w_value, query_scale, w_out, mlp_gain, w_up, b_up, w_down, b_down = params
    length = sequence.shape[0]
    normed = low(rms_norm(sequence, attn_gain))
    factor = SCORE_BASE / math.sqrt(HD) * softplus_of(query_scale)
    queries = low_back(matmul(normed, w_query)).reshape(length, H, HD)
    queries = low(queries * factor)
    keys_all = low(low_back(matmul(normed, w_key))).reshape(length, H, HD)
    values_all = low(low_back(matmul(normed, w_value))).reshape(length, H, HD)
    block_rows = min(512, length)
    count_blocks = length // block_rows
    attended = lax.map(lambda block_pair: jax.checkpoint(attend_block)(block_pair[0], block_pair[1], keys_all, values_all, seq_ids), (queries.reshape(count_blocks, block_rows, H, HD), seq_ids.reshape(count_blocks, block_rows)))
    attended = low_back(low(attended.reshape(length, H * HD)))
    hidden_state = sequence + low_back(matmul(attended, w_out))
    normed_mlp = low(rms_norm(hidden_state, mlp_gain))
    pre_act = low_back(matmul(normed_mlp, w_up) + b_up)
    activation = low(pre_act * jax.nn.sigmoid(pre_act))
    return hidden_state + matmul(activation, w_down) + b_down

def reference(tokens, cotangent, block_ids, attn_gain, w_query, w_key, w_value, query_scale, w_out, mlp_gain, w_up, b_up, w_down, b_down):
    params = tuple((argument.astype(jnp.float32) for argument in (attn_gain, w_query, w_key, w_value, query_scale, w_out, mlp_gain, w_up, b_up, w_down, b_down)))
    inputs = tokens.astype(jnp.float32).reshape(SEQS, SEQ_LEN, D)
    cotangents = cotangent.astype(jnp.float32).reshape(SEQS, SEQ_LEN, D)

    def one_sequence(summed, scan_entry):
        sequence, seq_cot, seq_ids = scan_entry
        result, pullback = jax.vjp(lambda weights, inputs_seq: layer(weights, inputs_seq, seq_ids), params, sequence)
        weight_grads, input_grad = pullback(seq_cot)
        return (jax.tree.map(jnp.add, summed, weight_grads), (result, input_grad))
    initial = tuple((jnp.zeros_like(argument) for argument in params))
    totals, (results, input_grads) = lax.scan(one_sequence, initial, (inputs, cotangents, block_ids))
    return (results.reshape(TOKENS, D).astype(jnp.bfloat16), input_grads.reshape(TOKENS, D).astype(jnp.bfloat16), totals[0], totals[1], totals[2], totals[3], totals[4], totals[5], totals[6], totals[7], totals[8], totals[9], totals[10])
```

```python
import math

import jax
import jax.numpy as jnp
from jax import lax
from jax.experimental import pallas as pl
from jax.experimental.pallas import tpu as pltpu
from jax.sharding import PartitionSpec as P

HD = 80
HP = 128
TILE = 256
BLOCK_MOST = 256
EPSILON = 1e-06
SCORE_BASE = 1.442695041
MASKED = -1e30
BF = jnp.bfloat16
F32 = jnp.float32


def mm(a, b, ca, cb):
    return lax.dot_general(a, b, (((ca,), (cb,)), ((), ())), preferred_element_type=F32)


def reach(tile, length):
    return min((tile + 1) * TILE + BLOCK_MOST, length)


def attend_kernel(q_ref, k_ref, v_ref, idr_ref, idc_ref, o_ref, lse_ref, vt_ref):
    length = q_ref.shape[0]
    tiles = length // TILE
    sub = lax.broadcasted_iota(jnp.int32, (HP, length), 0)
    vt_ref[...] = jnp.where(sub == HD, 1.0, v_ref[...].astype(F32).T).astype(BF)

    def scores(t):
        seen, low = reach(t, length), t * TILE
        st = mm(k_ref[:seen, :], q_ref[low : low + TILE, :], 1, 1)
        visible = idc_ref[low:seen, :] <= idr_ref[:, low : low + TILE]
        masked = jnp.where(visible, st[low:], MASKED)
        return jnp.concatenate([st[:low], masked], 0) if low else masked

    st = scores(0)
    for t in range(tiles):
        later = scores(t + 1) if t + 1 < tiles else None
        seen, low = st.shape[0], t * TILE
        group = jnp.max(st.reshape(seen // 64, 64, TILE), axis=0)
        highest = jnp.max(group, axis=0, keepdims=True)
        weights = jnp.exp(st - highest).astype(BF)
        ot = mm(vt_ref[:, :seen], weights, 1, 0)
        summed = ot[HD : HD + 1, :]
        o_ref[low : low + TILE, :] = (ot * (1.0 / summed)).T.astype(BF)
        lse_ref[0, :, low : low + TILE] = highest + jnp.log(summed)
        st = later


def attend(q, k, v, idr, idc):
    length, wide = q.shape
    heads = wide // HP
    col = pl.BlockSpec((length, HP), lambda h: (0, h))
    return pl.pallas_call(
        attend_kernel,
        grid=(heads,),
        out_shape=[
            jax.ShapeDtypeStruct((length, wide), BF),
            jax.ShapeDtypeStruct((heads, 1, length), F32),
        ],
        in_specs=[
            col,
            col,
            col,
            pl.BlockSpec((1, length), lambda h: (0, 0)),
            pl.BlockSpec((length, 1), lambda h: (0, 0)),
        ],
        out_specs=[col, pl.BlockSpec((1, 1, length), lambda h: (h, 0, 0))],
        scratch_shapes=[pltpu.VMEM((HP, length), BF)],
        compiler_params=pltpu.CompilerParams(vmem_limit_bytes=56 << 20),
        cost_estimate=pl.CostEstimate(
            flops=heads * length * length * 2 * 256 * 2, bytes_accessed=8 << 20, transcendentals=0
        ),
    )(q, k, v, idr, idc)


def attend_back_kernel(
    q_ref, k_ref, v_ref, o_ref, do_ref, lse_ref, fac_ref, idr_ref, idc_ref,
    dq_ref, dk_ref, dv_ref, qs_ref, dka, dva, kt_ref,
):
    length = q_ref.shape[0]
    tiles = length // TILE
    kt_ref[...] = k_ref[...].astype(F32).T.astype(BF)
    dka[...] = jnp.zeros_like(dka)
    dva[...] = jnp.zeros_like(dva)
    scale_sum = jnp.zeros((1, HP), F32)
    for t in range(tiles):
        seen, low = reach(t, length), t * TILE
        rows = slice(low, low + TILE)
        qt = q_ref[rows, :]
        dot_ = do_ref[rows, :]
        delta = jnp.sum((dot_.astype(F32) * o_ref[rows, :].astype(F32)).T, axis=0, keepdims=True)
        st = mm(k_ref[:seen, :], qt, 1, 1)
        p = jnp.exp(st - lse_ref[0, :, rows])
        visible = idc_ref[low:seen, :] <= idr_ref[:, rows]
        pm = jnp.where(visible, p[low:], 0.0)
        p = jnp.concatenate([p[:low], pm], 0) if low else pm
        dp = mm(v_ref[:seen, :], dot_, 1, 1)
        ds = (p * (dp - delta)).astype(BF)
        dva[:seen, :] += mm(p.astype(BF), dot_, 1, 0)
        dka[:seen, :] += mm(ds, qt, 1, 0)
        dq = mm(kt_ref[:, :seen], ds, 1, 0).T
        scale_sum = scale_sum + jnp.sum(dq * qt.astype(F32), axis=0, keepdims=True)
        dq_ref[rows, :] = (dq * fac_ref[...]).astype(BF)
    dk_ref[...] = dka[...].astype(BF)
    dv_ref[...] = dva[...].astype(BF)
    qs_ref[0] = scale_sum


def attend_back(q, k, v, o, do, lse, factor, idr, idc):
    length, wide = q.shape
    heads = wide // HP
    col = pl.BlockSpec((length, HP), lambda h: (0, h))
    return pl.pallas_call(
        attend_back_kernel,
        grid=(heads,),
        out_shape=[jax.ShapeDtypeStruct((length, wide), BF)] * 3
        + [jax.ShapeDtypeStruct((heads, 1, HP), F32)],
        in_specs=[
            col, col, col, col, col,
            pl.BlockSpec((1, 1, length), lambda h: (h, 0, 0)),
            pl.BlockSpec((1, HP), lambda h: (0, 0)),
            pl.BlockSpec((1, length), lambda h: (0, 0)),
            pl.BlockSpec((length, 1), lambda h: (0, 0)),
        ],
        out_specs=[col, col, col, pl.BlockSpec((1, 1, HP), lambda h: (h, 0, 0))],
        scratch_shapes=[pltpu.VMEM((length, HP), F32)] * 2 + [pltpu.VMEM((HP, length), BF)],
        compiler_params=pltpu.CompilerParams(vmem_limit_bytes=56 << 20),
        cost_estimate=pl.CostEstimate(
            flops=heads * length * length * 2 * 256 * 4, bytes_accessed=16 << 20, transcendentals=0
        ),
    )(q, k, v, o, do, lse, factor, idr, idc)


def swap(v, axis, size, mask):
    return lax.ppermute(v, axis, [(i, i ^ mask) for i in range(size)])


def gather_dp(shard, size):
    if size != 8:
        return lax.all_gather(shard, "dp", axis=0)
    far, here = size // 2, lax.axis_index("dp")
    major, minor = here // 2, here % 2
    parts = [shard]
    for step in range(1, far):
        parts.append(
            lax.ppermute(shard, "dp", [(i, (i + 2 * step) % size) for i in range(size)])
        )
    others = [swap(part, "dp", size, 1) for part in parts]
    whole = jnp.zeros((size,) + shard.shape, shard.dtype)
    for step in range(far):
        source = ((major + far - step) % far) * 2
        whole = lax.dynamic_update_slice(whole, parts[step][None], (source + minor, 0, 0))
        whole = lax.dynamic_update_slice(whole, others[step][None], (source + 1 - minor, 0, 0))
    return whole


def scatter_dp(grad, size):
    if size != 8:
        return lax.psum_scatter(grad, "dp", scatter_dimension=0, tiled=False)
    far, here = size // 2, lax.axis_index("dp")
    major, minor = here // 2, here % 2
    split = grad.reshape((far, 2) + grad.shape[1:])
    mine = lax.dynamic_index_in_dim(split, minor, 1, keepdims=False)
    theirs = lax.dynamic_index_in_dim(split, 1 - minor, 1, keepdims=False)
    half = mine + swap(theirs.astype(BF), "dp", size, 1).astype(F32)
    total = lax.dynamic_index_in_dim(half, major, 0, keepdims=False)
    for step in range(1, far):
        piece = lax.dynamic_index_in_dim(half, (major + step) % far, 0, keepdims=False)
        total = total + lax.ppermute(
            piece.astype(BF), "dp", [(i, (i + 2 * step) % size) for i in range(size)]
        ).astype(F32)
    return total


def sum_all(v, dp, tensor):
    if dp != 8:
        return lax.psum(v, ("dp", "tensor"))
    v = v + swap(v, "tensor", tensor, 1)
    v = v + swap(v, "tensor", tensor, 2)
    v = v + swap(v, "dp", dp, 1)
    parts = [lax.ppermute(v, "dp", [(i, (i + 2 * s) % dp) for i in range(dp)]) for s in (1, 2, 3)]
    here = lax.axis_index("dp") // 2
    stack = jnp.zeros((4,) + v.shape, v.dtype)
    for s, part in enumerate([v] + parts):
        stack = lax.dynamic_update_slice(stack, part[None], ((here + 4 - s) % 4,) + (0,) * v.ndim)
    return (stack[0] + stack[1]) + (stack[2] + stack[3])


def pad_heads(w):
    rows, cols = w.shape
    w = w.reshape(rows, cols // HD, HD)
    return jnp.pad(w, ((0, 0), (0, 0), (0, HP - HD))).reshape(rows, cols // HD * HP)


def trim_heads(w):
    rows, cols = w.shape
    return w.reshape(rows, cols // HP, HP)[:, :, :HD].reshape(rows, cols // HP * HD)


def rms_stats(v):
    inverse = lax.rsqrt(jnp.mean(v * v, axis=-1, keepdims=True) + EPSILON)
    return v * inverse, inverse


def rms_back(grad, hat, inverse, gain):
    scaled = grad * gain
    return inverse * (scaled - hat * jnp.mean(scaled * hat, axis=-1, keepdims=True))


def body(dp, tensor, tokens, cotangent, block_ids, attn_gain, w_query, w_key, w_value,
         query_scale, w_out, mlp_gain, w_up, b_up, w_down, b_down):
    assert tensor == 4
    here = lax.axis_index("tensor")
    rows, width = tokens.shape
    length = rows * tensor
    cols = w_query.shape[1]
    heads = cols // HD
    order = [here, here ^ 2, here ^ 1, here ^ 3]

    tokens_f32 = tokens.astype(F32)
    hat_one, inverse_one = rms_stats(tokens_f32)
    normed_own = (hat_one * attn_gain).astype(BF)
    normed_x = swap(normed_own, "tensor", tensor, 2)
    blocks = [normed_own, normed_x, swap(normed_own, "tensor", tensor, 1)]
    blocks.append(swap(normed_x, "tensor", tensor, 1))
    normed = jnp.zeros((length, width), BF)
    for at, block in zip(order, blocks):
        normed = lax.dynamic_update_slice(normed, block, (at * rows, 0))

    first = jnp.concatenate([w_query, w_key, w_value], axis=1)
    second = jnp.concatenate([w_out.T, w_up, w_down.T], axis=1)
    full_qkv = gather_dp(first, dp).reshape(width, 3 * cols)
    pair = jnp.concatenate([second, swap(second, "tensor", tensor, 2)], axis=1)
    half = gather_dp(pair, dp).reshape(width, 6 * cols)
    both = swap(half, "tensor", tensor, 1)

    def wide(at):
        return jnp.concatenate(
            [
                half[:, at * cols : (at + 1) * cols],
                half[:, (3 + at) * cols : (4 + at) * cols],
                both[:, at * cols : (at + 1) * cols],
                both[:, (3 + at) * cols : (4 + at) * cols],
            ],
            axis=1,
        )

    out_t, up, down_t = wide(0), wide(1), wide(2)
    wq, wk, wv = (pad_heads(full_qkv[:, i * cols : (i + 1) * cols]) for i in range(3))

    softplus = jnp.log1p(jnp.exp(query_scale))
    factor = SCORE_BASE / math.sqrt(HD) * softplus
    factor_pad = jnp.pad(factor, (0, HP - HD))[None, :]
    queries = (mm(normed, wq, 1, 0) * jnp.tile(factor_pad, (1, heads))).astype(BF)
    keys = mm(normed, wk, 1, 0).astype(BF)
    values = mm(normed, wv, 1, 0).astype(BF)
    idr = block_ids
    idc = block_ids.reshape(length, 1)
    attended, lse = attend(queries, keys, values, idr, idc)

    def trade(blocks_of):
        return [
            blocks_of(here),
            swap(blocks_of(order[1]), "tensor", tensor, 2),
            swap(blocks_of(order[2]), "tensor", tensor, 1),
            swap(blocks_of(order[3]), "tensor", tensor, 3),
        ]

    compact = trim_heads(attended)
    mine = jnp.concatenate(
        trade(lambda at: lax.dynamic_slice(compact, (at * rows, 0), (rows, cols))), axis=1
    )
    hidden = tokens_f32 + mm(mine, out_t, 1, 1)

    b_rel = jnp.concatenate([lax.dynamic_slice(b_up, (at * cols,), (cols,)) for at in order])
    cot_f32 = cotangent.astype(F32)
    grad_act = mm(cotangent, down_t, 1, 0)
    hat_two, inverse_two = rms_stats(hidden)
    normed_two = (hat_two * mlp_gain).astype(BF)
    pre = mm(normed_two, up, 1, 0) + b_rel
    sig = jax.nn.sigmoid(pre)
    activation = (pre * sig).astype(BF)
    d_pre = (grad_act * sig * (1.0 + pre * (1.0 - sig))).astype(BF)
    d_normed_two = mm(d_pre, up, 1, 1)
    d_hidden = cot_f32 + rms_back(d_normed_two, hat_two, inverse_two, mlp_gain)
    branch = d_hidden.astype(BF)
    d_mine = mm(branch, out_t, 1, 0).astype(BF)
    received = [
        d_mine[:, :cols],
        swap(d_mine[:, cols : 2 * cols], "tensor", tensor, 2),
        swap(d_mine[:, 2 * cols : 3 * cols], "tensor", tensor, 1),
        swap(d_mine[:, 3 * cols :], "tensor", tensor, 3),
    ]
    d_attended = jnp.zeros((length, cols), BF)
    for at, block in zip(order, received):
        d_attended = lax.dynamic_update_slice(d_attended, block, (at * rows, 0))
    d_attended = pad_heads(d_attended)

    output = (hidden + mm(activation, down_t, 1, 1) + b_down).astype(BF)
    d_down_t = mm(cotangent, activation, 0, 0)
    d_up = mm(normed_two, d_pre, 0, 0)
    d_out_t = mm(branch, mine, 0, 0)
    d_mlp_gain = jnp.sum(d_normed_two * hat_two, axis=0)
    d_b_rel = jnp.sum(d_pre.astype(F32), axis=0)
    d_b_up = jnp.zeros_like(b_up)
    for i, at in enumerate(order):
        d_b_up = lax.dynamic_update_slice(d_b_up, d_b_rel[i * cols : (i + 1) * cols], (at * cols,))
    d_b_down = jnp.sum(cot_f32, axis=0)
    early = sum_all(jnp.stack([d_mlp_gain, d_b_up, d_b_down]), dp, tensor)

    keep = jnp.concatenate([g[:, : 2 * cols] for g in (d_out_t, d_up, d_down_t)], axis=1)
    give = jnp.concatenate([g[:, 2 * cols :] for g in (d_out_t, d_up, d_down_t)], axis=1)
    keep = keep + swap(give.astype(BF), "tensor", tensor, 1).astype(F32)
    kept = scatter_dp(keep.reshape(dp, width // dp, 6 * cols), dp)
    kept = kept.reshape(width // dp, 3, 2, cols)
    second_grads = kept[:, :, 0] + swap(kept[:, :, 1].astype(BF), "tensor", tensor, 2).astype(F32)
    s_out, s_up, s_down = second_grads[:, 0].T, second_grads[:, 1], second_grads[:, 2].T

    dq, dk, dv, q_sums = attend_back(
        queries, keys, values, attended, d_attended, lse, factor_pad, idr, idc
    )
    d_scale = jnp.sum(q_sums[:, 0, :HD], axis=0) / softplus * jax.nn.sigmoid(query_scale)

    def part(at):
        return sum(
            mm(lax.dynamic_slice(d, (at * rows, 0), (rows, d.shape[1])), w, 1, 1)
            for d, w in ((dq, wq), (dk, wk), (dv, wv))
        )

    far_same = part(order[1])
    far_other = part(order[3])
    near_same = part(order[0])
    near_other = part(order[2])
    from_x_same = swap(far_same.astype(BF), "tensor", tensor, 2).astype(F32)
    from_x_other = swap(far_other.astype(BF), "tensor", tensor, 2).astype(F32)
    chip_other = near_other + from_x_other
    d_normed = near_same + from_x_same + swap(chip_other.astype(BF), "tensor", tensor, 1).astype(F32)

    d_wq, d_wk, d_wv = (mm(normed, d, 0, 0) for d in (dq, dk, dv))
    w_dot = sum(
        jnp.sum(g * w.astype(F32), axis=1) for g, w in ((d_wq, wq), (d_wk, wk), (d_wv, wv))
    )
    late = jnp.concatenate([w_dot / attn_gain, jnp.pad(d_scale, (0, HP - HD))])
    late = sum_all(late.reshape(-1, HP), dp, tensor).reshape(-1)
    qkv_grad = jnp.concatenate([trim_heads(g) for g in (d_wq, d_wk, d_wv)], axis=1)
    s_qkv = scatter_dp(qkv_grad.reshape(dp, width // dp, 3 * cols), dp)

    d_tokens = (d_hidden + rms_back(d_normed, hat_one, inverse_one, attn_gain)).astype(BF)
    return (
        output,
        d_tokens,
        late[:width],
        s_qkv[:, :cols],
        s_qkv[:, cols : 2 * cols],
        s_qkv[:, 2 * cols :],
        late[width : width + HD],
        s_out,
        early[0],
        s_up,
        early[1],
        s_down,
        early[2],
    )


def solution(mesh):
    weight, turned, whole = P("dp", "tensor"), P("tensor", "dp"), P()
    positions = P(("dp", "tensor"), None)
    return jax.shard_map(
        lambda *args: body(mesh.shape["dp"], mesh.shape["tensor"], *args),
        mesh=mesh,
        in_specs=(positions, positions, P("dp", None), whole, weight, weight, weight, whole,
                  turned, whole, weight, whole, turned, whole),
        out_specs=(positions, positions, whole, weight, weight, weight, whole, turned, whole,
                   weight, whole, turned, whole),
        check_vma=False,
    )
```

```python
import math

import jax
import jax.numpy as jnp
from jax import lax
from jax.experimental import pallas as pl
from jax.experimental.pallas import tpu as pltpu
from jax.sharding import PartitionSpec as P

HD = 80
HP = 128
TILE = 256
BLOCK_MOST = 256
EPSILON = 1e-06
SCORE_BASE = 1.442695041
MASKED = -1e30
BF = jnp.bfloat16
F32 = jnp.float32


def mm(a, b, ca, cb):
    return lax.dot_general(a, b, (((ca,), (cb,)), ((), ())), preferred_element_type=F32)


def reach(tile, length):
    return min((tile + 1) * TILE + BLOCK_MOST, length)


def attend_back_kernel(
    q_ref, k_ref, v_ref, o_ref, do_ref, lse_ref, fac_ref, idr_ref, idc_ref,
    dq_ref, dk_ref, dv_ref, qs_ref, dka, dva, kt_ref,
):
    q_ref, k_ref, v_ref = q_ref.at[0], k_ref.at[0], v_ref.at[0]
    length = q_ref.shape[0]
    tiles = length // TILE
    kt_ref[...] = k_ref[...].astype(F32).T.astype(BF)
    dka[...] = jnp.zeros_like(dka)
    dva[...] = jnp.zeros_like(dva)
    scale_sum = jnp.zeros((1, HP), F32)
    for t in range(tiles):
        seen, low = reach(t, length), t * TILE
        rows = slice(low, low + TILE)
        qt = q_ref[rows, :]
        dot_ = do_ref[rows, :]
        delta = jnp.sum(
            dot_.astype(F32).T[:HD] * o_ref[0, :, rows].astype(F32), axis=0, keepdims=True
        )
        st = mm(k_ref[:seen, :], qt, 1, 1)
        p = jnp.exp(st - lse_ref[0, :, rows])
        visible = idc_ref[low:seen, :] <= idr_ref[:, rows]
        pm = jnp.where(visible, p[low:], 0.0)
        p = jnp.concatenate([p[:low], pm], 0) if low else pm
        dp = mm(v_ref[:seen, :], dot_, 1, 1)
        ds = (p * (dp - delta)).astype(BF)
        dva[:seen, :] += mm(p.astype(BF), dot_, 1, 0)
        dka[:seen, :] += mm(ds, qt, 1, 0)
        dq = mm(kt_ref[:, :seen], ds, 1, 0).T
        scale_sum = scale_sum + jnp.sum(dq * qt.astype(F32), axis=0, keepdims=True)
        dq_ref[rows, :] = (dq * fac_ref[...]).astype(BF)
    dk_ref[...] = dka[...].astype(BF)
    dv_ref[...] = dva[...].astype(BF)
    qs_ref[0] = scale_sum


def attend_back(q, k, v, o, do, lse, factor, idr, idc):
    heads, length, _ = q.shape
    wide = heads * HP
    col = pl.BlockSpec((length, HP), lambda h: (0, h))
    head = pl.BlockSpec((1, length, HP), lambda h: (h, 0, 0))
    return pl.pallas_call(
        attend_back_kernel,
        grid=(heads,),
        out_shape=[jax.ShapeDtypeStruct((length, wide), BF)] * 3
        + [jax.ShapeDtypeStruct((heads, 1, HP), F32)],
        in_specs=[
            head, head, head, pl.BlockSpec((1, HD, length), lambda h: (h, 0, 0)), col,
            pl.BlockSpec((1, 1, length), lambda h: (h, 0, 0)),
            pl.BlockSpec((1, HP), lambda h: (0, 0)),
            pl.BlockSpec((1, length), lambda h: (0, 0)),
            pl.BlockSpec((length, 1), lambda h: (0, 0)),
        ],
        out_specs=[col, col, col, pl.BlockSpec((1, 1, HP), lambda h: (h, 0, 0))],
        scratch_shapes=[pltpu.VMEM((length, HP), F32)] * 2 + [pltpu.VMEM((HP, length), BF)],
        compiler_params=pltpu.CompilerParams(vmem_limit_bytes=56 << 20),
        cost_estimate=pl.CostEstimate(
            flops=heads * length * length * 2 * 256 * 4, bytes_accessed=16 << 20, transcendentals=0
        ),
    )(q, k, v, o, do, lse, factor, idr, idc)


MESH = pl.DeviceIdType.MESH
PARTNERS = (2, 1, 3)
SLOT = {0: 0, 2: 1, 1: 2, 3: 3}


def remote(src, dst, send, recv, where):
    return pltpu.make_async_remote_copy(
        src_ref=src, dst_ref=dst, send_sem=send, recv_sem=recv, device_id=where, device_id_type=MESH
    )


def greet(peers):
    barrier = pltpu.get_barrier_semaphore()
    for where in peers:
        pl.semaphore_signal(barrier, inc=1, device_id=where, device_id_type=MESH)
    pl.semaphore_wait(barrier, len(peers))


def front_kernel(
    dp, far, tok_ref, gain_ref, w1_ref, w2_ref, fac_ref, idr_ref, idc_ref,
    q_out, k_out, v_out, norm_out, wpad_out, att_out, lse_ref, got_out, wide_out,
    norm, wpad, qkv, att, got, vt_ref, z1, y1, x2, pair,
    sx, rx, sc, rc, sf, rf, sz1, rz1, sy1, ry1, sx2, rx2, sz2, rz2, sy2, ry2, sc2, rc2,
    st_, rt_, so,
):
    here, me = lax.axis_index("tensor"), lax.axis_index("dp")
    rows, width = tok_ref.shape
    length = norm.shape[0]
    tiles = length // TILE
    cols = w1_ref.shape[2] // 2
    heads = cols // HD
    packed = w1_ref.shape[1]
    depth = 2 * packed
    fused = far > 0
    major, minor = me // 2, me % 2

    def at(mask):
        return (me, here ^ mask)

    across = (me ^ 1, here)

    def along(step):
        return (lax.rem(major + step, far) * 2 + minor, here)

    def source(step):
        return lax.rem(major + far - step, far)

    peers = [at(mask) for mask in PARTNERS]
    if fused:
        peers += [across] + [along(step) for step in range(1, far)]
    greet(peers)

    def z_first(w, step):
        return remote(
            w1_ref.at[w], z1.at[step, w], sz1.at[step, w], rz1.at[step, w], along(step)
        )

    def y_first(w, step):
        src = w1_ref.at[w] if isinstance(step, int) and step == 0 else z1.at[step, w]
        return remote(src, y1.at[step, w], sy1.at[step, w], ry1.at[step, w], across)

    swap_two = remote(w2_ref, x2, sx2, rx2, at(2)) if fused else None
    if fused:
        for w in range(3):
            for step in range(1, far):
                z_first(w, step).start()
            y_first(w, 0).start()

    chunk = TILE
    count = rows // chunk

    @pl.loop(0, count)
    def _(c):
        low = pl.multiple_of(c * chunk, chunk)
        v = tok_ref[pl.ds(low, chunk), :].astype(F32)
        hat = v * lax.rsqrt(jnp.mean(v * v, axis=-1, keepdims=True) + EPSILON)
        norm[pl.ds(pl.multiple_of(here * rows + low, chunk), chunk), :] = (
            hat * gain_ref[...]
        ).astype(BF)

    def rows_of(mask, c):
        return norm.at[pl.ds(pl.multiple_of((here ^ mask) * rows + c * chunk, chunk), chunk), :]

    def send_x(c):
        return remote(rows_of(0, c), rows_of(0, c), sx.at[c], rx.at[c], at(2))

    def send_c(c):
        return remote(rows_of(0, c), rows_of(0, c), sc.at[c], rc.at[c], at(1))

    def forward(c):
        return remote(rows_of(2, c), rows_of(2, c), sf.at[c], rf.at[c], at(1))

    for c in range(count):
        send_x(c).start()
        send_c(c).start()
    if fused:
        swap_two.start()

    def project(w, mask, c):
        low = pl.multiple_of((here ^ mask) * rows + c * chunk, chunk)
        y = mm(norm[pl.ds(low, chunk), :], wpad[w], 1, 0)
        if w == 0:
            y = y * fac_ref[...]
        y = y.astype(BF)
        for h in range(heads):
            qkv[w, h, pl.ds(low, chunk), :] = y[:, h * HP : (h + 1) * HP]

    if not fused:
        wpad[...] = w1_ref[...]
        for c in range(count):
            send_c(c).wait_recv()
        for w in range(3):
            for mask in (0, 1):
                for c in range(count):
                    project(w, mask, c)
    else:
        wpad[...] = jnp.zeros_like(wpad)

        def unpack(w, block, device):
            for part in range(2):
                low = pl.multiple_of(device * depth + part * packed, 16)
                for h in range(heads):
                    lane = part * cols + h * HD
                    wpad[w, pl.ds(low, packed), h * HP : h * HP + HD] = block[:, lane : lane + HD]

        for w in (1, 0, 2):
            unpack(w, w1_ref[w], me)
            for step in range(1, far):
                z_first(w, step).wait_recv()
                y_first(w, step).start()
                unpack(w, z1[step, w], source(step) * 2 + minor)
            for step in range(far):
                y_first(w, step).wait_recv()
                unpack(w, y1[step, w], source(step) * 2 + 1 - minor)
            if w == 1:
                for c in range(count):
                    send_c(c).wait_recv()
            for mask in (0, 1):
                for c in range(count):
                    project(w, mask, c)

    def rows_two(index):
        return pl.ds(pl.multiple_of(index * depth, 16), depth)

    def z_second(w, step):
        return remote(
            pair.at[w], wide_out.at[w, rows_two(me), pl.ds(0, 2 * cols)],
            sz2.at[w, step], rz2.at[w, step], along(step),
        )

    def block_two(w, index):
        return wide_out.at[w, rows_two(index), pl.ds(0, 2 * cols)]

    def y_second(w, step):
        ref = block_two(w, source(step) * 2 + minor)
        return remote(ref, ref, sy2.at[w, step], ry2.at[w, step], across)

    def c_second(w, step, side):
        index = source(step) * 2 + (minor if side == 0 else 1 - minor)
        return remote(
            block_two(w, index), wide_out.at[w, rows_two(index), pl.ds(2 * cols, 2 * cols)],
            sc2.at[w, step, side], rc2.at[w, step, side], at(1),
        )

    def own_two(w):
        return pltpu.make_async_copy(pair.at[w], block_two(w, me), so.at[8 + w])

    if fused:
        swap_two.wait_recv()
        for w in range(3):
            for which, ref in ((0, w2_ref), (1, x2)):
                block = ref[w]
                for part in range(2):
                    pair[w, part * packed : (part + 1) * packed,
                         which * cols : (which + 1) * cols] = (
                        block[:, part * cols : (part + 1) * cols]
                    )
            own_two(w).start()
            for step in range(1, far):
                z_second(w, step).start()

    for c in range(count):
        send_x(c).wait_recv()
        forward(c).start()
        for w in range(3):
            project(w, 2, c)
    for c in range(count):
        forward(c).wait_recv()
        for w in range(3):
            project(w, 3, c)

    keep = [
        pltpu.make_async_copy(norm, norm_out, so.at[0]),
        pltpu.make_async_copy(wpad, wpad_out, so.at[1]),
        pltpu.make_async_copy(qkv.at[0], q_out, so.at[2]),
        pltpu.make_async_copy(qkv.at[1], k_out, so.at[3]),
        pltpu.make_async_copy(qkv.at[2], v_out, so.at[4]),
    ]
    for copy in keep:
        copy.start()

    def trade(h, mask):
        spot = pl.ds(pl.multiple_of((here ^ mask) * rows, HP), rows)
        return remote(
            att.at[h, :, spot], got.at[SLOT[mask], h], st_.at[mask, h], rt_.at[mask, h], at(mask)
        )

    def second_on(w):
        own_two(w).wait()
        for step in range(far):
            if step:
                z_second(w, step).wait_recv()
            y_second(w, step).start()
            c_second(w, step, 0).start()

    sub = lax.broadcasted_iota(jnp.int32, (HP, length), 0)

    @pl.loop(0, heads)
    def _(h):
        q_ref, k_ref, v_ref = qkv.at[0, h], qkv.at[1, h], qkv.at[2, h]
        vt_ref[...] = jnp.where(sub == HD, 1.0, v_ref[...].astype(F32).T).astype(BF)

        def scores(t):
            seen, low = reach(t, length), t * TILE
            st = mm(k_ref[:seen, :], q_ref[low : low + TILE, :], 1, 1)
            visible = idc_ref[low:seen, :] <= idr_ref[:, low : low + TILE]
            masked = jnp.where(visible, st[low:], MASKED)
            return jnp.concatenate([st[:low], masked], 0) if low else masked

        st = scores(0)
        for t in range(tiles):
            later = scores(t + 1) if t + 1 < tiles else None
            seen, low = st.shape[0], t * TILE
            group = jnp.max(st.reshape(seen // 64, 64, TILE), axis=0)
            highest = jnp.max(group, axis=0, keepdims=True)
            weights = jnp.exp(st - highest).astype(BF)
            ot = mm(vt_ref[:, :seen], weights, 1, 0)
            summed = ot[HD : HD + 1, :]
            att[h, :, low : low + TILE] = (ot[:HD] * (1.0 / summed)).astype(BF)
            lse_ref[h, :, low : low + TILE] = highest + jnp.log(summed)
            st = later
        for mask in PARTNERS:
            trade(h, mask).start()
        if fused:

            @pl.when(h > 0)
            def _():
                second_on(h - 1)

    got[0] = att[:, :, pl.ds(pl.multiple_of(here * rows, HP), rows)]
    keep.append(pltpu.make_async_copy(att, att_out, so.at[5]))
    keep[-1].start()
    if fused:
        for w in range(3):
            for step in range(far):
                y_second(w, step).wait_recv()
                c_second(w, step, 1).start()
    for h in range(heads):
        for mask in PARTNERS:
            trade(h, mask).wait_recv()
    keep.append(pltpu.make_async_copy(got, got_out, so.at[6]))
    keep[-1].start()

    for c in range(count):
        send_x(c).wait_send()
        send_c(c).wait_send()
        forward(c).wait_send()
    for h in range(heads):
        for mask in PARTNERS:
            trade(h, mask).wait_send()
    if fused:
        swap_two.wait_send()
        for w in range(3):
            for step in range(far):
                if step:
                    z_first(w, step).wait_send()
                    z_second(w, step).wait_send()
                y_first(w, step).wait_send()
                y_second(w, step).wait_send()
                c_second(w, step, 0).wait()
                c_second(w, step, 1).wait()
    for copy in keep:
        copy.wait()


def front(dp, far, tokens, gain, first, second, factor, idr, idc, cols):
    rows, width = tokens.shape
    length = idr.shape[1]
    heads = cols // HD
    wide = heads * HP
    packed = first.shape[1]
    count = rows // TILE
    vmem = pl.BlockSpec(memory_space=pltpu.VMEM)
    hbm = pl.BlockSpec(memory_space=pl.ANY)
    sem = pltpu.SemaphoreType.DMA
    far_n = max(far, 1)
    fused = far > 0
    small = (packed, 2 * cols) if fused else (16, 128)
    per_head = jax.ShapeDtypeStruct((heads, length, HP), BF)
    return pl.pallas_call(
        lambda *refs: front_kernel(dp, far, *refs),
        out_shape=[
            per_head,
            per_head,
            per_head,
            jax.ShapeDtypeStruct((length, width), BF),
            jax.ShapeDtypeStruct((3, width, wide), BF),
            jax.ShapeDtypeStruct((heads, HD, length), BF),
            jax.ShapeDtypeStruct((heads, 1, length), F32),
            jax.ShapeDtypeStruct((4, heads, HD, rows), BF),
            jax.ShapeDtypeStruct((3, width, 4 * cols) if fused else (3, 16, 128), BF),
        ],
        in_specs=[vmem] * 7,
        out_specs=[hbm] * 6 + [vmem] + [hbm] * 2,
        scratch_shapes=[
            pltpu.VMEM((length, width), BF),
            pltpu.VMEM((3, width, wide), BF),
            pltpu.VMEM((3, heads, length, HP), BF),
            pltpu.VMEM((heads, HD, length), BF),
            pltpu.VMEM((4, heads, HD, rows), BF),
            pltpu.VMEM((HP, length), BF),
            pltpu.VMEM((far_n, 3) + small, BF),
            pltpu.VMEM((far_n, 3) + small, BF),
            pltpu.VMEM((3,) + small, BF),
            pltpu.VMEM((3, 2 * packed, 2 * cols) if fused else (3, 16, 128), BF),
            sem((count,)), sem((count,)), sem((count,)), sem((count,)), sem((count,)), sem((count,)),
            sem((far_n, 3)), sem((far_n, 3)), sem((far_n, 3)), sem((far_n, 3)),
            sem, sem,
            sem((3, far_n)), sem((3, far_n)), sem((3, far_n)), sem((3, far_n)),
            sem((3, far_n, 2)), sem((3, far_n, 2)),
            sem((4, heads)), sem((4, heads)),
            sem((12,)),
        ],
        compiler_params=pltpu.CompilerParams(
            vmem_limit_bytes=60 << 20, collective_id=1, has_side_effects=True
        ),
    )(tokens, gain, first, second, factor, idr, idc)


def swap(v, axis, size, mask):
    return lax.ppermute(v, axis, [(i, i ^ mask) for i in range(size)])


def gather_dp(shard, size):
    if size != 8:
        return lax.all_gather(shard, "dp", axis=0)
    far, here = size // 2, lax.axis_index("dp")
    major, minor = here // 2, here % 2
    parts = [shard]
    for step in range(1, far):
        parts.append(
            lax.ppermute(shard, "dp", [(i, (i + 2 * step) % size) for i in range(size)])
        )
    others = [swap(part, "dp", size, 1) for part in parts]
    whole = jnp.zeros((size,) + shard.shape, shard.dtype)
    for step in range(far):
        source = ((major + far - step) % far) * 2
        whole = lax.dynamic_update_slice(whole, parts[step][None], (source + minor, 0, 0))
        whole = lax.dynamic_update_slice(whole, others[step][None], (source + 1 - minor, 0, 0))
    return whole


def scatter_dp(grad, size):
    if size != 8:
        return lax.psum_scatter(grad, "dp", scatter_dimension=0, tiled=False)
    far, here = size // 2, lax.axis_index("dp")
    major, minor = here // 2, here % 2
    split = grad.reshape((far, 2) + grad.shape[1:])
    mine = lax.dynamic_index_in_dim(split, minor, 1, keepdims=False)
    theirs = lax.dynamic_index_in_dim(split, 1 - minor, 1, keepdims=False)
    half = mine + swap(theirs.astype(BF), "dp", size, 1).astype(F32)
    total = lax.dynamic_index_in_dim(half, major, 0, keepdims=False)
    for step in range(1, far):
        piece = lax.dynamic_index_in_dim(half, (major + step) % far, 0, keepdims=False)
        total = total + lax.ppermute(
            piece.astype(BF), "dp", [(i, (i + 2 * step) % size) for i in range(size)]
        ).astype(F32)
    return total


def sum_all(v, dp, tensor):
    if dp != 8:
        return lax.psum(v, ("dp", "tensor"))
    v = v + swap(v, "tensor", tensor, 1)
    v = v + swap(v, "tensor", tensor, 2)
    v = v + swap(v, "dp", dp, 1)
    parts = [lax.ppermute(v, "dp", [(i, (i + 2 * s) % dp) for i in range(dp)]) for s in (1, 2, 3)]
    here = lax.axis_index("dp") // 2
    stack = jnp.zeros((4,) + v.shape, v.dtype)
    for s, part in enumerate([v] + parts):
        stack = lax.dynamic_update_slice(stack, part[None], ((here + 4 - s) % 4,) + (0,) * v.ndim)
    return (stack[0] + stack[1]) + (stack[2] + stack[3])


def pack(w):
    half = w.shape[0] // 2
    return jnp.concatenate([w[:half], w[half:]], axis=1)


def pad_heads(w):
    rows, cols = w.shape
    w = w.reshape(rows, cols // HD, HD)
    return jnp.pad(w, ((0, 0), (0, 0), (0, HP - HD))).reshape(rows, cols // HD * HP)


def trim_heads(w):
    rows, cols = w.shape
    return w.reshape(rows, cols // HP, HP)[:, :, :HD].reshape(rows, cols // HP * HD)


def rms_stats(v):
    inverse = lax.rsqrt(jnp.mean(v * v, axis=-1, keepdims=True) + EPSILON)
    return v * inverse, inverse


def rms_back(grad, hat, inverse, gain):
    scaled = grad * gain
    return inverse * (scaled - hat * jnp.mean(scaled * hat, axis=-1, keepdims=True))


def body(dp, tensor, tokens, cotangent, block_ids, attn_gain, w_query, w_key, w_value,
         query_scale, w_out, mlp_gain, w_up, b_up, w_down, b_down):
    assert tensor == 4
    here = lax.axis_index("tensor")
    rows, width = tokens.shape
    length = rows * tensor
    cols = w_query.shape[1]
    heads = cols // HD
    order = [here, here ^ 2, here ^ 1, here ^ 3]

    tokens_f32 = tokens.astype(F32)
    hat_one, inverse_one = rms_stats(tokens_f32)
    softplus = jnp.log1p(jnp.exp(query_scale))
    factor = SCORE_BASE / math.sqrt(HD) * softplus
    factor_pad = jnp.pad(factor, (0, HP - HD))[None, :]
    idr = block_ids
    idc = block_ids.reshape(length, 1)

    first = (w_query, w_key, w_value)
    second = (w_out.T, w_up, w_down.T)
    far = dp // 2 if dp == 8 else 0
    if far:
        first = jnp.stack([pack(w) for w in first])
        second = jnp.stack([pack(w) for w in second])
    else:
        pair = [jnp.concatenate([w, swap(w, "tensor", tensor, 2)], axis=1) for w in second]
        half = gather_dp(jnp.concatenate(pair, axis=1), dp).reshape(width, 3, 2 * cols)
        both = jnp.concatenate([half, swap(half, "tensor", tensor, 1)], axis=2)
        full = gather_dp(jnp.concatenate(first, axis=1), dp).reshape(width, 3 * cols)
        first = jnp.stack([pad_heads(full[:, i * cols : (i + 1) * cols]) for i in range(3)])
        second = jnp.zeros((3, 16, 128), BF)
    queries, keys, values, normed, padded, attended, lse, got, wide = front(
        dp, far, tokens, attn_gain[None, :], first, second, jnp.tile(factor_pad, (1, heads)),
        idr, idc, cols,
    )
    if not far:
        wide = both.transpose(1, 0, 2)
    wq, wk, wv = padded[0], padded[1], padded[2]
    out_t, up, down_t = wide[0], wide[1], wide[2]
    mine = got.reshape(4 * cols, rows).T
    hidden = tokens_f32 + mm(mine, out_t, 1, 1)

    b_rel = jnp.concatenate([lax.dynamic_slice(b_up, (at * cols,), (cols,)) for at in order])
    cot_f32 = cotangent.astype(F32)
    grad_act = mm(cotangent, down_t, 1, 0)
    hat_two, inverse_two = rms_stats(hidden)
    normed_two = (hat_two * mlp_gain).astype(BF)
    pre = mm(normed_two, up, 1, 0) + b_rel
    sig = jax.nn.sigmoid(pre)
    activation = (pre * sig).astype(BF)
    d_pre = (grad_act * sig * (1.0 + pre * (1.0 - sig))).astype(BF)
    d_normed_two = mm(d_pre, up, 1, 1)
    d_hidden = cot_f32 + rms_back(d_normed_two, hat_two, inverse_two, mlp_gain)
    branch = d_hidden.astype(BF)
    d_mine = mm(branch, out_t, 1, 0).astype(BF)
    received = [
        d_mine[:, :cols],
        swap(d_mine[:, cols : 2 * cols], "tensor", tensor, 2),
        swap(d_mine[:, 2 * cols : 3 * cols], "tensor", tensor, 1),
        swap(d_mine[:, 3 * cols :], "tensor", tensor, 3),
    ]
    d_attended = jnp.zeros((length, cols), BF)
    for at, block in zip(order, received):
        d_attended = lax.dynamic_update_slice(d_attended, block, (at * rows, 0))
    d_attended = pad_heads(d_attended)

    output = (hidden + mm(activation, down_t, 1, 1) + b_down).astype(BF)
    d_down_t = mm(cotangent, activation, 0, 0)
    d_up = mm(normed_two, d_pre, 0, 0)
    d_out_t = mm(branch, mine, 0, 0)
    d_mlp_gain = jnp.sum(d_normed_two * hat_two, axis=0)
    d_b_rel = jnp.sum(d_pre.astype(F32), axis=0)
    d_b_up = jnp.zeros_like(b_up)
    for i, at in enumerate(order):
        d_b_up = lax.dynamic_update_slice(d_b_up, d_b_rel[i * cols : (i + 1) * cols], (at * cols,))
    d_b_down = jnp.sum(cot_f32, axis=0)
    early = sum_all(jnp.stack([d_mlp_gain, d_b_up, d_b_down]), dp, tensor)

    keep = jnp.concatenate([g[:, : 2 * cols] for g in (d_out_t, d_up, d_down_t)], axis=1)
    give = jnp.concatenate([g[:, 2 * cols :] for g in (d_out_t, d_up, d_down_t)], axis=1)
    keep = keep + swap(give.astype(BF), "tensor", tensor, 1).astype(F32)
    kept = scatter_dp(keep.reshape(dp, width // dp, 6 * cols), dp)
    kept = kept.reshape(width // dp, 3, 2, cols)
    second_grads = kept[:, :, 0] + swap(kept[:, :, 1].astype(BF), "tensor", tensor, 2).astype(F32)
    s_out, s_up, s_down = second_grads[:, 0].T, second_grads[:, 1], second_grads[:, 2].T

    dq, dk, dv, q_sums = attend_back(
        queries, keys, values, attended, d_attended, lse, factor_pad, idr, idc
    )
    d_scale = jnp.sum(q_sums[:, 0, :HD], axis=0) / softplus * jax.nn.sigmoid(query_scale)

    def part(at):
        return sum(
            mm(lax.dynamic_slice(d, (at * rows, 0), (rows, d.shape[1])), w, 1, 1)
            for d, w in ((dq, wq), (dk, wk), (dv, wv))
        )

    far_same = part(order[1])
    far_other = part(order[3])
    near_same = part(order[0])
    near_other = part(order[2])
    from_x_same = swap(far_same.astype(BF), "tensor", tensor, 2).astype(F32)
    from_x_other = swap(far_other.astype(BF), "tensor", tensor, 2).astype(F32)
    chip_other = near_other + from_x_other
    d_normed = near_same + from_x_same + swap(chip_other.astype(BF), "tensor", tensor, 1).astype(F32)

    d_wq, d_wk, d_wv = (mm(normed, d, 0, 0) for d in (dq, dk, dv))
    w_dot = sum(
        jnp.sum(g * w.astype(F32), axis=1) for g, w in ((d_wq, wq), (d_wk, wk), (d_wv, wv))
    )
    late = jnp.concatenate([w_dot / attn_gain, jnp.pad(d_scale, (0, HP - HD))])
    late = sum_all(late.reshape(-1, HP), dp, tensor).reshape(-1)
    qkv_grad = jnp.concatenate([trim_heads(g) for g in (d_wq, d_wk, d_wv)], axis=1)
    s_qkv = scatter_dp(qkv_grad.reshape(dp, width // dp, 3 * cols), dp)

    d_tokens = (d_hidden + rms_back(d_normed, hat_one, inverse_one, attn_gain)).astype(BF)
    return (
        output,
        d_tokens,
        late[:width],
        s_qkv[:, :cols],
        s_qkv[:, cols : 2 * cols],
        s_qkv[:, 2 * cols :],
        late[width : width + HD],
        s_out,
        early[0],
        s_up,
        early[1],
        s_down,
        early[2],
    )


def solution(mesh):
    weight, turned, whole = P("dp", "tensor"), P("tensor", "dp"), P()
    positions = P(("dp", "tensor"), None)
    return jax.shard_map(
        lambda *args: body(mesh.shape["dp"], mesh.shape["tensor"], *args),
        mesh=mesh,
        in_specs=(positions, positions, P("dp", None), whole, weight, weight, weight, whole,
                  turned, whole, weight, whole, turned, whole),
        out_specs=(positions, positions, whole, weight, weight, weight, whole, turned, whole,
                   weight, whole, turned, whole),
        check_vma=False,
    )
```

```python
import math

import jax
import jax.numpy as jnp
from jax import lax
from jax.experimental import pallas as pl
from jax.experimental.pallas import tpu as pltpu
from jax.sharding import PartitionSpec as P

HD = 80
HP = 128
TILE = 256
BLOCK_MOST = 256
EPSILON = 1e-06
SCORE_BASE = 1.442695041
MASKED = -1e30
BF = jnp.bfloat16
F32 = jnp.float32


def mm(a, b, ca, cb):
    return lax.dot_general(a, b, (((ca,), (cb,)), ((), ())), preferred_element_type=F32)


def reach(tile, length):
    return min((tile + 1) * TILE + BLOCK_MOST, length)


MESH = pl.DeviceIdType.MESH
PARTNERS = (2, 1, 3)
SLOT = {0: 0, 2: 1, 1: 2, 3: 3}


def remote(src, dst, send, recv, where):
    return pltpu.make_async_remote_copy(
        src_ref=src, dst_ref=dst, send_sem=send, recv_sem=recv, device_id=where, device_id_type=MESH
    )


def greet(peers):
    barrier = pltpu.get_barrier_semaphore()
    for where in peers:
        pl.semaphore_signal(barrier, inc=1, device_id=where, device_id_type=MESH)
    pl.semaphore_wait(barrier, len(peers))


def front_kernel(
    dp, far, tok_ref, gain_ref, w1_ref, w2_ref, fac_ref, idr_ref, idc_ref,
    qkv_out, normt_out, wpad_out, att_out, lse_ref, got_out, wide_out,
    norm, normt, wpad, qkv, att, got, vt_ref, z1, y1, x2, pair,
    sx, rx, sc, rc, sf, rf, sz1, rz1, sy1, ry1, sx2, rx2, sz2, rz2, sy2, ry2, sc2, rc2,
    st_, rt_, so,
):
    here, me = lax.axis_index("tensor"), lax.axis_index("dp")
    rows, width = tok_ref.shape
    length = norm.shape[0]
    tiles = length // TILE
    cols = w1_ref.shape[2] // 2
    heads = cols // HD
    packed = w1_ref.shape[1]
    depth = 2 * packed
    fused = far > 0
    major, minor = me // 2, me % 2

    def at(mask):
        return (me, here ^ mask)

    across = (me ^ 1, here)

    def along(step):
        return (lax.rem(major + step, far) * 2 + minor, here)

    def source(step):
        return lax.rem(major + far - step, far)

    peers = [at(mask) for mask in PARTNERS]
    if fused:
        peers += [across] + [along(step) for step in range(1, far)]
    greet(peers)

    def z_first(w, step):
        return remote(
            w1_ref.at[w], z1.at[step, w], sz1.at[step, w], rz1.at[step, w], along(step)
        )

    def y_first(w, step):
        src = w1_ref.at[w] if isinstance(step, int) and step == 0 else z1.at[step, w]
        return remote(src, y1.at[step, w], sy1.at[step, w], ry1.at[step, w], across)

    swap_two = remote(w2_ref, x2, sx2, rx2, at(2)) if fused else None
    if fused:
        for w in range(3):
            for step in range(1, far):
                z_first(w, step).start()
            y_first(w, 0).start()

    chunk = TILE
    count = rows // chunk

    @pl.loop(0, count)
    def _(c):
        low = pl.multiple_of(c * chunk, chunk)
        v = tok_ref[pl.ds(low, chunk), :].astype(F32)
        hat = v * lax.rsqrt(jnp.mean(v * v, axis=-1, keepdims=True) + EPSILON)
        norm[pl.ds(pl.multiple_of(here * rows + low, chunk), chunk), :] = (
            hat * gain_ref[...]
        ).astype(BF)

    def rows_of(mask, c):
        return norm.at[pl.ds(pl.multiple_of((here ^ mask) * rows + c * chunk, chunk), chunk), :]

    def send_x(c):
        return remote(rows_of(0, c), rows_of(0, c), sx.at[c], rx.at[c], at(2))

    def send_c(c):
        return remote(rows_of(0, c), rows_of(0, c), sc.at[c], rc.at[c], at(1))

    def forward(c):
        return remote(rows_of(2, c), rows_of(2, c), sf.at[c], rf.at[c], at(1))

    for c in range(count):
        send_x(c).start()
        send_c(c).start()
    if fused:
        swap_two.start()

    def project(w, mask, c):
        low = pl.multiple_of((here ^ mask) * rows + c * chunk, chunk)
        x = norm[pl.ds(low, chunk), :]
        y = mm(x, wpad[w], 1, 0)
        if w == 0:
            y = y * fac_ref[...]
        qkv[w, pl.ds(low, chunk), :] = y.astype(BF)
        if w == 2:
            normt[:, pl.ds(low, chunk)] = x.astype(F32).T.astype(BF)

    if not fused:
        wpad[...] = w1_ref[...]
        for c in range(count):
            send_c(c).wait_recv()
        for w in range(3):
            for mask in (0, 1):
                for c in range(count):
                    project(w, mask, c)
    else:
        wpad[...] = jnp.zeros_like(wpad)

        def unpack(w, block, device):
            for part in range(2):
                low = pl.multiple_of(device * depth + part * packed, 16)
                for h in range(heads):
                    lane = part * cols + h * HD
                    wpad[w, pl.ds(low, packed), h * HP : h * HP + HD] = block[:, lane : lane + HD]

        for w in (1, 0, 2):
            unpack(w, w1_ref[w], me)
            for step in range(1, far):
                z_first(w, step).wait_recv()
                y_first(w, step).start()
                unpack(w, z1[step, w], source(step) * 2 + minor)
            for step in range(far):
                y_first(w, step).wait_recv()
                unpack(w, y1[step, w], source(step) * 2 + 1 - minor)
            if w == 1:
                for c in range(count):
                    send_c(c).wait_recv()
            for mask in (0, 1):
                for c in range(count):
                    project(w, mask, c)

    def rows_two(index):
        return pl.ds(pl.multiple_of(index * depth, 16), depth)

    def z_second(w, step):
        return remote(
            pair.at[w], wide_out.at[w, rows_two(me), pl.ds(0, 2 * cols)],
            sz2.at[w, step], rz2.at[w, step], along(step),
        )

    def block_two(w, index):
        return wide_out.at[w, rows_two(index), pl.ds(0, 2 * cols)]

    def y_second(w, step):
        ref = block_two(w, source(step) * 2 + minor)
        return remote(ref, ref, sy2.at[w, step], ry2.at[w, step], across)

    def c_second(w, step, side):
        index = source(step) * 2 + (minor if side == 0 else 1 - minor)
        return remote(
            block_two(w, index), wide_out.at[w, rows_two(index), pl.ds(2 * cols, 2 * cols)],
            sc2.at[w, step, side], rc2.at[w, step, side], at(1),
        )

    def own_two(w):
        return pltpu.make_async_copy(pair.at[w], block_two(w, me), so.at[8 + w])

    if fused:
        swap_two.wait_recv()
        for w in range(3):
            for which, ref in ((0, w2_ref), (1, x2)):
                block = ref[w]
                for part in range(2):
                    pair[w, part * packed : (part + 1) * packed,
                         which * cols : (which + 1) * cols] = (
                        block[:, part * cols : (part + 1) * cols]
                    )
            own_two(w).start()
            for step in range(1, far):
                z_second(w, step).start()

    for c in range(count):
        send_x(c).wait_recv()
        forward(c).start()
        for w in range(3):
            project(w, 2, c)
    for c in range(count):
        forward(c).wait_recv()
        for w in range(3):
            project(w, 3, c)

    keep = [
        pltpu.make_async_copy(normt, normt_out, so.at[0]),
        pltpu.make_async_copy(wpad, wpad_out, so.at[1]),
        pltpu.make_async_copy(qkv, qkv_out, so.at[2]),
    ]
    for copy in keep:
        copy.start()

    def trade(h, mask):
        spot = pl.ds(pl.multiple_of((here ^ mask) * rows, HP), rows)
        return remote(
            att.at[h, :, spot], got.at[SLOT[mask], h], st_.at[mask, h], rt_.at[mask, h], at(mask)
        )

    def second_on(w):
        own_two(w).wait()
        for step in range(far):
            if step:
                z_second(w, step).wait_recv()
            y_second(w, step).start()
            c_second(w, step, 0).start()

    sub = lax.broadcasted_iota(jnp.int32, (HP, length), 0)

    @pl.loop(0, heads)
    def _(h):
        lanes = pl.ds(pl.multiple_of(h * HP, HP), HP)
        vt_ref[...] = jnp.where(sub == HD, 1.0, qkv[2, :, lanes].astype(F32).T).astype(BF)

        def scores(t):
            seen, low = reach(t, length), t * TILE
            st = mm(qkv[1, :seen, lanes], qkv[0, low : low + TILE, lanes], 1, 1)
            visible = idc_ref[low:seen, :] <= idr_ref[:, low : low + TILE]
            masked = jnp.where(visible, st[low:], MASKED)
            return jnp.concatenate([st[:low], masked], 0) if low else masked

        st = scores(0)
        for t in range(tiles):
            later = scores(t + 1) if t + 1 < tiles else None
            seen, low = st.shape[0], t * TILE
            group = jnp.max(st.reshape(seen // 64, 64, TILE), axis=0)
            highest = jnp.max(group, axis=0, keepdims=True)
            weights = jnp.exp(st - highest).astype(BF)
            ot = mm(vt_ref[:, :seen], weights, 1, 0)
            summed = ot[HD : HD + 1, :]
            att[h, :, low : low + TILE] = (ot[:HD] * (1.0 / summed)).astype(BF)
            lse_ref[h, :, low : low + TILE] = highest + jnp.log(summed)
            st = later
        for mask in PARTNERS:
            trade(h, mask).start()
        if fused:

            @pl.when(h > 0)
            def _():
                second_on(h - 1)

    got[0] = att[:, :, pl.ds(pl.multiple_of(here * rows, HP), rows)]
    keep.append(pltpu.make_async_copy(att, att_out, so.at[5]))
    keep[-1].start()
    if fused:
        for w in range(3):
            for step in range(far):
                y_second(w, step).wait_recv()
                c_second(w, step, 1).start()
    for h in range(heads):
        for mask in PARTNERS:
            trade(h, mask).wait_recv()
    keep.append(pltpu.make_async_copy(got, got_out, so.at[6]))
    keep[-1].start()

    for c in range(count):
        send_x(c).wait_send()
        send_c(c).wait_send()
        forward(c).wait_send()
    for h in range(heads):
        for mask in PARTNERS:
            trade(h, mask).wait_send()
    if fused:
        swap_two.wait_send()
        for w in range(3):
            for step in range(far):
                if step:
                    z_first(w, step).wait_send()
                    z_second(w, step).wait_send()
                y_first(w, step).wait_send()
                y_second(w, step).wait_send()
                c_second(w, step, 0).wait()
                c_second(w, step, 1).wait()
    for copy in keep:
        copy.wait()


def front(dp, far, tokens, gain, first, second, factor, idr, idc, cols):
    rows, width = tokens.shape
    length = idr.shape[1]
    heads = cols // HD
    wide = heads * HP
    packed = first.shape[1]
    count = rows // TILE
    vmem = pl.BlockSpec(memory_space=pltpu.VMEM)
    hbm = pl.BlockSpec(memory_space=pl.ANY)
    sem = pltpu.SemaphoreType.DMA
    far_n = max(far, 1)
    fused = far > 0
    small = (packed, 2 * cols) if fused else (16, 128)
    return pl.pallas_call(
        lambda *refs: front_kernel(dp, far, *refs),
        out_shape=[
            jax.ShapeDtypeStruct((3, length, wide), BF),
            jax.ShapeDtypeStruct((width, length), BF),
            jax.ShapeDtypeStruct((3, width, wide), BF),
            jax.ShapeDtypeStruct((heads, HD, length), BF),
            jax.ShapeDtypeStruct((heads, 1, length), F32),
            jax.ShapeDtypeStruct((4, heads, HD, rows), BF),
            jax.ShapeDtypeStruct((3, width, 4 * cols) if fused else (3, 16, 128), BF),
        ],
        in_specs=[vmem] * 7,
        out_specs=[hbm] * 4 + [vmem] + [hbm] * 2,
        scratch_shapes=[
            pltpu.VMEM((length, width), BF),
            pltpu.VMEM((width, length), BF),
            pltpu.VMEM((3, width, wide), BF),
            pltpu.VMEM((3, length, wide), BF),
            pltpu.VMEM((heads, HD, length), BF),
            pltpu.VMEM((4, heads, HD, rows), BF),
            pltpu.VMEM((HP, length), BF),
            pltpu.VMEM((far_n, 3) + small, BF),
            pltpu.VMEM((far_n, 3) + small, BF),
            pltpu.VMEM((3,) + small, BF),
            pltpu.VMEM((3, 2 * packed, 2 * cols) if fused else (3, 16, 128), BF),
            sem((count,)), sem((count,)), sem((count,)), sem((count,)), sem((count,)), sem((count,)),
            sem((far_n, 3)), sem((far_n, 3)), sem((far_n, 3)), sem((far_n, 3)),
            sem, sem,
            sem((3, far_n)), sem((3, far_n)), sem((3, far_n)), sem((3, far_n)),
            sem((3, far_n, 2)), sem((3, far_n, 2)),
            sem((4, heads)), sem((4, heads)),
            sem((12,)),
        ],
        compiler_params=pltpu.CompilerParams(
            vmem_limit_bytes=60 << 20, collective_id=1, has_side_effects=True
        ),
    )(tokens, gain, first, second, factor, idr, idc)


def mid_kernel(
    tok_ref, cot_ref, got_ref, gain_ref, bup_ref, bdown_ref, wide_ref,
    out_ref, dhid_ref, drec_out, xk_out, xg_out, pb_out, early_ref,
    w, att, n2, act, dpre, branch, hid, give, grec, db, drec, kept, bs,
    ss, rs, sg, rg, so,
):
    here, me = lax.axis_index("tensor"), lax.axis_index("dp")
    rows, width = tok_ref.shape
    wide = w.shape[1]
    cols = wide // 4
    pair = 2 * cols
    chunk = TILE
    half = chunk // 2
    count = rows // chunk

    def at(mask):
        return (me, here ^ mask)

    loads = [pltpu.make_async_copy(wide_ref.at[i], w.at[i], so.at[i]) for i in range(3)]
    for i in (0, 2, 1):
        loads[i].start()
    greet([at(mask) for mask in PARTNERS])
    att[...] = got_ref[...].astype(F32).T.astype(BF)
    early_ref[...] = jnp.zeros_like(early_ref)
    bs[...] = jnp.zeros_like(bs)
    for i in range(3):
        loads[i].wait()

    def trade(c, mask):
        return remote(
            db.at[c, SLOT[mask]], drec.at[c, SLOT[mask]],
            ss.at[c, mask], rs.at[c, mask], at(mask),
        )

    @pl.loop(0, count)
    def _(c):
        low = pl.multiple_of(c * chunk, chunk)
        spot = pl.ds(low, chunk)
        hidden = tok_ref[spot, :].astype(F32) + mm(att[spot, :], w[0], 1, 1)
        hid[spot, :] = hidden
        cot = cot_ref[spot, :]
        d_act = mm(cot, w[2], 1, 0)
        inverse = lax.rsqrt(jnp.mean(hidden * hidden, axis=-1, keepdims=True) + EPSILON)
        hat = hidden * inverse
        normed = (hat * gain_ref[...]).astype(BF)
        n2[spot, :] = normed
        pre = mm(normed, w[1], 1, 0) + bup_ref[...]
        sig = jax.nn.sigmoid(pre)
        act[spot, :] = (pre * sig).astype(BF)
        d_pre = (d_act * sig * (1.0 + pre * (1.0 - sig))).astype(BF)
        dpre[spot, :] = d_pre
        d_n2 = mm(d_pre, w[1], 1, 1)
        scaled = d_n2 * gain_ref[...]
        cot_f32 = cot.astype(F32)
        d_hidden = cot_f32 + inverse * (
            scaled - hat * jnp.mean(scaled * hat, axis=-1, keepdims=True)
        )
        dhid_ref[spot, :] = d_hidden
        br = d_hidden.astype(BF)
        branch[spot, :] = br
        d_att = mm(br, w[0], 1, 0).astype(BF)
        for i in range(4):
            for part in range(2):
                db[c, i, :, part * cols : (part + 1) * cols] = d_att[
                    part * half : (part + 1) * half, i * cols : (i + 1) * cols
                ]
        for mask in PARTNERS:
            trade(c, mask).start()
        drec[c, 0] = db[c, 0]
        early_ref[0:1, :] += jnp.sum(d_n2 * hat, axis=0, keepdims=True)
        early_ref[1:2, :] += jnp.sum(cot_f32, axis=0, keepdims=True)
        bs[0:1, :] += jnp.sum(d_pre.astype(F32), axis=0, keepdims=True)

    pieces = ((branch, att), (n2, dpre), (cot_ref, act))

    def gradient(i, low, first):
        left, right = pieces[i]
        return mm(left[:, pl.ds(low, chunk)], right[:, first : first + pair], 0, 0)

    def hand(i):
        return remote(give.at[i], grec.at[i], sg.at[i], rg.at[i], at(1))

    for i in range(3):

        @pl.loop(0, width // chunk)
        def _(j):
            low = pl.multiple_of(j * chunk, chunk)
            give[i, pl.ds(low, chunk), :] = gradient(i, low, pair).astype(BF)

        hand(i).start()

    for i in range(4):
        place = here ^ (0, 2, 1, 3)[i]
        early_ref[pl.ds(2 + place, 1), 0:cols] = bs[0:1, i * cols : (i + 1) * cols]

    @pl.loop(0, count)
    def _(c):
        spot = pl.ds(pl.multiple_of(c * chunk, chunk), chunk)
        out_ref[spot, :] = (hid[spot, :] + mm(act[spot, :], w[2], 1, 1) + bdown_ref[...]).astype(BF)

    for i in range(3):
        hand(i).wait_recv()

        @pl.loop(0, width // chunk)
        def _(j):
            low = pl.multiple_of(j * chunk, chunk)
            spot = pl.ds(low, chunk)
            total = (gradient(i, low, 0) + grec[i, spot, :].astype(F32)).astype(BF)
            if i == 0:
                kept[2, spot, :] = total
            else:
                lane = (i - 1) * cols
                kept[0, spot, lane : lane + cols] = total[:, :cols]
                kept[1, spot, lane : lane + cols] = total[:, cols:]

        if i == 0:
            keep = [pltpu.make_async_copy(kept.at[2], pb_out, so.at[3])]
            keep[0].start()
    keep.append(pltpu.make_async_copy(kept.at[0], xk_out, so.at[4]))
    keep.append(pltpu.make_async_copy(kept.at[1], xg_out, so.at[5]))
    for copy in keep[1:]:
        copy.start()
    for c in range(count):
        for mask in PARTNERS:
            trade(c, mask).wait_recv()
    keep.append(pltpu.make_async_copy(drec, drec_out, so.at[6]))
    keep[-1].start()
    for c in range(count):
        for mask in PARTNERS:
            trade(c, mask).wait_send()
    for i in range(3):
        hand(i).wait_send()
    for copy in keep:
        copy.wait()


def middle(tokens, cotangent, got, gain, b_rel, b_down, wide):
    rows, width = tokens.shape
    all_cols = wide.shape[2]
    cols = all_cols // 4
    count = rows // TILE
    vmem = pl.BlockSpec(memory_space=pltpu.VMEM)
    hbm = pl.BlockSpec(memory_space=pl.ANY)
    sem = pltpu.SemaphoreType.DMA
    blocks = (count, 4, TILE // 2, 2 * cols)
    halves = jax.ShapeDtypeStruct((width, 2 * cols), BF)
    return pl.pallas_call(
        mid_kernel,
        out_shape=[
            jax.ShapeDtypeStruct((rows, width), BF),
            jax.ShapeDtypeStruct((rows, width), F32),
            jax.ShapeDtypeStruct(blocks, BF),
            halves,
            halves,
            halves,
            jax.ShapeDtypeStruct((16, width), F32),
        ],
        in_specs=[vmem] * 6 + [hbm],
        out_specs=[vmem, vmem, hbm, hbm, hbm, hbm, vmem],
        scratch_shapes=[
            pltpu.VMEM((3, width, all_cols), BF),
            pltpu.VMEM((rows, all_cols), BF),
            pltpu.VMEM((rows, width), BF),
            pltpu.VMEM((rows, all_cols), BF),
            pltpu.VMEM((rows, all_cols), BF),
            pltpu.VMEM((rows, width), BF),
            pltpu.VMEM((rows, width), F32),
            pltpu.VMEM((3, width, 2 * cols), BF),
            pltpu.VMEM((3, width, 2 * cols), BF),
            pltpu.VMEM(blocks, BF),
            pltpu.VMEM(blocks, BF),
            pltpu.VMEM((3, width, 2 * cols), BF),
            pltpu.VMEM((8, all_cols), F32),
            sem((count, 4)), sem((count, 4)), sem((3,)), sem((3,)), sem((8,)),
        ],
        compiler_params=pltpu.CompilerParams(
            vmem_limit_bytes=60 << 20, collective_id=2, has_side_effects=True
        ),
    )(tokens, cotangent, got, gain, b_rel, b_down, wide)


def back_kernel(
    dp, far, o_ref, lse_ref, drec_ref, fac_ref, idr_ref, idc_ref, gain_ref, xk_ref, early_ref,
    qkv_hbm, xg_ref, pb_ref, tok_hbm, dhid_hbm, normt_hbm, wpad_hbm,
    dtok_ref, dq_out, dk_out, dv_out, dout_ref, dup_ref, ddown_ref, sums_ref,
    do, dka, dva, kt_ref, dqkv, tok, dhid, normt, wpad,
    xrec, pbown, yrec, zrec, last, lastsend, lastrec,
    gpay, gyrec, gzrec, fo, crec, fs, frec, nrec, qsum, lvec, ar, arec, aorder,
    so, sxa, rxa, sy, ry, sz, rz, sl, rl, sgy, rgy, sgz, rgz, sfo, rfo, sfs, rfs, sno, rno, sar, rar,
):
    here, me = lax.axis_index("tensor"), lax.axis_index("dp")
    heads, _, length = o_ref.shape
    rows, width = tok.shape
    cols = heads * HD
    tiles = length // TILE
    depth = width // dp
    packed = depth // 2
    fused = far > 0
    major, minor = me // 2, me % 2
    chunk = TILE
    count = rows // chunk

    def at(mask):
        return (me, here ^ mask)

    across = (me ^ 1, here)

    def along(step):
        return (lax.rem(major + step, far) * 2 + minor, here)

    def target(step):
        return lax.rem(major + step, far)

    loads = [
        pltpu.make_async_copy(src, dst, so.at[i])
        for i, (src, dst) in enumerate(
            ((wpad_hbm, wpad), (normt_hbm, normt), (tok_hbm, tok), (dhid_hbm, dhid))
        )
    ]
    load_qkv = pltpu.make_async_copy(qkv_hbm, dqkv, so.at[4])
    load_qkv.start()
    if fused:
        load_pb = pltpu.make_async_copy(pb_ref.at[:, minor], pbown, so.at[5])
        load_pb.start()
    for copy in loads:
        copy.start()
    peers = [at(2), at(1)]
    if fused:
        peers += [across] + [along(step) for step in range(1, far)]
    greet(peers)

    turn = list(range(1, far)) + [0]

    def x_send(step):
        spot = target(step)
        return remote(xg_ref.at[spot], xrec.at[spot], sxa.at[step], rxa.at[step], at(2))

    def y_send(p, step):
        spot = target(step)
        src = xrec.at[spot, 1 - minor] if p == 0 else pb_ref.at[spot, 1 - minor]
        return remote(src, yrec.at[p, spot], sy.at[p, step], ry.at[p, step], across)

    def z_send(p, step):
        return remote(
            yrec.at[p, target(step)], zrec.at[p, step - 1],
            sz.at[p, step], rz.at[p, step], along(step),
        )

    def after_x(step):
        x_send(step).wait_recv()
        spot = target(step)
        xrec[spot] = (xk_ref[spot].astype(F32) + xrec[spot].astype(F32)).astype(BF)
        y_send(0, step).start()

    def after_y(p, step):
        y_send(p, step).wait_recv()
        spot = target(step)
        mine = xrec[spot, minor] if p == 0 else pbown[spot]
        total = mine.astype(F32) + yrec[p, spot].astype(F32)
        if step:
            yrec[p, spot] = total.astype(BF)
            z_send(p, step).start()
        else:
            last[p] = total

    def after_z(p):
        for step in range(1, far):
            z_send(p, step).wait_recv()
            last[p] += zrec[p, step - 1].astype(F32)

    if fused:
        for step in turn:
            x_send(step).start()
            y_send(1, step).start()

    do[...] = jnp.zeros_like(do)
    half = chunk // 2
    for c in range(count):
        for i, mask in enumerate((0, 2, 1, 3)):
            block = drec_ref[c, i]
            for part in range(2):
                low = pl.multiple_of((here ^ mask) * rows + c * chunk + part * half, half)
                for h in range(heads):
                    lane = part * cols + h * HD
                    do[h, pl.ds(low, half), 0:HD] = block[:, lane : lane + HD]
    qsum[...] = jnp.zeros_like(qsum)

    load_qkv.wait()
    if fused:
        load_pb.wait()

    def one_head(h):
        lanes = pl.ds(pl.multiple_of(h * HP, HP), HP)
        kt_ref[...] = dqkv[1, :, lanes].astype(F32).T.astype(BF)
        dka[...] = jnp.zeros_like(dka)
        dva[...] = jnp.zeros_like(dva)
        scale_sum = jnp.zeros((1, HP), F32)
        for t in range(tiles):
            seen, low = reach(t, length), t * TILE
            spot = slice(low, low + TILE)
            qt = dqkv[0, spot, lanes]
            dot_ = do[h, spot, :]
            delta = jnp.sum(
                dot_.astype(F32).T[:HD] * o_ref[h, :, spot].astype(F32), axis=0, keepdims=True
            )
            st = mm(dqkv[1, :seen, lanes], qt, 1, 1)
            p = jnp.exp(st - lse_ref[h, :, spot])
            visible = idc_ref[low:seen, :] <= idr_ref[:, spot]
            pm = jnp.where(visible, p[low:], 0.0)
            p = jnp.concatenate([p[:low], pm], 0) if low else pm
            d_p = mm(dqkv[2, :seen, lanes], dot_, 1, 1)
            ds = (p * (d_p - delta)).astype(BF)
            dva[:seen, :] += mm(p.astype(BF), dot_, 1, 0)
            dka[:seen, :] += mm(ds, qt, 1, 0)
            dq = mm(kt_ref[:, :seen], ds, 1, 0).T
            scale_sum = scale_sum + jnp.sum(dq * qt.astype(F32), axis=0, keepdims=True)
            dqkv[0, spot, lanes] = (dq * fac_ref[...]).astype(BF)
        dqkv[1, :, lanes] = dka[...].astype(BF)
        dqkv[2, :, lanes] = dva[...].astype(BF)
        qsum[0:1, :] += scale_sum

    @pl.loop(0, heads)
    def _(h):
        one_head(h)
        if fused:
            for n in range(far):

                @pl.when(h == n)
                def _(n=n):
                    after_x(turn[n])
                    after_y(1, turn[n])
                    if n:
                        after_y(0, turn[n - 1])

    for copy in loads[:2]:
        copy.wait()

    def part(mask, c):
        spot = pl.ds(pl.multiple_of((here ^ mask) * rows + c * chunk, chunk), chunk)
        total = mm(dqkv[0, spot, :], wpad[0], 1, 1)
        total = total + mm(dqkv[1, spot, :], wpad[1], 1, 1)
        return total + mm(dqkv[2, spot, :], wpad[2], 1, 1)

    def c_far(c):
        return remote(fo.at[c], crec.at[c], sfo.at[c], rfo.at[c], at(1))

    def x_far(c):
        return remote(fs.at[c], frec.at[c], sfs.at[c], rfs.at[c], at(2))

    def c_near(c):
        return remote(fo.at[c], nrec.at[c], sno.at[c], rno.at[c], at(1))

    def weight_block(step, side):
        spot = target(step) if fused else step
        index = spot * 2 + side
        low = pl.multiple_of(index * depth, 4 if depth % 16 else 16)
        dots = jnp.zeros((depth, 1), F32)
        for i in range(3):
            g = mm(normt[pl.ds(low, depth), :], dqkv[i], 1, 0)
            dots = dots + jnp.sum(
                g * wpad[i, pl.ds(low, depth), :].astype(F32), axis=1, keepdims=True
            )
            for h in range(heads):
                for piece in range(2):
                    lane = piece * cols + h * HD
                    gpay[spot, side, i, :, lane : lane + HD] = g[
                        piece * packed : (piece + 1) * packed, h * HP : h * HP + HD
                    ].astype(BF)
        lvec[pl.ds(index, 1), :] = jnp.broadcast_to(dots, (depth, HP)).T[0:1, :]

    def gy_send(step):
        spot = target(step)
        return remote(
            gpay.at[spot, 1 - minor], gyrec.at[spot], sgy.at[step], rgy.at[step], across
        )

    def gz_send(step):
        return remote(
            gyrec.at[target(step)], gzrec.at[step - 1], sgz.at[step], rgz.at[step], along(step)
        )

    def far_chunk(c):
        fo[c] = part(3, c).astype(BF)
        c_far(c).start()

    def far_finish(c):
        own = part(2, c)
        c_far(c).wait_recv()
        fs[c] = (own + crec[c].astype(F32)).astype(BF)
        x_far(c).start()

    far_chunk(0)
    far_finish(0)
    if fused:
        for n, step in enumerate(turn):
            weight_block(step, 1 - minor)
            gy_send(step).start()
            if n == 0:
                after_y(0, turn[far - 1])
            if n == 1:
                far_chunk(1)
            if n == 2:
                far_finish(1)
                after_z(1)
        for step in turn:
            weight_block(step, minor)
    else:
        for c in range(1, count):
            far_chunk(c)
            far_finish(c)

        @pl.loop(0, 3)
        def _(i):
            for j in range(width // chunk):
                dq_out[i, j * chunk : (j + 1) * chunk, :] = mm(
                    normt[j * chunk : (j + 1) * chunk, :], dqkv[i], 1, 0
                )

    def hop(n, where):
        return remote(ar.at[n], arec.at[n], sar.at[n], rar.at[n], where)

    def z_hop(step):
        return remote(ar.at[3], arec.at[3 + step], sar.at[3 + step], rar.at[3 + step], along(step))

    if fused:
        ar[0] = jnp.zeros_like(ar[0])
        ar[0, 0:6, :] = early_ref[0:6, :]
        ar[0, 6:7, 0:HP] = qsum[0:1, :]
        ar[0, 8:16, 0:depth] = lvec[...]
        hop(0, at(1)).start()
        for piece in range(2):
            last_half = last[1, piece * packed : (piece + 1) * packed, cols:]
            lastsend[:, piece * cols : (piece + 1) * cols] = last_half.astype(BF)
        cross = remote(lastsend, lastrec, sl, rl, at(2))
        cross.start()
    else:
        sums_ref[...] = jnp.zeros_like(sums_ref)
        sums_ref[0:6, :] = early_ref[0:6, :]
        sums_ref[6:7, 0:HP] = qsum[0:1, :]

    for c in range(count):
        c_far(c).wait_send()
        fo[c] = part(1, c).astype(BF)
        c_near(c).start()
        if fused:
            for step in turn[2 * c : 2 * c + 2]:
                gy_send(step).wait_recv()
                spot = target(step)
                total = gpay[spot, minor].astype(F32) + gyrec[spot].astype(F32)
                if step:
                    gyrec[spot] = total.astype(BF)
                    gz_send(step).start()
                else:
                    ownsum = total
            if c == 0:
                hop(0, at(1)).wait_recv()
                ar[1] = ar[0] + arec[0]
                hop(1, at(2)).start()
    if fused:
        hop(1, at(2)).wait_recv()
        ar[2] = ar[1] + arec[1]
        hop(2, across).start()
        after_z(0)
        dup_ref[...] = last[0, :, :cols]
        ddown_ref[...] = last[0, :, cols:].T
    for copy in loads[2:]:
        copy.wait()
    near = [part(0, c) for c in range(1)]
    if fused:
        hop(2, across).wait_recv()
        ar[3] = ar[2] + arec[2]
        for step in range(1, far):
            z_hop(step).start()
        cross.wait_recv()
        arrived = jnp.concatenate([lastrec[:, :cols], lastrec[:, cols:]], axis=0)
        dout_ref[...] = (last[1, :, :cols] + arrived.astype(F32)).T

    for c in range(count):
        d_normed = near[c] if c < len(near) else part(0, c)
        c_near(c).wait_recv()
        x_far(c).wait_recv()
        d_normed = d_normed + nrec[c].astype(F32) + frec[c].astype(F32)
        spot = slice(c * chunk, (c + 1) * chunk)
        v = tok[spot, :].astype(F32)
        inverse = lax.rsqrt(jnp.mean(v * v, axis=-1, keepdims=True) + EPSILON)
        hat = v * inverse
        scaled = d_normed * gain_ref[...]
        dtok_ref[spot, :] = (
            dhid[spot, :]
            + inverse * (scaled - hat * jnp.mean(scaled * hat, axis=-1, keepdims=True))
        ).astype(BF)
    if fused:
        for step in range(1, far):
            gz_send(step).wait_recv()
            ownsum = ownsum + gzrec[step - 1].astype(F32)
        for i, ref in enumerate((dq_out, dk_out, dv_out)):
            for piece in range(2):
                ref[piece * packed : (piece + 1) * packed, :] = ownsum[
                    i, :, piece * cols : (piece + 1) * cols
                ]
        aorder[major] = ar[3]
        for step in range(1, far):
            z_hop(step).wait_recv()
            aorder[lax.rem(major + far - step, far)] = arec[3 + step]
        sums_ref[...] = (aorder[0] + aorder[1]) + (aorder[2] + aorder[3])
    else:
        dk_out[...] = jnp.zeros_like(dk_out)
        dv_out[...] = jnp.zeros_like(dv_out)
        dout_ref[...] = jnp.zeros_like(dout_ref)
        dup_ref[...] = jnp.zeros_like(dup_ref)
        ddown_ref[...] = jnp.zeros_like(ddown_ref)

    for c in range(count):
        x_far(c).wait_send()
        c_near(c).wait_send()
    if fused:
        for step in range(far):
            x_send(step).wait_send()
            gy_send(step).wait_send()
            for p in range(2):
                y_send(p, step).wait_send()
            if step:
                gz_send(step).wait_send()
                z_hop(step).wait_send()
                for p in range(2):
                    z_send(p, step).wait_send()
        cross.wait_send()
        hop(0, at(1)).wait_send()
        hop(1, at(2)).wait_send()
        hop(2, across).wait_send()


def backward(dp, far, o, lse, drec, factor, idr, idc, gain, xk, early, qkv, xg, pb,
             tokens, d_hidden, normt, wpad):
    heads, _, length = o.shape
    rows, width = tokens.shape
    cols, wide = heads * HD, heads * HP
    depth = width // dp
    packed = depth // 2
    count = rows // TILE
    fused = far > 0
    far_n = max(far, 1)
    vmem = pl.BlockSpec(memory_space=pltpu.VMEM)
    hbm = pl.BlockSpec(memory_space=pl.ANY)
    sem = pltpu.SemaphoreType.DMA
    tiny = jax.ShapeDtypeStruct((8, 128), F32)
    shard = jax.ShapeDtypeStruct((depth, cols), F32) if fused else tiny
    turned = jax.ShapeDtypeStruct((cols, depth), F32) if fused else tiny
    whole = shard if fused else jax.ShapeDtypeStruct((3, width, wide), F32)

    def buf(*shape, dtype=BF, only=True):
        return pltpu.VMEM(shape if fused or not only else (8, 128), dtype)

    pair = 2 * cols
    return pl.pallas_call(
        lambda *refs: back_kernel(dp, far, *refs),
        out_shape=[jax.ShapeDtypeStruct((rows, width), BF), whole, shard, shard, turned, shard,
                   turned, jax.ShapeDtypeStruct((16, width), F32)],
        in_specs=[vmem] * 9 + [hbm] * 7,
        out_specs=[vmem] * 8,
        scratch_shapes=[
            buf(heads, length, HP, only=False),
            buf(length, HP, dtype=F32, only=False),
            buf(length, HP, dtype=F32, only=False),
            buf(HP, length, only=False),
            buf(3, length, wide, only=False),
            buf(rows, width, only=False),
            buf(rows, width, dtype=F32, only=False),
            buf(width, length, only=False),
            buf(3, width, wide, only=False),
            buf(far_n, 2, depth, pair),
            buf(far_n, depth, pair),
            buf(2, far_n, depth, pair),
            buf(2, far_n - 1, depth, pair),
            buf(2, depth, pair, dtype=F32),
            buf(packed, pair),
            buf(packed, pair),
            buf(far_n, 2, 3, packed, pair),
            buf(far_n, 3, packed, pair),
            buf(far_n - 1, 3, packed, pair),
            buf(count, TILE, width, only=False),
            buf(count, TILE, width, only=False),
            buf(count, TILE, width, only=False),
            buf(count, TILE, width, only=False),
            buf(count, TILE, width, only=False),
            buf(8, HP, dtype=F32, only=False),
            buf(dp, depth, dtype=F32),
            buf(4, 16, width, dtype=F32),
            buf(3 + far_n, 16, width, dtype=F32),
            buf(far_n, 16, width, dtype=F32),
            sem((6,)),
            sem((far_n,)), sem((far_n,)),
            sem((2, far_n)), sem((2, far_n)), sem((2, far_n)), sem((2, far_n)),
            sem, sem,
            sem((far_n,)), sem((far_n,)), sem((far_n,)), sem((far_n,)),
            sem((count,)), sem((count,)), sem((count,)), sem((count,)), sem((count,)), sem((count,)),
            sem((3 + far_n,)), sem((3 + far_n,)),
        ],
        compiler_params=pltpu.CompilerParams(
            vmem_limit_bytes=62 << 20, collective_id=3, has_side_effects=True
        ),
    )(o, lse, drec, factor, idr, idc, gain, xk, early, qkv, xg, pb,
      tokens, d_hidden, normt, wpad)


def swap(v, axis, size, mask):
    return lax.ppermute(v, axis, [(i, i ^ mask) for i in range(size)])


def gather_dp(shard):
    return lax.all_gather(shard, "dp", axis=0, tiled=True)


def scatter_dp(grad, size):
    return lax.psum_scatter(grad, "dp", scatter_dimension=0, tiled=True)


def pack(w):
    half = w.shape[0] // 2
    return jnp.concatenate([w[:half], w[half:]], axis=1)


def pad_heads(w):
    rows, cols = w.shape
    w = w.reshape(rows, cols // HD, HD)
    return jnp.pad(w, ((0, 0), (0, 0), (0, HP - HD))).reshape(rows, cols // HD * HP)


def trim_heads(w):
    rows, cols = w.shape
    return w.reshape(rows, cols // HP, HP)[:, :, :HD].reshape(rows, cols // HP * HD)


def body(dp, tensor, tokens, cotangent, block_ids, attn_gain, w_query, w_key, w_value,
         query_scale, w_out, mlp_gain, w_up, b_up, w_down, b_down):
    assert tensor == 4
    here = lax.axis_index("tensor")
    rows, width = tokens.shape
    length = rows * tensor
    cols = w_query.shape[1]
    heads = cols // HD
    order = [here, here ^ 2, here ^ 1, here ^ 3]

    softplus = jnp.log1p(jnp.exp(query_scale))
    factor = SCORE_BASE / math.sqrt(HD) * softplus
    factor_pad = jnp.pad(factor, (0, HP - HD))[None, :]
    idr = block_ids
    idc = block_ids.reshape(length, 1)

    first = (w_query, w_key, w_value)
    second = (w_out.T, w_up, w_down.T)
    far = dp // 2 if dp == 8 else 0
    if far:
        first = jnp.stack([pack(w) for w in first])
        second = jnp.stack([pack(w) for w in second])
    else:
        pair = [jnp.concatenate([w, swap(w, "tensor", tensor, 2)], axis=1) for w in second]
        half = gather_dp(jnp.concatenate(pair, axis=1)).reshape(width, 3, 2 * cols)
        both = jnp.concatenate([half, swap(half, "tensor", tensor, 1)], axis=2)
        full = gather_dp(jnp.concatenate(first, axis=1))
        first = jnp.stack([pad_heads(full[:, i * cols : (i + 1) * cols]) for i in range(3)])
        second = jnp.zeros((3, 16, 128), BF)
    qkv, normed_t, padded, attended, lse, got, wide = front(
        dp, far, tokens, attn_gain[None, :], first, second, jnp.tile(factor_pad, (1, heads)),
        idr, idc, cols,
    )
    if not far:
        wide = both.transpose(1, 0, 2)

    b_rel = jnp.concatenate([lax.dynamic_slice(b_up, (at * cols,), (cols,)) for at in order])
    output, d_hidden, received, xk, xg, pb, early = middle(
        tokens, cotangent, got.reshape(4 * cols, rows), mlp_gain[None, :], b_rel[None, :],
        b_down[None, :], wide,
    )
    depth = width // dp
    if far:
        xk, xg, pb = (v.reshape(far, 2, depth, 2 * cols) for v in (xk, xg, pb))
    d_tokens, s_q, s_k, s_v, s_out, s_up, s_down, sums = backward(
        dp, far, attended, lse, received, factor_pad, idr, idc, attn_gain[None, :], xk, early,
        qkv, xg, pb, tokens, d_hidden, normed_t, padded,
    )
    if far:
        dots = sums[8 : 8 + dp, :depth].reshape(width)
    else:
        dots = lax.psum(jnp.sum(s_q * padded.astype(F32), axis=(0, 2)), ("dp", "tensor"))
        sums = lax.psum(sums, ("dp", "tensor"))
        s_qkv = scatter_dp(jnp.concatenate([trim_heads(g) for g in s_q], axis=1), dp)
        s_q, s_k, s_v = (s_qkv[:, i * cols : (i + 1) * cols] for i in range(3))
        both = xk.astype(F32) + swap(xg, "tensor", tensor, 2).astype(F32)
        both = scatter_dp(both, dp)
        s_up, s_down = both[:, :cols], both[:, cols:].T
        both = scatter_dp(pb.astype(F32), dp)
        s_out = (both[:, :cols] + swap(both[:, cols:], "tensor", tensor, 2)).T
    d_scale = sums[6, :HD] / softplus * jax.nn.sigmoid(query_scale)
    return (
        output,
        d_tokens,
        dots / attn_gain,
        s_q,
        s_k,
        s_v,
        d_scale,
        s_out,
        sums[0],
        s_up,
        sums[2:6, :cols].reshape(4 * cols),
        s_down,
        sums[1],
    )


def solution(mesh):
    weight, turned, whole = P("dp", "tensor"), P("tensor", "dp"), P()
    positions = P(("dp", "tensor"), None)
    return jax.shard_map(
        lambda *args: body(mesh.shape["dp"], mesh.shape["tensor"], *args),
        mesh=mesh,
        in_specs=(positions, positions, P("dp", None), whole, weight, weight, weight, whole,
                  turned, whole, weight, whole, turned, whole),
        out_specs=(positions, positions, whole, weight, weight, weight, whole, turned, whole,
                   weight, whole, turned, whole),
        check_vma=False,
    )
```

```python
import math

import jax
import jax.numpy as jnp
from jax import lax
from jax.experimental import pallas as pl
from jax.experimental.pallas import tpu as pltpu
from jax.sharding import PartitionSpec as P

HD = 80
HP = 128
TILE = 256
BLOCK_MOST = 256
EPSILON = 1e-06
SCORE_BASE = 1.442695041
MASKED = -1e30
BF = jnp.bfloat16
F32 = jnp.float32


def mm(a, b, ca, cb):
    return lax.dot_general(a, b, (((ca,), (cb,)), ((), ())), preferred_element_type=F32)


def reach(tile, length):
    return min((tile + 1) * TILE + BLOCK_MOST, length)


MESH = pl.DeviceIdType.MESH
PARTNERS = (2, 1, 3)
SLOT = {0: 0, 2: 1, 1: 2, 3: 3}


def remote(src, dst, send, recv, where):
    return pltpu.make_async_remote_copy(
        src_ref=src, dst_ref=dst, send_sem=send, recv_sem=recv, device_id=where, device_id_type=MESH
    )


def greet(peers):
    barrier = pltpu.get_barrier_semaphore()
    for where in peers:
        pl.semaphore_signal(barrier, inc=1, device_id=where, device_id_type=MESH)
    pl.semaphore_wait(barrier, len(peers))


def front_kernel(
    dp, far, tok_ref, vec_ref, idr_ref, wq_ref, wk_ref, wv_ref, wo_ref, wu_ref, wd_ref,
    qkv_out, normt_out, wpad_out, att_out, lse_ref, got_out, wide_out,
    norm, normt, wpad, qkv, att, got, vt_ref, idc_ref, w1_ref, w2_ref, z1, y1, x2, pair,
    sx, rx, sc, rc, sf, rf, sz1, rz1, sy1, ry1, sx2, rx2, sz2, rz2, sy2, ry2, sc2, rc2,
    st_, rt_, so,
):
    here, me = lax.axis_index("tensor"), lax.axis_index("dp")
    rows, width = tok_ref.shape
    length = norm.shape[0]
    tiles = length // TILE
    heads = qkv.shape[2] // HP
    cols = heads * HD
    depth = width // dp
    packed = depth // 2
    fused = far > 0
    major, minor = me // 2, me % 2

    def at(mask):
        return (me, here ^ mask)

    across = (me ^ 1, here)

    def along(step):
        return (lax.rem(major + step, far) * 2 + minor, here)

    def source(step):
        return lax.rem(major + far - step, far)

    peers = [at(mask) for mask in PARTNERS]
    if fused:
        peers += [across] + [along(step) for step in range(1, far)]
    greet(peers)

    def z_first(w, step):
        return remote(
            w1_ref.at[w], z1.at[step, w], sz1.at[step, w], rz1.at[step, w], along(step)
        )

    def y_first(w, step):
        src = w1_ref.at[w] if isinstance(step, int) and step == 0 else z1.at[step, w]
        return remote(src, y1.at[step, w], sy1.at[step, w], ry1.at[step, w], across)

    swap_two = remote(w2_ref, x2, sx2, rx2, at(2)) if fused else None
    if fused:
        for w, ref in ((1, wk_ref), (0, wq_ref), (2, wv_ref)):
            w1_ref[w, :, :cols] = ref[:packed, :]
            w1_ref[w, :, cols:] = ref[packed:, :]
            for step in range(1, far):
                z_first(w, step).start()
            y_first(w, 0).start()
        for w, ref in enumerate((wo_ref, wu_ref, wd_ref)):
            shard = ref[...]
            w2_ref[w, :, :cols] = shard[:packed, :]
            w2_ref[w, :, cols:] = shard[packed:, :]
            for part in range(2):
                pair[w, part * packed : (part + 1) * packed, :cols] = shard[
                    part * packed : (part + 1) * packed
                ]
        swap_two.start()

    chunk = TILE
    count = rows // chunk

    @pl.loop(0, count)
    def _(c):
        low = pl.multiple_of(c * chunk, chunk)
        v = tok_ref[pl.ds(low, chunk), :].astype(F32)
        hat = v * lax.rsqrt(jnp.mean(v * v, axis=-1, keepdims=True) + EPSILON)
        norm[pl.ds(pl.multiple_of(here * rows + low, chunk), chunk), :] = (
            hat * vec_ref[0:1, :]
        ).astype(BF)

    def rows_of(mask, c):
        return norm.at[pl.ds(pl.multiple_of((here ^ mask) * rows + c * chunk, chunk), chunk), :]

    def send_x(c):
        return remote(rows_of(0, c), rows_of(0, c), sx.at[c], rx.at[c], at(2))

    def send_c(c):
        return remote(rows_of(0, c), rows_of(0, c), sc.at[c], rc.at[c], at(1))

    def forward(c):
        return remote(rows_of(2, c), rows_of(2, c), sf.at[c], rf.at[c], at(1))

    for c in range(count):
        send_x(c).start()
        send_c(c).start()
    idc_ref[...] = jnp.broadcast_to(idr_ref[...].astype(F32), (HP, length)).T.astype(jnp.int32)

    def project(w, mask, c):
        low = pl.multiple_of((here ^ mask) * rows + c * chunk, chunk)
        x = norm[pl.ds(low, chunk), :]
        y = mm(x, wpad[w], 1, 0)
        if w == 0:
            y = y * vec_ref[4:5, : heads * HP]
        qkv[w, pl.ds(low, chunk), :] = y.astype(BF)
        if w == 2:
            normt[:, pl.ds(low, chunk)] = x.astype(F32).T.astype(BF)

    def rows_two(index):
        return pl.ds(pl.multiple_of(index * depth, 16), depth)

    def z_second(w, step):
        return remote(
            pair.at[w], wide_out.at[w, rows_two(me), pl.ds(0, 2 * cols)],
            sz2.at[w, step], rz2.at[w, step], along(step),
        )

    def block_two(w, index):
        return wide_out.at[w, rows_two(index), pl.ds(0, 2 * cols)]

    def y_second(w, step):
        ref = block_two(w, source(step) * 2 + minor)
        src = pair.at[w] if step == 0 else ref
        return remote(src, ref, sy2.at[w, step], ry2.at[w, step], across)

    def c_second(w, step, side):
        index = source(step) * 2 + (minor if side == 0 else 1 - minor)
        src = pair.at[w] if step == 0 and side == 0 else block_two(w, index)
        return remote(
            src, wide_out.at[w, rows_two(index), pl.ds(2 * cols, 2 * cols)],
            sc2.at[w, step, side], rc2.at[w, step, side], at(1),
        )

    def own_two(w):
        return pltpu.make_async_copy(pair.at[w], block_two(w, me), so.at[8 + w])

    if fused:
        swap_two.wait_recv()
        for w in range(3):
            for part in range(2):
                pair[w, part * packed : (part + 1) * packed, cols:] = x2[
                    w, :, part * cols : (part + 1) * cols
                ]
            own_two(w).start()
            for step in range(1, far):
                z_second(w, step).start()
            y_second(w, 0).start()
            c_second(w, 0, 0).start()

    if not fused:
        wpad[...] = wq_ref[...]
        for c in range(count):
            send_c(c).wait_recv()
        for w in range(3):
            for mask in (0, 1):
                for c in range(count):
                    project(w, mask, c)
    else:
        wpad[...] = jnp.zeros_like(wpad)

        def unpack(w, block, device):
            for part in range(2):
                low = pl.multiple_of(device * depth + part * packed, 16)
                for h in range(heads):
                    lane = part * cols + h * HD
                    wpad[w, pl.ds(low, packed), h * HP : h * HP + HD] = block[:, lane : lane + HD]

        for w in (1, 0, 2):
            unpack(w, w1_ref[w], me)
            for step in range(1, far):
                z_first(w, step).wait_recv()
                y_first(w, step).start()
                unpack(w, z1[step, w], source(step) * 2 + minor)
            for step in range(far):
                y_first(w, step).wait_recv()
                unpack(w, y1[step, w], source(step) * 2 + 1 - minor)
            if w == 1:
                for c in range(count):
                    send_c(c).wait_recv()
            for mask in (0, 1):
                for c in range(count):
                    project(w, mask, c)

    for c in range(count):
        send_x(c).wait_recv()
        forward(c).start()
        for w in range(3):
            project(w, 2, c)
    for c in range(count):
        forward(c).wait_recv()
        for w in range(3):
            project(w, 3, c)

    keep = [
        pltpu.make_async_copy(normt, normt_out, so.at[0]),
        pltpu.make_async_copy(wpad, wpad_out, so.at[1]),
        pltpu.make_async_copy(qkv, qkv_out, so.at[2]),
    ]
    for copy in keep:
        copy.start()

    def trade(h, mask):
        spot = pl.ds(pl.multiple_of((here ^ mask) * rows, HP), rows)
        return remote(
            att.at[h, :, spot], got.at[SLOT[mask], h], st_.at[mask, h], rt_.at[mask, h], at(mask)
        )

    def second_on(w):
        for step in range(1, far):
            z_second(w, step).wait_recv()
            y_second(w, step).start()
            c_second(w, step, 0).start()

    sub = lax.broadcasted_iota(jnp.int32, (HP, length), 0)

    @pl.loop(0, heads)
    def _(h):
        lanes = pl.ds(pl.multiple_of(h * HP, HP), HP)
        vt_ref[...] = jnp.where(sub == HD, 1.0, qkv[2, :, lanes].astype(F32).T).astype(BF)

        def scores(t):
            seen, low = reach(t, length), t * TILE
            st = mm(qkv[1, :seen, lanes], qkv[0, low : low + TILE, lanes], 1, 1)
            visible = idc_ref[low:seen, 0:1] <= idr_ref[:, low : low + TILE]
            masked = jnp.where(visible, st[low:], MASKED)
            return jnp.concatenate([st[:low], masked], 0) if low else masked

        st = scores(0)
        for t in range(tiles):
            later = scores(t + 1) if t + 1 < tiles else None
            seen, low = st.shape[0], t * TILE
            group = jnp.max(st.reshape(seen // 64, 64, TILE), axis=0)
            highest = jnp.max(group, axis=0, keepdims=True)
            weights = jnp.exp(st - highest).astype(BF)
            ot = mm(vt_ref[:, :seen], weights, 1, 0)
            summed = ot[HD : HD + 1, :]
            att[h, :, low : low + TILE] = (ot[:HD] * (1.0 / summed)).astype(BF)
            lse_ref[h, :, low : low + TILE] = highest + jnp.log(summed)
            st = later
        for mask in PARTNERS:
            trade(h, mask).start()
        if fused:

            @pl.when(h > 0)
            def _():
                second_on(h - 1)

    got[0] = att[:, :, pl.ds(pl.multiple_of(here * rows, HP), rows)]
    keep.append(pltpu.make_async_copy(att, att_out, so.at[5]))
    keep[-1].start()
    if fused:
        for w in range(3):
            for step in range(far):
                y_second(w, step).wait_recv()
                c_second(w, step, 1).start()
    for h in range(heads):
        for mask in PARTNERS:
            trade(h, mask).wait_recv()
    keep.append(pltpu.make_async_copy(got, got_out, so.at[6]))
    keep[-1].start()

    for c in range(count):
        send_x(c).wait_send()
        send_c(c).wait_send()
        forward(c).wait_send()
    for h in range(heads):
        for mask in PARTNERS:
            trade(h, mask).wait_send()
    if fused:
        swap_two.wait_send()
        for w in range(3):
            for step in range(far):
                if step:
                    z_first(w, step).wait_send()
                    z_second(w, step).wait_send()
                y_first(w, step).wait_send()
                y_second(w, step).wait_send()
                c_second(w, step, 0).wait()
                c_second(w, step, 1).wait()
        for w in range(3):
            own_two(w).wait()
    for copy in keep:
        copy.wait()


def front(dp, far, tokens, vectors, idr, cols, matrices):
    rows, width = tokens.shape
    length = idr.shape[1]
    heads = cols // HD
    wide = heads * HP
    packed = width // dp // 2
    count = rows // TILE
    vmem = pl.BlockSpec(memory_space=pltpu.VMEM)
    hbm = pl.BlockSpec(memory_space=pl.ANY)
    sem = pltpu.SemaphoreType.DMA
    far_n = max(far, 1)
    fused = far > 0
    small = (packed, 2 * cols) if fused else (16, 128)
    return pl.pallas_call(
        lambda *refs: front_kernel(dp, far, *refs),
        out_shape=[
            jax.ShapeDtypeStruct((3, length, wide), BF),
            jax.ShapeDtypeStruct((width, length), BF),
            jax.ShapeDtypeStruct((3, width, wide), BF),
            jax.ShapeDtypeStruct((heads, HD, length), BF),
            jax.ShapeDtypeStruct((heads, 1, length), F32),
            jax.ShapeDtypeStruct((4, heads, HD, rows), BF),
            jax.ShapeDtypeStruct((3, width, 4 * cols) if fused else (3, 16, 128), BF),
        ],
        in_specs=[vmem] * 9,
        out_specs=[hbm] * 4 + [vmem] + [hbm] * 2,
        scratch_shapes=[
            pltpu.VMEM((length, width), BF),
            pltpu.VMEM((width, length), BF),
            pltpu.VMEM((3, width, wide), BF),
            pltpu.VMEM((3, length, wide), BF),
            pltpu.VMEM((heads, HD, length), BF),
            pltpu.VMEM((4, heads, HD, rows), BF),
            pltpu.VMEM((HP, length), BF),
            pltpu.VMEM((length, HP), jnp.int32),
            pltpu.VMEM((3,) + small, BF),
            pltpu.VMEM((3,) + small, BF),
            pltpu.VMEM((far_n, 3) + small, BF),
            pltpu.VMEM((far_n, 3) + small, BF),
            pltpu.VMEM((3,) + small, BF),
            pltpu.VMEM((3, 2 * packed, 2 * cols) if fused else (3, 16, 128), BF),
            sem((count,)), sem((count,)), sem((count,)), sem((count,)), sem((count,)), sem((count,)),
            sem((far_n, 3)), sem((far_n, 3)), sem((far_n, 3)), sem((far_n, 3)),
            sem, sem,
            sem((3, far_n)), sem((3, far_n)), sem((3, far_n)), sem((3, far_n)),
            sem((3, far_n, 2)), sem((3, far_n, 2)),
            sem((4, heads)), sem((4, heads)),
            sem((12,)),
        ],
        compiler_params=pltpu.CompilerParams(
            vmem_limit_bytes=60 << 20, collective_id=1, has_side_effects=True
        ),
    )(tokens, vectors, idr, *matrices)


def mid_kernel(
    tok_ref, cot_ref, got_ref, vec_ref, wide_ref,
    out_ref, dhid_ref, drec_out, xk_out, xg_out, pb_out, early_ref,
    w, att, n2, act, dpre, branch, hid, give, grec, db, drec, kept, bs,
    ss, rs, sg, rg, so,
):
    here, me = lax.axis_index("tensor"), lax.axis_index("dp")
    rows, width = tok_ref.shape
    wide = w.shape[1]
    cols = wide // 4
    pair = 2 * cols
    chunk = TILE
    half = chunk // 2
    count = rows // chunk

    def at(mask):
        return (me, here ^ mask)

    loads = [pltpu.make_async_copy(wide_ref.at[i], w.at[i], so.at[i]) for i in range(3)]
    for i in (0, 2, 1):
        loads[i].start()
    greet([at(mask) for mask in PARTNERS])
    att[...] = got_ref[...].astype(F32).T.astype(BF)
    early_ref[...] = jnp.zeros_like(early_ref)
    bs[...] = jnp.zeros_like(bs)
    for i in range(3):
        loads[i].wait()

    def trade(c, mask):
        return remote(
            db.at[c, SLOT[mask]], drec.at[c, SLOT[mask]],
            ss.at[c, mask], rs.at[c, mask], at(mask),
        )

    @pl.loop(0, count)
    def _(c):
        low = pl.multiple_of(c * chunk, chunk)
        spot = pl.ds(low, chunk)
        hidden = tok_ref[spot, :].astype(F32) + mm(att[spot, :], w[0], 1, 1)
        hid[spot, :] = hidden
        cot = cot_ref[spot, :]
        d_act = mm(cot, w[2], 1, 0)
        inverse = lax.rsqrt(jnp.mean(hidden * hidden, axis=-1, keepdims=True) + EPSILON)
        hat = hidden * inverse
        normed = (hat * vec_ref[1:2, :]).astype(BF)
        n2[spot, :] = normed
        pre = mm(normed, w[1], 1, 0) + vec_ref[2:3, :]
        sig = jax.nn.sigmoid(pre)
        act[spot, :] = (pre * sig).astype(BF)
        d_pre = (d_act * sig * (1.0 + pre * (1.0 - sig))).astype(BF)
        dpre[spot, :] = d_pre
        d_n2 = mm(d_pre, w[1], 1, 1)
        scaled = d_n2 * vec_ref[1:2, :]
        cot_f32 = cot.astype(F32)
        d_hidden = cot_f32 + inverse * (
            scaled - hat * jnp.mean(scaled * hat, axis=-1, keepdims=True)
        )
        dhid_ref[spot, :] = d_hidden
        br = d_hidden.astype(BF)
        branch[spot, :] = br
        d_att = mm(br, w[0], 1, 0).astype(BF)
        for i in range(4):
            for part in range(2):
                db[c, i, :, part * cols : (part + 1) * cols] = d_att[
                    part * half : (part + 1) * half, i * cols : (i + 1) * cols
                ]
        for mask in PARTNERS:
            trade(c, mask).start()
        drec[c, 0] = db[c, 0]
        early_ref[0:1, :] += jnp.sum(d_n2 * hat, axis=0, keepdims=True)
        early_ref[1:2, :] += jnp.sum(cot_f32, axis=0, keepdims=True)
        bs[0:1, :] += jnp.sum(d_pre.astype(F32), axis=0, keepdims=True)

    pieces = ((branch, att), (n2, dpre), (cot_ref, act))

    def gradient(i, low, first):
        left, right = pieces[i]
        return mm(left[:, pl.ds(low, chunk)], right[:, first : first + pair], 0, 0)

    def hand(i):
        return remote(give.at[i], grec.at[i], sg.at[i], rg.at[i], at(1))

    for i in range(3):

        @pl.loop(0, width // chunk)
        def _(j):
            low = pl.multiple_of(j * chunk, chunk)
            give[i, pl.ds(low, chunk), :] = gradient(i, low, pair).astype(BF)

        hand(i).start()

    for i in range(4):
        place = here ^ (0, 2, 1, 3)[i]
        early_ref[pl.ds(2 + place, 1), 0:cols] = bs[0:1, i * cols : (i + 1) * cols]

    @pl.loop(0, count)
    def _(c):
        spot = pl.ds(pl.multiple_of(c * chunk, chunk), chunk)
        out_ref[spot, :] = (hid[spot, :] + mm(act[spot, :], w[2], 1, 1) + vec_ref[3:4, :]).astype(BF)

    for i in range(3):
        hand(i).wait_recv()

        @pl.loop(0, width // chunk)
        def _(j):
            low = pl.multiple_of(j * chunk, chunk)
            spot = pl.ds(low, chunk)
            total = (gradient(i, low, 0) + grec[i, spot, :].astype(F32)).astype(BF)
            if i == 0:
                kept[2, spot, :] = total
            else:
                lane = (i - 1) * cols
                kept[0, spot, lane : lane + cols] = total[:, :cols]
                kept[1, spot, lane : lane + cols] = total[:, cols:]

        if i == 0:
            keep = [pltpu.make_async_copy(kept.at[2], pb_out, so.at[3])]
            keep[0].start()
    keep.append(pltpu.make_async_copy(kept.at[0], xk_out, so.at[4]))
    keep.append(pltpu.make_async_copy(kept.at[1], xg_out, so.at[5]))
    for copy in keep[1:]:
        copy.start()
    for c in range(count):
        for mask in PARTNERS:
            trade(c, mask).wait_recv()
    keep.append(pltpu.make_async_copy(drec, drec_out, so.at[6]))
    keep[-1].start()
    for c in range(count):
        for mask in PARTNERS:
            trade(c, mask).wait_send()
    for i in range(3):
        hand(i).wait_send()
    for copy in keep:
        copy.wait()


def middle(tokens, cotangent, got, vectors, wide):
    rows, width = tokens.shape
    all_cols = wide.shape[2]
    cols = all_cols // 4
    count = rows // TILE
    vmem = pl.BlockSpec(memory_space=pltpu.VMEM)
    hbm = pl.BlockSpec(memory_space=pl.ANY)
    sem = pltpu.SemaphoreType.DMA
    blocks = (count, 4, TILE // 2, 2 * cols)
    halves = jax.ShapeDtypeStruct((width, 2 * cols), BF)
    return pl.pallas_call(
        mid_kernel,
        out_shape=[
            jax.ShapeDtypeStruct((rows, width), BF),
            jax.ShapeDtypeStruct((rows, width), F32),
            jax.ShapeDtypeStruct(blocks, BF),
            halves,
            halves,
            halves,
            jax.ShapeDtypeStruct((16, width), F32),
        ],
        in_specs=[vmem] * 4 + [hbm],
        out_specs=[vmem, vmem, hbm, hbm, hbm, hbm, vmem],
        scratch_shapes=[
            pltpu.VMEM((3, width, all_cols), BF),
            pltpu.VMEM((rows, all_cols), BF),
            pltpu.VMEM((rows, width), BF),
            pltpu.VMEM((rows, all_cols), BF),
            pltpu.VMEM((rows, all_cols), BF),
            pltpu.VMEM((rows, width), BF),
            pltpu.VMEM((rows, width), F32),
            pltpu.VMEM((3, width, 2 * cols), BF),
            pltpu.VMEM((3, width, 2 * cols), BF),
            pltpu.VMEM(blocks, BF),
            pltpu.VMEM(blocks, BF),
            pltpu.VMEM((3, width, 2 * cols), BF),
            pltpu.VMEM((8, all_cols), F32),
            sem((count, 4)), sem((count, 4)), sem((3,)), sem((3,)), sem((8,)),
        ],
        compiler_params=pltpu.CompilerParams(
            vmem_limit_bytes=60 << 20, collective_id=2, has_side_effects=True
        ),
    )(tokens, cotangent, got, vectors, wide)


def back_kernel(
    dp, far, o_ref, lse_ref, drec_ref, vec_ref, idr_ref, xk_ref, early_ref,
    qkv_hbm, xg_ref, pb_ref, tok_hbm, dhid_hbm, normt_hbm, wpad_hbm,
    dtok_ref, dq_out, dk_out, dv_out, dout_ref, dup_ref, ddown_ref, sums_ref,
    do, dka, dva, kt_ref, idc_ref, dqkv, tok, dhid, normt, wpad,
    xrec, pbown, yrec, zrec, last, lastsend, lastrec,
    gpay, gyrec, gzrec, fo, crec, fs, frec, nrec, qsum, lvec, ar, arec, aorder,
    so, sxa, rxa, sy, ry, sz, rz, sl, rl, sgy, rgy, sgz, rgz, sfo, rfo, sfs, rfs, sno, rno, sar, rar,
):
    here, me = lax.axis_index("tensor"), lax.axis_index("dp")
    heads, _, length = o_ref.shape
    rows, width = tok.shape
    cols = heads * HD
    tiles = length // TILE
    depth = width // dp
    packed = depth // 2
    fused = far > 0
    major, minor = me // 2, me % 2
    chunk = TILE
    count = rows // chunk

    def at(mask):
        return (me, here ^ mask)

    across = (me ^ 1, here)

    def along(step):
        return (lax.rem(major + step, far) * 2 + minor, here)

    def target(step):
        return lax.rem(major + step, far)

    loads = [
        pltpu.make_async_copy(src, dst, so.at[i])
        for i, (src, dst) in enumerate(
            ((wpad_hbm, wpad), (normt_hbm, normt), (tok_hbm, tok), (dhid_hbm, dhid))
        )
    ]
    load_qkv = pltpu.make_async_copy(qkv_hbm, dqkv, so.at[4])
    load_qkv.start()
    if fused:
        load_pb = pltpu.make_async_copy(pb_ref.at[:, minor], pbown, so.at[5])
        load_pb.start()
    for copy in loads:
        copy.start()
    peers = [at(2), at(1)]
    if fused:
        peers += [across] + [along(step) for step in range(1, far)]
    greet(peers)

    turn = list(range(1, far)) + [0]

    def x_send(step):
        spot = target(step)
        return remote(xg_ref.at[spot], xrec.at[spot], sxa.at[step], rxa.at[step], at(2))

    def y_send(p, step):
        spot = target(step)
        src = xrec.at[spot, 1 - minor] if p == 0 else pb_ref.at[spot, 1 - minor]
        return remote(src, yrec.at[p, spot], sy.at[p, step], ry.at[p, step], across)

    def z_send(p, step):
        return remote(
            yrec.at[p, target(step)], zrec.at[p, step - 1],
            sz.at[p, step], rz.at[p, step], along(step),
        )

    def after_x(step):
        x_send(step).wait_recv()
        spot = target(step)
        xrec[spot] = (xk_ref[spot].astype(F32) + xrec[spot].astype(F32)).astype(BF)
        y_send(0, step).start()

    def after_y(p, step):
        y_send(p, step).wait_recv()
        spot = target(step)
        mine = xrec[spot, minor] if p == 0 else pbown[spot]
        total = mine.astype(F32) + yrec[p, spot].astype(F32)
        if step:
            yrec[p, spot] = total.astype(BF)
            z_send(p, step).start()
        else:
            last[p] = total

    def after_z(p):
        for step in range(1, far):
            z_send(p, step).wait_recv()
            last[p] += zrec[p, step - 1].astype(F32)

    if fused:
        for step in turn:
            x_send(step).start()
            y_send(1, step).start()

    do[...] = jnp.zeros_like(do)
    half = chunk // 2
    for c in range(count):
        for i, mask in enumerate((0, 2, 1, 3)):
            block = drec_ref[c, i]
            for part in range(2):
                low = pl.multiple_of((here ^ mask) * rows + c * chunk + part * half, half)
                for h in range(heads):
                    lane = part * cols + h * HD
                    do[h, pl.ds(low, half), 0:HD] = block[:, lane : lane + HD]
    qsum[...] = jnp.zeros_like(qsum)
    idc_ref[...] = jnp.broadcast_to(idr_ref[...].astype(F32), (HP, length)).T.astype(jnp.int32)

    load_qkv.wait()
    if fused:
        load_pb.wait()

    def one_head(h):
        lanes = pl.ds(pl.multiple_of(h * HP, HP), HP)
        kt_ref[...] = dqkv[1, :, lanes].astype(F32).T.astype(BF)
        dka[...] = jnp.zeros_like(dka)
        dva[...] = jnp.zeros_like(dva)
        scale_sum = jnp.zeros((1, HP), F32)
        for t in range(tiles):
            seen, low = reach(t, length), t * TILE
            spot = slice(low, low + TILE)
            qt = dqkv[0, spot, lanes]
            dot_ = do[h, spot, :]
            delta = jnp.sum(
                dot_.astype(F32).T[:HD] * o_ref[h, :, spot].astype(F32), axis=0, keepdims=True
            )
            st = mm(dqkv[1, :seen, lanes], qt, 1, 1)
            p = jnp.exp(st - lse_ref[h, :, spot])
            visible = idc_ref[low:seen, 0:1] <= idr_ref[:, spot]
            pm = jnp.where(visible, p[low:], 0.0)
            p = jnp.concatenate([p[:low], pm], 0) if low else pm
            d_p = mm(dqkv[2, :seen, lanes], dot_, 1, 1)
            ds = (p * (d_p - delta)).astype(BF)
            dva[:seen, :] += mm(p.astype(BF), dot_, 1, 0)
            dka[:seen, :] += mm(ds, qt, 1, 0)
            dq = mm(kt_ref[:, :seen], ds, 1, 0).T
            scale_sum = scale_sum + jnp.sum(dq * qt.astype(F32), axis=0, keepdims=True)
            dqkv[0, spot, lanes] = (dq * vec_ref[4:5, :HP]).astype(BF)
        dqkv[1, :, lanes] = dka[...].astype(BF)
        dqkv[2, :, lanes] = dva[...].astype(BF)
        qsum[0:1, :] += scale_sum

    @pl.loop(0, heads)
    def _(h):
        one_head(h)
        if fused:
            for n in range(far):

                @pl.when(h == n)
                def _(n=n):
                    after_x(turn[n])
                    after_y(1, turn[n])
                    if n:
                        after_y(0, turn[n - 1])

    for copy in loads[:2]:
        copy.wait()

    def part(mask, c):
        spot = pl.ds(pl.multiple_of((here ^ mask) * rows + c * chunk, chunk), chunk)
        total = mm(dqkv[0, spot, :], wpad[0], 1, 1)
        total = total + mm(dqkv[1, spot, :], wpad[1], 1, 1)
        return total + mm(dqkv[2, spot, :], wpad[2], 1, 1)

    def c_far(c):
        return remote(fo.at[c], crec.at[c], sfo.at[c], rfo.at[c], at(1))

    def x_far(c):
        return remote(fs.at[c], frec.at[c], sfs.at[c], rfs.at[c], at(2))

    def c_near(c):
        return remote(fo.at[c], nrec.at[c], sno.at[c], rno.at[c], at(1))

    def weight_blocks(step):
        spot = target(step)
        low = pl.multiple_of(spot * 2 * depth, 16)
        dots = jnp.zeros((2 * depth, 1), F32)
        for i in range(3):
            g = mm(normt[pl.ds(low, 2 * depth), :], dqkv[i], 1, 0)
            dots = dots + jnp.sum(
                g * wpad[i, pl.ds(low, 2 * depth), :].astype(F32), axis=1, keepdims=True
            )
            g = g.astype(BF)
            for side in range(2):
                for h in range(heads):
                    for piece in range(2):
                        lane, top = piece * cols + h * HD, (2 * side + piece) * packed
                        gpay[spot, side, i, :, lane : lane + HD] = g[
                            top : top + packed, h * HP : h * HP + HD
                        ]
        flat = jnp.broadcast_to(dots, (2 * depth, HP)).T[0:1, :]
        lvec[pl.ds(spot * 2, 1), :] = flat[:, :depth]
        lvec[pl.ds(spot * 2 + 1, 1), :] = flat[:, depth:]

    def gy_send(step):
        spot = target(step)
        return remote(
            gpay.at[spot, 1 - minor], gyrec.at[spot], sgy.at[step], rgy.at[step], across
        )

    def gz_send(step):
        return remote(
            gyrec.at[target(step)], gzrec.at[step - 1], sgz.at[step], rgz.at[step], along(step)
        )

    def far_chunk(c):
        fo[c] = part(3, c).astype(BF)
        c_far(c).start()

    def far_finish(c):
        own = part(2, c)
        c_far(c).wait_recv()
        fs[c] = (own + crec[c].astype(F32)).astype(BF)
        x_far(c).start()

    far_chunk(0)
    far_finish(0)
    if fused:
        for n, step in enumerate(turn):
            weight_blocks(step)
            gy_send(step).start()
            if n == 0:
                after_y(0, turn[far - 1])
            if n == 1:
                far_chunk(1)
            if n == 2:
                far_finish(1)
                after_z(1)
    else:
        for c in range(1, count):
            far_chunk(c)
            far_finish(c)

        @pl.loop(0, 3)
        def _(i):
            for j in range(width // chunk):
                dq_out[i, j * chunk : (j + 1) * chunk, :] = mm(
                    normt[j * chunk : (j + 1) * chunk, :], dqkv[i], 1, 0
                )

    def hop(n, where):
        return remote(ar.at[n], arec.at[n], sar.at[n], rar.at[n], where)

    def z_hop(step):
        return remote(ar.at[3], arec.at[3 + step], sar.at[3 + step], rar.at[3 + step], along(step))

    if fused:
        ar[0] = jnp.zeros_like(ar[0])
        ar[0, 0:6, :] = early_ref[0:6, :]
        ar[0, 6:7, 0:HP] = qsum[0:1, :]
        ar[0, 8:16, 0:depth] = lvec[...]
        hop(0, at(1)).start()
        for piece in range(2):
            last_half = last[1, piece * packed : (piece + 1) * packed, cols:]
            lastsend[:, piece * cols : (piece + 1) * cols] = last_half.astype(BF)
        cross = remote(lastsend, lastrec, sl, rl, at(2))
        cross.start()
    else:
        sums_ref[...] = jnp.zeros_like(sums_ref)
        sums_ref[0:6, :] = early_ref[0:6, :]
        sums_ref[6:7, 0:HP] = qsum[0:1, :]

    for c in range(count):
        c_far(c).wait_send()
        fo[c] = part(1, c).astype(BF)
        c_near(c).start()
        if fused:
            for step in turn[2 * c : 2 * c + 2]:
                gy_send(step).wait_recv()
                spot = target(step)
                total = gpay[spot, minor].astype(F32) + gyrec[spot].astype(F32)
                if step:
                    gyrec[spot] = total.astype(BF)
                    gz_send(step).start()
                else:
                    ownsum = total
            if c == 0:
                hop(0, at(1)).wait_recv()
                ar[1] = ar[0] + arec[0]
                hop(1, at(2)).start()
    if fused:
        hop(1, at(2)).wait_recv()
        ar[2] = ar[1] + arec[1]
        hop(2, across).start()
        after_z(0)
        dup_ref[...] = last[0, :, :cols]
        ddown_ref[...] = last[0, :, cols:]
    for copy in loads[2:]:
        copy.wait()
    near = [part(0, c) for c in range(1)]
    if fused:
        hop(2, across).wait_recv()
        ar[3] = ar[2] + arec[2]
        for step in range(1, far):
            z_hop(step).start()
        cross.wait_recv()
        arrived = jnp.concatenate([lastrec[:, :cols], lastrec[:, cols:]], axis=0)
        dout_ref[...] = last[1, :, :cols] + arrived.astype(F32)

    for c in range(count):
        d_normed = near[c] if c < len(near) else part(0, c)
        c_near(c).wait_recv()
        x_far(c).wait_recv()
        d_normed = d_normed + nrec[c].astype(F32) + frec[c].astype(F32)
        spot = slice(c * chunk, (c + 1) * chunk)
        v = tok[spot, :].astype(F32)
        inverse = lax.rsqrt(jnp.mean(v * v, axis=-1, keepdims=True) + EPSILON)
        hat = v * inverse
        scaled = d_normed * vec_ref[0:1, :]
        dtok_ref[spot, :] = (
            dhid[spot, :]
            + inverse * (scaled - hat * jnp.mean(scaled * hat, axis=-1, keepdims=True))
        ).astype(BF)
    if fused:
        for step in range(1, far):
            gz_send(step).wait_recv()
            ownsum = ownsum + gzrec[step - 1].astype(F32)
        for i, ref in enumerate((dq_out, dk_out, dv_out)):
            for piece in range(2):
                ref[piece * packed : (piece + 1) * packed, :] = ownsum[
                    i, :, piece * cols : (piece + 1) * cols
                ]
        aorder[major] = ar[3]
        for step in range(1, far):
            z_hop(step).wait_recv()
            aorder[lax.rem(major + far - step, far)] = arec[3 + step]
        sums_ref[...] = (aorder[0] + aorder[1]) + (aorder[2] + aorder[3])
    else:
        dk_out[...] = jnp.zeros_like(dk_out)
        dv_out[...] = jnp.zeros_like(dv_out)
        dout_ref[...] = jnp.zeros_like(dout_ref)
        dup_ref[...] = jnp.zeros_like(dup_ref)
        ddown_ref[...] = jnp.zeros_like(ddown_ref)

    for c in range(count):
        x_far(c).wait_send()
        c_near(c).wait_send()
    if fused:
        for step in range(far):
            x_send(step).wait_send()
            gy_send(step).wait_send()
            for p in range(2):
                y_send(p, step).wait_send()
            if step:
                gz_send(step).wait_send()
                z_hop(step).wait_send()
                for p in range(2):
                    z_send(p, step).wait_send()
        cross.wait_send()
        hop(0, at(1)).wait_send()
        hop(1, at(2)).wait_send()
        hop(2, across).wait_send()


def backward(dp, far, o, lse, drec, vectors, idr, xk, early, qkv, xg, pb,
             tokens, d_hidden, normt, wpad):
    heads, _, length = o.shape
    rows, width = tokens.shape
    cols, wide = heads * HD, heads * HP
    depth = width // dp
    packed = depth // 2
    count = rows // TILE
    fused = far > 0
    far_n = max(far, 1)
    vmem = pl.BlockSpec(memory_space=pltpu.VMEM)
    hbm = pl.BlockSpec(memory_space=pl.ANY)
    sem = pltpu.SemaphoreType.DMA
    tiny = jax.ShapeDtypeStruct((8, 128), F32)
    shard = jax.ShapeDtypeStruct((depth, cols), F32) if fused else tiny
    whole = shard if fused else jax.ShapeDtypeStruct((3, width, wide), F32)

    def buf(*shape, dtype=BF, only=True):
        return pltpu.VMEM(shape if fused or not only else (8, 128), dtype)

    pair = 2 * cols
    return pl.pallas_call(
        lambda *refs: back_kernel(dp, far, *refs),
        out_shape=[jax.ShapeDtypeStruct((rows, width), BF), whole, shard, shard, shard, shard,
                   shard, jax.ShapeDtypeStruct((16, width), F32)],
        in_specs=[vmem] * 7 + [hbm] * 7,
        out_specs=[vmem] * 8,
        scratch_shapes=[
            buf(heads, length, HP, only=False),
            buf(length, HP, dtype=F32, only=False),
            buf(length, HP, dtype=F32, only=False),
            buf(HP, length, only=False),
            buf(length, HP, dtype=jnp.int32, only=False),
            buf(3, length, wide, only=False),
            buf(rows, width, only=False),
            buf(rows, width, dtype=F32, only=False),
            buf(width, length, only=False),
            buf(3, width, wide, only=False),
            buf(far_n, 2, depth, pair),
            buf(far_n, depth, pair),
            buf(2, far_n, depth, pair),
            buf(2, far_n - 1, depth, pair),
            buf(2, depth, pair, dtype=F32),
            buf(packed, pair),
            buf(packed, pair),
            buf(far_n, 2, 3, packed, pair),
            buf(far_n, 3, packed, pair),
            buf(far_n - 1, 3, packed, pair),
            buf(count, TILE, width, only=False),
            buf(count, TILE, width, only=False),
            buf(count, TILE, width, only=False),
            buf(count, TILE, width, only=False),
            buf(count, TILE, width, only=False),
            buf(8, HP, dtype=F32, only=False),
            buf(dp, depth, dtype=F32),
            buf(4, 16, width, dtype=F32),
            buf(3 + far_n, 16, width, dtype=F32),
            buf(far_n, 16, width, dtype=F32),
            sem((6,)),
            sem((far_n,)), sem((far_n,)),
            sem((2, far_n)), sem((2, far_n)), sem((2, far_n)), sem((2, far_n)),
            sem, sem,
            sem((far_n,)), sem((far_n,)), sem((far_n,)), sem((far_n,)),
            sem((count,)), sem((count,)), sem((count,)), sem((count,)), sem((count,)), sem((count,)),
            sem((3 + far_n,)), sem((3 + far_n,)),
        ],
        compiler_params=pltpu.CompilerParams(
            vmem_limit_bytes=62 << 20, collective_id=3, has_side_effects=True
        ),
    )(o, lse, drec, vectors, idr, xk, early, qkv, xg, pb,
      tokens, d_hidden, normt, wpad)


def finish_kernel(dp, cols, scale_ref, sums_ref, vec_ref, *refs):
    moves, outs, held = refs[:8], refs[8:21], refs[21:29]
    row, sem = refs[29:]
    width = vec_ref.shape[1]
    depth = width // dp
    places = (0, 1, 3, 4, 5, 7, 9, 11)
    enter = [pltpu.make_async_copy(moves[i], held[i], sem.at[i]) for i in range(8)]
    leave = [pltpu.make_async_copy(held[i], outs[places[i]], sem.at[8 + i]) for i in range(8)]
    for copy in enter:
        copy.start()
    outs[6][...] = sums_ref[6, 0:HP] * scale_ref[0, :]
    outs[8][...] = sums_ref[0, :]
    outs[12][...] = sums_ref[1, :]
    row[...] = jnp.zeros_like(row)
    for i in range(width // cols):
        row[0:1, i * cols : (i + 1) * cols] = sums_ref[2 + i : 3 + i, :cols]
    for i in range(dp):
        spot = slice(i * depth, (i + 1) * depth)
        row[1:2, spot] = sums_ref[8 + i : 9 + i, :depth] / vec_ref[0:1, spot]
    outs[10][...] = row[0, :]
    outs[2][...] = row[1, :]
    for come, go in zip(enter, leave):
        come.wait()
        go.start()
    for copy in leave:
        copy.wait()


def finish(dp, cols, scale, sums, vectors, moves):
    width = vectors.shape[1]
    vmem = pl.BlockSpec(memory_space=pltpu.VMEM)
    hbm = pl.BlockSpec(memory_space=pl.ANY)
    row = jax.ShapeDtypeStruct((width,), F32)
    like = [jax.ShapeDtypeStruct(v.shape, v.dtype) for v in moves]
    shapes = like[:2] + [row] + like[2:5] + [jax.ShapeDtypeStruct((HP,), F32)]
    shapes += [like[5], row, like[6], row, like[7], row]
    small = (2, 6, 8, 10, 12)
    return pl.pallas_call(
        lambda *refs: finish_kernel(dp, cols, *refs),
        out_shape=shapes,
        in_specs=[vmem] * 3 + [hbm] * 8,
        out_specs=[vmem if i in small else hbm for i in range(13)],
        scratch_shapes=[pltpu.VMEM(v.shape, v.dtype) for v in moves]
        + [pltpu.VMEM((8, width), F32), pltpu.SemaphoreType.DMA((16,))],
        compiler_params=pltpu.CompilerParams(vmem_limit_bytes=60 << 20),
    )(scale, sums, vectors, *moves)


def swap(v, axis, size, mask):
    return lax.ppermute(v, axis, [(i, i ^ mask) for i in range(size)])


def gather_dp(shard):
    return lax.all_gather(shard, "dp", axis=0, tiled=True)


def scatter_dp(grad, size):
    return lax.psum_scatter(grad, "dp", scatter_dimension=0, tiled=True)


def pad_heads(w):
    rows, cols = w.shape
    w = w.reshape(rows, cols // HD, HD)
    return jnp.pad(w, ((0, 0), (0, 0), (0, HP - HD))).reshape(rows, cols // HD * HP)


def trim_heads(w):
    rows, cols = w.shape
    return w.reshape(rows, cols // HP, HP)[:, :, :HD].reshape(rows, cols // HP * HD)


def body(dp, tensor, tokens, cotangent, block_ids, attn_gain, w_query, w_key, w_value,
         query_scale, w_out, mlp_gain, w_up, b_up, w_down, b_down):
    assert tensor == 4
    here = lax.axis_index("tensor")
    rows, width = tokens.shape
    length = rows * tensor
    cols = w_query.shape[1]
    heads = cols // HD
    order = [here, here ^ 2, here ^ 1, here ^ 3]

    softplus = jnp.log1p(jnp.exp(query_scale))
    factor = jnp.pad(SCORE_BASE / math.sqrt(HD) * softplus, (0, HP - HD))
    b_rel = jnp.concatenate([lax.dynamic_slice(b_up, (at * cols,), (cols,)) for at in order])
    repeat = jnp.pad(jnp.tile(factor, heads), (0, width - heads * HP))
    vectors = jnp.concatenate([attn_gain, mlp_gain, b_rel, b_down, repeat]).reshape(5, width)

    far = dp // 2 if dp == 8 else 0
    matrices = (w_query, w_key, w_value, w_out.T, w_up, w_down.T)
    if not far:
        pair = [jnp.concatenate([w, swap(w, "tensor", tensor, 2)], axis=1) for w in matrices[3:]]
        half = gather_dp(jnp.concatenate(pair, axis=1)).reshape(width, 3, 2 * cols)
        both = jnp.concatenate([half, swap(half, "tensor", tensor, 1)], axis=2)
        full = gather_dp(jnp.concatenate(matrices[:3], axis=1))
        first = jnp.stack([pad_heads(full[:, i * cols : (i + 1) * cols]) for i in range(3)])
        matrices = (first,) + matrices[1:]
    qkv, normed_t, padded, attended, lse, got, wide = front(
        dp, far, tokens, vectors, block_ids, cols, matrices
    )
    if not far:
        wide = both.transpose(1, 0, 2)

    output, d_hidden, received, xk, xg, pb, early = middle(
        tokens, cotangent, got.reshape(4 * cols, rows), vectors, wide
    )
    depth = width // dp
    if far:
        xk, xg, pb = (v.reshape(far, 2, depth, 2 * cols) for v in (xk, xg, pb))
    d_tokens, s_q, s_k, s_v, s_out, s_up, s_down, sums = backward(
        dp, far, attended, lse, received, vectors, block_ids, xk, early,
        qkv, xg, pb, tokens, d_hidden, normed_t, padded,
    )
    slope = jax.nn.sigmoid(query_scale) / softplus
    if far:
        scale = jnp.pad(slope, (0, HP - HD))[None, :]
        final = list(
            finish(
                dp, cols, scale, sums, vectors,
                (output, d_tokens, s_q, s_k, s_v, s_out, s_up, s_down),
            )
        )
        final[6] = final[6][:HD]
        final[7], final[11] = final[7].T, final[11].T
        return tuple(final)
    else:
        dots = lax.psum(jnp.sum(s_q * padded.astype(F32), axis=(0, 2)), ("dp", "tensor"))
        sums = lax.psum(sums, ("dp", "tensor"))
        s_qkv = scatter_dp(jnp.concatenate([trim_heads(g) for g in s_q], axis=1), dp)
        s_q, s_k, s_v = (s_qkv[:, i * cols : (i + 1) * cols] for i in range(3))
        both = xk.astype(F32) + swap(xg, "tensor", tensor, 2).astype(F32)
        both = scatter_dp(both, dp)
        s_up, s_down = both[:, :cols], both[:, cols:].T
        both = scatter_dp(pb.astype(F32), dp)
        s_out = (both[:, :cols] + swap(both[:, cols:], "tensor", tensor, 2)).T
    d_scale = sums[6, :HD] * slope
    return (
        output,
        d_tokens,
        dots / attn_gain,
        s_q,
        s_k,
        s_v,
        d_scale,
        s_out,
        sums[0],
        s_up,
        sums[2:6, :cols].reshape(4 * cols),
        s_down,
        sums[1],
    )


def solution(mesh):
    weight, turned, whole = P("dp", "tensor"), P("tensor", "dp"), P()
    positions = P(("dp", "tensor"), None)
    return jax.shard_map(
        lambda *args: body(mesh.shape["dp"], mesh.shape["tensor"], *args),
        mesh=mesh,
        in_specs=(positions, positions, P("dp", None), whole, weight, weight, weight, whole,
                  turned, whole, weight, whole, turned, whole),
        out_specs=(positions, positions, whole, weight, weight, weight, whole, turned, whole,
                   weight, whole, turned, whole),
        check_vma=False,
    )
```

```python
import math

import jax
import jax.numpy as jnp
from jax import lax
from jax.experimental import pallas as pl
from jax.experimental.pallas import tpu as pltpu
from jax.sharding import PartitionSpec as P

HD = 80
HP = 128
TILE = 256
BLOCK_MOST = 256
EPSILON = 1e-06
SCORE_BASE = 1.442695041
MASKED = -1e30
BF = jnp.bfloat16
F32 = jnp.float32


def mm(a, b, ca, cb):
    return lax.dot_general(a, b, (((ca,), (cb,)), ((), ())), preferred_element_type=F32)


def reach(tile, length):
    return min((tile + 1) * TILE + BLOCK_MOST, length)


MESH = pl.DeviceIdType.MESH
PARTNERS = (2, 1, 3)
SLOT = {0: 0, 2: 1, 1: 2, 3: 3}


def remote(src, dst, send, recv, where):
    return pltpu.make_async_remote_copy(
        src_ref=src, dst_ref=dst, send_sem=send, recv_sem=recv, device_id=where, device_id_type=MESH
    )


def greet(peers):
    barrier = pltpu.get_barrier_semaphore()
    for where in peers:
        pl.semaphore_signal(barrier, inc=1, device_id=where, device_id_type=MESH)
    pl.semaphore_wait(barrier, len(peers))


def front_kernel(
    dp, far, tok_ref, vec_ref, idr_ref, wq_ref, wk_ref, wv_ref, wo_ref, wu_ref, wd_ref,
    qkv_out, normt_out, wpad_out, att_out, lse_ref, got_out, both_out, wide_out,
    norm, normt, wpad, qkv, att, got, vt_ref, idc_ref, w1_ref, w2_ref, z1, y1, x2, pair,
    sx, rx, sc, rc, sf, rf, sz1, rz1, sy1, ry1, sx2, rx2, sz2, rz2, sy2, ry2, sc2, rc2,
    sx3, rx3, sc3, rc3, st_, rt_, so,
):
    here, me = lax.axis_index("tensor"), lax.axis_index("dp")
    rows, width = tok_ref.shape
    length = norm.shape[0]
    tiles = length // TILE
    heads = qkv.shape[2] // HP
    cols = heads * HD
    depth = width // dp
    packed = depth // 2
    fused = far > 0
    major, minor = me // 2, me % 2

    def at(mask):
        return (me, here ^ mask)

    across = (me ^ 1, here)

    def along(step):
        return (lax.rem(major + step, far) * 2 + minor, here)

    def source(step):
        return lax.rem(major + far - step, far)

    peers = [at(mask) for mask in PARTNERS]
    if fused:
        peers += [across] + [along(step) for step in range(1, far)]
    greet(peers)

    def z_first(w, step):
        return remote(
            w1_ref.at[w], z1.at[step, w], sz1.at[step, w], rz1.at[step, w], along(step)
        )

    def y_first(w, step):
        src = w1_ref.at[w] if isinstance(step, int) and step == 0 else z1.at[step, w]
        return remote(src, y1.at[step, w], sy1.at[step, w], ry1.at[step, w], across)

    swap_two = remote(w2_ref, x2, sx2, rx2, at(2)) if fused else None
    if fused:
        for w, ref in ((1, wk_ref), (0, wq_ref), (2, wv_ref)):
            w1_ref[w, :, :cols] = ref[:packed, :]
            w1_ref[w, :, cols:] = ref[packed:, :]
            for step in range(1, far):
                z_first(w, step).start()
            y_first(w, 0).start()
        pair[0, :, :cols] = wu_ref[...]
        pair[0, :, cols:] = wd_ref[...]
        pair[1, :, :cols] = wo_ref[...]
        w2_ref[:, :cols] = wo_ref[:packed, :]
        w2_ref[:, cols:] = wo_ref[packed:, :]
        swap_two.start()

    chunk = TILE
    count = rows // chunk

    @pl.loop(0, count)
    def _(c):
        low = pl.multiple_of(c * chunk, chunk)
        v = tok_ref[pl.ds(low, chunk), :].astype(F32)
        hat = v * lax.rsqrt(jnp.mean(v * v, axis=-1, keepdims=True) + EPSILON)
        norm[pl.ds(pl.multiple_of(here * rows + low, chunk), chunk), :] = (
            hat * vec_ref[0:1, :]
        ).astype(BF)

    def rows_of(mask, c):
        return norm.at[pl.ds(pl.multiple_of((here ^ mask) * rows + c * chunk, chunk), chunk), :]

    def send_x(c):
        return remote(rows_of(0, c), rows_of(0, c), sx.at[c], rx.at[c], at(2))

    def send_c(c):
        return remote(rows_of(0, c), rows_of(0, c), sc.at[c], rc.at[c], at(1))

    def forward(c):
        return remote(rows_of(2, c), rows_of(2, c), sf.at[c], rf.at[c], at(1))

    for c in range(count):
        send_x(c).start()
        send_c(c).start()
    idc_ref[...] = jnp.broadcast_to(idr_ref[...].astype(F32), (HP, length)).T.astype(jnp.int32)

    def project(w, mask, c):
        low = pl.multiple_of((here ^ mask) * rows + c * chunk, chunk)
        x = norm[pl.ds(low, chunk), :]
        y = mm(x, wpad[w], 1, 0)
        if w == 0:
            y = y * vec_ref[4:5, : heads * HP]
        qkv[w, pl.ds(low, chunk), :] = y.astype(BF)
        if w == 2:
            normt[:, pl.ds(low, chunk)] = x.astype(F32).T.astype(BF)

    def rows_two(index):
        return pl.ds(pl.multiple_of(index * depth, 16), depth)

    def index_of(step, side):
        return source(step) * 2 + (minor if side == 0 else 1 - minor)

    def block_two(p, index):
        if p == 0:
            return both_out.at[0, rows_two(index), :]
        return wide_out.at[rows_two(index), pl.ds(0, 2 * cols)]

    def held_two(p, step, side):
        return pair.at[p] if step == 0 and side == 0 else block_two(p, index_of(step, side))

    def z_second(p, step):
        return remote(
            pair.at[p], block_two(p, me), sz2.at[p, step], rz2.at[p, step], along(step)
        )

    def y_second(p, step):
        return remote(
            held_two(p, step, 0), block_two(p, index_of(step, 0)),
            sy2.at[p, step], ry2.at[p, step], across,
        )

    def c_second(p, step, side):
        index = index_of(step, side)
        if p == 0:
            dst = both_out.at[2, rows_two(index), :]
        else:
            dst = wide_out.at[rows_two(index), pl.ds(2 * cols, 2 * cols)]
        return remote(
            held_two(p, step, side), dst, sc2.at[p, step, side], rc2.at[p, step, side], at(1)
        )

    def x_second(step, side):
        return remote(
            held_two(0, step, side), both_out.at[1, rows_two(index_of(step, side)), :],
            sx3.at[step, side], rx3.at[step, side], at(2),
        )

    def c_third(step, side):
        spot = rows_two(index_of(step, side))
        return remote(
            both_out.at[1, spot, :], both_out.at[3, spot, :],
            sc3.at[step, side], rc3.at[step, side], at(1),
        )

    def own_two(p):
        return pltpu.make_async_copy(pair.at[p], block_two(p, me), so.at[8 + p])

    def start_second(p):
        for step in range(1, far):
            z_second(p, step).start()
        y_second(p, 0).start()
        own_two(p).start()

    def spread(p, step, side):
        c_second(p, step, side).start()
        if p == 0:
            x_second(step, side).start()

    def after_z(p):
        for step in range(1, far):
            z_second(p, step).wait_recv()
            y_second(p, step).start()
            spread(p, step, 0)

    def after_y(p, step):
        y_second(p, step).wait_recv()
        spread(p, step, 1)

    if fused:
        start_second(0)
        spread(0, 0, 0)
        swap_two.wait_recv()
        for part in range(2):
            pair[1, part * packed : (part + 1) * packed, cols:] = x2[
                :, part * cols : (part + 1) * cols
            ]
        start_second(1)
        spread(1, 0, 0)

    if not fused:
        wpad[...] = wq_ref[...]
        for c in range(count):
            send_c(c).wait_recv()
        for w in range(3):
            for mask in (0, 1):
                for c in range(count):
                    project(w, mask, c)
    else:
        wpad[...] = jnp.zeros_like(wpad)

        def unpack(w, block, device):
            for part in range(2):
                low = pl.multiple_of(device * depth + part * packed, 16)
                for h in range(heads):
                    lane = part * cols + h * HD
                    wpad[w, pl.ds(low, packed), h * HP : h * HP + HD] = block[:, lane : lane + HD]

        for w in (1, 0, 2):
            unpack(w, w1_ref[w], me)
            for step in range(1, far):
                z_first(w, step).wait_recv()
                y_first(w, step).start()
                unpack(w, z1[step, w], source(step) * 2 + minor)
            for step in range(far):
                y_first(w, step).wait_recv()
                unpack(w, y1[step, w], source(step) * 2 + 1 - minor)
            if w == 1:
                for c in range(count):
                    send_c(c).wait_recv()
            for mask in (0, 1):
                for c in range(count):
                    project(w, mask, c)
            if w == 0:
                after_y(0, 0)
        after_z(0)

    for c in range(count):
        send_x(c).wait_recv()
        forward(c).start()
        for w in range(3):
            project(w, 2, c)
    for c in range(count):
        forward(c).wait_recv()
        for w in range(3):
            project(w, 3, c)

    keep = [
        pltpu.make_async_copy(normt, normt_out, so.at[0]),
        pltpu.make_async_copy(wpad, wpad_out, so.at[1]),
        pltpu.make_async_copy(qkv, qkv_out, so.at[2]),
    ]
    for copy in keep:
        copy.start()

    def trade(h, mask):
        spot = pl.ds(pl.multiple_of((here ^ mask) * rows, HP), rows)
        return remote(
            att.at[h, :, spot], got.at[SLOT[mask], h], st_.at[mask, h], rt_.at[mask, h], at(mask)
        )

    sub = lax.broadcasted_iota(jnp.int32, (HP, length), 0)

    @pl.loop(0, heads)
    def _(h):
        lanes = pl.ds(pl.multiple_of(h * HP, HP), HP)
        vt_ref[...] = jnp.where(sub == HD, 1.0, qkv[2, :, lanes].astype(F32).T).astype(BF)

        def scores(t):
            seen, low = reach(t, length), t * TILE
            st = mm(qkv[1, :seen, lanes], qkv[0, low : low + TILE, lanes], 1, 1)
            visible = idc_ref[low:seen, 0:1] <= idr_ref[:, low : low + TILE]
            masked = jnp.where(visible, st[low:], MASKED)
            return jnp.concatenate([st[:low], masked], 0) if low else masked

        st = scores(0)
        for t in range(tiles):
            later = scores(t + 1) if t + 1 < tiles else None
            seen, low = st.shape[0], t * TILE
            group = jnp.max(st.reshape(seen // 64, 64, TILE), axis=0)
            highest = jnp.max(group, axis=0, keepdims=True)
            weights = jnp.exp(st - highest).astype(BF)
            ot = mm(vt_ref[:, :seen], weights, 1, 0)
            summed = ot[HD : HD + 1, :]
            att[h, :, low : low + TILE] = (ot[:HD] * (1.0 / summed)).astype(BF)
            lse_ref[h, :, low : low + TILE] = highest + jnp.log(summed)
            st = later
        for mask in PARTNERS:
            trade(h, mask).start()
        if fused:
            for n in range(heads):

                @pl.when(h == n)
                def _(n=n):
                    if n == 0:
                        after_y(0, 1)
                    if n == 1:
                        after_y(0, 2)
                        after_y(0, 3)
                    if n == 2:
                        after_z(1)
                        after_y(1, 0)

    got[0] = att[:, :, pl.ds(pl.multiple_of(here * rows, HP), rows)]
    keep.append(pltpu.make_async_copy(att, att_out, so.at[5]))
    keep[-1].start()
    if fused:
        for step in range(far):
            x_second(step, 0).wait_recv()
            c_third(step, 0).start()
        for step in range(1, far):
            after_y(1, step)
        for step in range(far):
            x_second(step, 1).wait_recv()
            c_third(step, 1).start()
    for h in range(heads):
        for mask in PARTNERS:
            trade(h, mask).wait_recv()
    keep.append(pltpu.make_async_copy(got, got_out, so.at[6]))
    keep[-1].start()

    for c in range(count):
        send_x(c).wait_send()
        send_c(c).wait_send()
        forward(c).wait_send()
    for h in range(heads):
        for mask in PARTNERS:
            trade(h, mask).wait_send()
    if fused:
        swap_two.wait_send()
        for w in range(3):
            for step in range(far):
                if step:
                    z_first(w, step).wait_send()
                y_first(w, step).wait_send()
        for p in range(2):
            own_two(p).wait()
            for step in range(far):
                if step:
                    z_second(p, step).wait_send()
                y_second(p, step).wait_send()
                for side in range(2):
                    c_second(p, step, side).wait()
                    if p == 0:
                        x_second(step, side).wait_send()
                        c_third(step, side).wait()
    for copy in keep:
        copy.wait()


def front(dp, far, tokens, vectors, idr, cols, matrices):
    rows, width = tokens.shape
    length = idr.shape[1]
    heads = cols // HD
    wide = heads * HP
    packed = width // dp // 2
    count = rows // TILE
    vmem = pl.BlockSpec(memory_space=pltpu.VMEM)
    hbm = pl.BlockSpec(memory_space=pl.ANY)
    sem = pltpu.SemaphoreType.DMA
    far_n = max(far, 1)
    fused = far > 0
    small = (packed, 2 * cols) if fused else (16, 128)
    return pl.pallas_call(
        lambda *refs: front_kernel(dp, far, *refs),
        out_shape=[
            jax.ShapeDtypeStruct((3, length, wide), BF),
            jax.ShapeDtypeStruct((width, length), BF),
            jax.ShapeDtypeStruct((3, width, wide), BF),
            jax.ShapeDtypeStruct((heads, HD, length), BF),
            jax.ShapeDtypeStruct((heads, 1, length), F32),
            jax.ShapeDtypeStruct((4, heads, HD, rows), BF),
            jax.ShapeDtypeStruct((4, width, 2 * cols) if fused else (16, 128), BF),
            jax.ShapeDtypeStruct((width, 4 * cols) if fused else (16, 128), BF),
        ],
        in_specs=[vmem] * 9,
        out_specs=[hbm] * 4 + [vmem] + [hbm] * 3,
        scratch_shapes=[
            pltpu.VMEM((length, width), BF),
            pltpu.VMEM((width, length), BF),
            pltpu.VMEM((3, width, wide), BF),
            pltpu.VMEM((3, length, wide), BF),
            pltpu.VMEM((heads, HD, length), BF),
            pltpu.VMEM((4, heads, HD, rows), BF),
            pltpu.VMEM((HP, length), BF),
            pltpu.VMEM((length, HP), jnp.int32),
            pltpu.VMEM((3,) + small, BF),
            pltpu.VMEM(small, BF),
            pltpu.VMEM((far_n, 3) + small, BF),
            pltpu.VMEM((far_n, 3) + small, BF),
            pltpu.VMEM(small, BF),
            pltpu.VMEM((2, 2 * packed, 2 * cols) if fused else (2, 16, 128), BF),
            sem((count,)), sem((count,)), sem((count,)), sem((count,)), sem((count,)), sem((count,)),
            sem((far_n, 3)), sem((far_n, 3)), sem((far_n, 3)), sem((far_n, 3)),
            sem, sem,
            sem((2, far_n)), sem((2, far_n)), sem((2, far_n)), sem((2, far_n)),
            sem((2, far_n, 2)), sem((2, far_n, 2)),
            sem((far_n, 2)), sem((far_n, 2)), sem((far_n, 2)), sem((far_n, 2)),
            sem((4, heads)), sem((4, heads)),
            sem((12,)),
        ],
        compiler_params=pltpu.CompilerParams(
            vmem_limit_bytes=60 << 20, collective_id=1, has_side_effects=True
        ),
    )(tokens, vectors, idr, *matrices)


def mid_kernel(
    tok_ref, cot_ref, got_ref, vec_ref, wide_ref, both_ref,
    out_ref, dhid_ref, drec_out, xk_out, xg_out, pb_out, early_ref,
    w, both, att, n2, act, dpre, branch, hid, give, grec, db, drec, kept, bs,
    ss, rs, sg, rg, so,
):
    here, me = lax.axis_index("tensor"), lax.axis_index("dp")
    rows, width = tok_ref.shape
    wide = w.shape[1]
    cols = wide // 4
    pair = 2 * cols
    chunk = TILE
    half = chunk // 2
    count = rows // chunk

    def at(mask):
        return (me, here ^ mask)

    loads = [
        pltpu.make_async_copy(both_ref, both, so.at[1]),
        pltpu.make_async_copy(wide_ref, w.at[0], so.at[0]),
    ]
    for copy in loads:
        copy.start()
    greet([at(mask) for mask in PARTNERS])
    att[...] = got_ref[...].astype(F32).T.astype(BF)
    early_ref[...] = jnp.zeros_like(early_ref)
    bs[...] = jnp.zeros_like(bs)
    loads[0].wait()

    @pl.loop(0, width // chunk)
    def _(j):
        spot = pl.ds(pl.multiple_of(j * chunk, chunk), chunk)
        for i in range(4):
            w[1, spot, i * cols : (i + 1) * cols] = both[i, spot, :cols]
            w[2, spot, i * cols : (i + 1) * cols] = both[i, spot, cols:]

    loads[1].wait()

    def trade(c, mask):
        return remote(
            db.at[c, SLOT[mask]], drec.at[c, SLOT[mask]],
            ss.at[c, mask], rs.at[c, mask], at(mask),
        )

    @pl.loop(0, count)
    def _(c):
        low = pl.multiple_of(c * chunk, chunk)
        spot = pl.ds(low, chunk)
        hidden = tok_ref[spot, :].astype(F32) + mm(att[spot, :], w[0], 1, 1)
        hid[spot, :] = hidden
        cot = cot_ref[spot, :]
        d_act = mm(cot, w[2], 1, 0)
        inverse = lax.rsqrt(jnp.mean(hidden * hidden, axis=-1, keepdims=True) + EPSILON)
        hat = hidden * inverse
        normed = (hat * vec_ref[1:2, :]).astype(BF)
        n2[spot, :] = normed
        pre = mm(normed, w[1], 1, 0) + vec_ref[2:3, :]
        sig = jax.nn.sigmoid(pre)
        act[spot, :] = (pre * sig).astype(BF)
        d_pre = (d_act * sig * (1.0 + pre * (1.0 - sig))).astype(BF)
        dpre[spot, :] = d_pre
        d_n2 = mm(d_pre, w[1], 1, 1)
        scaled = d_n2 * vec_ref[1:2, :]
        cot_f32 = cot.astype(F32)
        d_hidden = cot_f32 + inverse * (
            scaled - hat * jnp.mean(scaled * hat, axis=-1, keepdims=True)
        )
        dhid_ref[spot, :] = d_hidden
        br = d_hidden.astype(BF)
        branch[spot, :] = br
        d_att = mm(br, w[0], 1, 0).astype(BF)
        for i in range(4):
            for part in range(2):
                db[c, i, :, part * cols : (part + 1) * cols] = d_att[
                    part * half : (part + 1) * half, i * cols : (i + 1) * cols
                ]
        for mask in PARTNERS:
            trade(c, mask).start()
        drec[c, 0] = db[c, 0]
        early_ref[0:1, :] += jnp.sum(d_n2 * hat, axis=0, keepdims=True)
        early_ref[1:2, :] += jnp.sum(cot_f32, axis=0, keepdims=True)
        bs[0:1, :] += jnp.sum(d_pre.astype(F32), axis=0, keepdims=True)

    pieces = ((branch, att), (n2, dpre), (cot_ref, act))

    def hand(i):
        return remote(give.at[i], grec.at[i], sg.at[i], rg.at[i], at(1))

    for i in range(3):

        @pl.loop(0, width // chunk)
        def _(j):
            spot = pl.ds(pl.multiple_of(j * chunk, chunk), chunk)
            left, right = pieces[i]
            g = mm(left[:, spot], right[...], 0, 0).astype(BF)
            give[i, spot, :] = g[:, pair:]
            if i == 0:
                kept[2, spot, :] = g[:, :pair]
            else:
                lane = (i - 1) * cols
                kept[0, spot, lane : lane + cols] = g[:, :cols]
                kept[1, spot, lane : lane + cols] = g[:, cols:pair]

        hand(i).start()

    for i in range(4):
        place = here ^ (0, 2, 1, 3)[i]
        early_ref[pl.ds(2 + place, 1), 0:cols] = bs[0:1, i * cols : (i + 1) * cols]

    @pl.loop(0, count)
    def _(c):
        spot = pl.ds(pl.multiple_of(c * chunk, chunk), chunk)
        out_ref[spot, :] = (hid[spot, :] + mm(act[spot, :], w[2], 1, 1) + vec_ref[3:4, :]).astype(BF)

    for i in range(3):
        hand(i).wait_recv()

        @pl.loop(0, width // chunk)
        def _(j):
            spot = pl.ds(pl.multiple_of(j * chunk, chunk), chunk)
            came = grec[i, spot, :]
            if i == 0:
                kept[2, spot, :] += came
            else:
                lane = (i - 1) * cols
                kept[0, spot, lane : lane + cols] += came[:, :cols]
                kept[1, spot, lane : lane + cols] += came[:, cols:]

        if i == 0:
            keep = [pltpu.make_async_copy(kept.at[2], pb_out, so.at[3])]
            keep[0].start()
    keep.append(pltpu.make_async_copy(kept.at[0], xk_out, so.at[4]))
    keep.append(pltpu.make_async_copy(kept.at[1], xg_out, so.at[5]))
    for copy in keep[1:]:
        copy.start()
    for c in range(count):
        for mask in PARTNERS:
            trade(c, mask).wait_recv()
    keep.append(pltpu.make_async_copy(drec, drec_out, so.at[6]))
    keep[-1].start()
    for c in range(count):
        for mask in PARTNERS:
            trade(c, mask).wait_send()
    for i in range(3):
        hand(i).wait_send()
    for copy in keep:
        copy.wait()


def middle(tokens, cotangent, got, vectors, wide, both):
    rows, width = tokens.shape
    all_cols = wide.shape[1]
    cols = all_cols // 4
    count = rows // TILE
    vmem = pl.BlockSpec(memory_space=pltpu.VMEM)
    hbm = pl.BlockSpec(memory_space=pl.ANY)
    sem = pltpu.SemaphoreType.DMA
    blocks = (count, 4, TILE // 2, 2 * cols)
    halves = jax.ShapeDtypeStruct((width, 2 * cols), BF)
    return pl.pallas_call(
        mid_kernel,
        out_shape=[
            jax.ShapeDtypeStruct((rows, width), BF),
            jax.ShapeDtypeStruct((rows, width), F32),
            jax.ShapeDtypeStruct(blocks, BF),
            halves,
            halves,
            halves,
            jax.ShapeDtypeStruct((16, width), F32),
        ],
        in_specs=[vmem] * 4 + [hbm] * 2,
        out_specs=[vmem, vmem, hbm, hbm, hbm, hbm, vmem],
        scratch_shapes=[
            pltpu.VMEM((3, width, all_cols), BF),
            pltpu.VMEM((4, width, 2 * cols), BF),
            pltpu.VMEM((rows, all_cols), BF),
            pltpu.VMEM((rows, width), BF),
            pltpu.VMEM((rows, all_cols), BF),
            pltpu.VMEM((rows, all_cols), BF),
            pltpu.VMEM((rows, width), BF),
            pltpu.VMEM((rows, width), F32),
            pltpu.VMEM((3, width, 2 * cols), BF),
            pltpu.VMEM((3, width, 2 * cols), BF),
            pltpu.VMEM(blocks, BF),
            pltpu.VMEM(blocks, BF),
            pltpu.VMEM((3, width, 2 * cols), BF),
            pltpu.VMEM((8, all_cols), F32),
            sem((count, 4)), sem((count, 4)), sem((3,)), sem((3,)), sem((8,)),
        ],
        compiler_params=pltpu.CompilerParams(
            vmem_limit_bytes=60 << 20, collective_id=2, has_side_effects=True
        ),
    )(tokens, cotangent, got, vectors, wide, both)


def back_kernel(
    dp, far, o_ref, lse_ref, drec_ref, vec_ref, idr_ref, xk_ref, early_ref,
    qkv_hbm, xg_ref, pb_ref, tok_hbm, dhid_hbm, normt_hbm, wpad_hbm,
    dtok_ref, dq_out, dk_out, dv_out, dout_ref, dup_ref, ddown_ref, sums_ref,
    do, dka, dva, kt_ref, idc_ref, dqkv, tok, dhid, normt, wpad,
    xrec, pbown, yrec, zrec, last, lastsend, lastrec,
    gpay, gyrec, gzrec, ownsum, fo, crec, fs, frec, nrec, qsum, lvec, ar, arec, aorder,
    so, sxa, rxa, sy, ry, sz, rz, sl, rl, sgy, rgy, sgz, rgz, sfo, rfo, sfs, rfs, sno, rno, sar, rar,
):
    here, me = lax.axis_index("tensor"), lax.axis_index("dp")
    heads, _, length = o_ref.shape
    rows, width = tok.shape
    cols = heads * HD
    tiles = length // TILE
    depth = width // dp
    packed = depth // 2
    fused = far > 0
    major, minor = me // 2, me % 2
    chunk = TILE
    count = rows // chunk

    def at(mask):
        return (me, here ^ mask)

    across = (me ^ 1, here)

    def along(step):
        return (lax.rem(major + step, far) * 2 + minor, here)

    def target(step):
        return lax.rem(major + step, far)

    loads = [
        pltpu.make_async_copy(src, dst, so.at[i])
        for i, (src, dst) in enumerate(
            ((wpad_hbm, wpad), (normt_hbm, normt), (tok_hbm, tok), (dhid_hbm, dhid))
        )
    ]
    load_qkv = pltpu.make_async_copy(qkv_hbm, dqkv, so.at[4])
    load_qkv.start()
    if fused:
        load_pb = pltpu.make_async_copy(pb_ref.at[:, minor], pbown, so.at[5])
        load_pb.start()
    for copy in loads:
        copy.start()
    peers = [at(2), at(1)]
    if fused:
        peers += [across] + [along(step) for step in range(1, far)]
    greet(peers)

    turn = list(range(1, far)) + [0]

    def x_send(step):
        spot = target(step)
        return remote(xg_ref.at[spot], xrec.at[spot], sxa.at[step], rxa.at[step], at(2))

    def y_send(p, step):
        spot = target(step)
        src = xrec.at[spot, 1 - minor] if p == 0 else pb_ref.at[spot, 1 - minor]
        return remote(src, yrec.at[p, spot], sy.at[p, step], ry.at[p, step], across)

    def z_send(p, step):
        return remote(
            yrec.at[p, target(step)], zrec.at[p, step - 1],
            sz.at[p, step], rz.at[p, step], along(step),
        )

    def after_x(step):
        x_send(step).wait_recv()
        spot = target(step)
        xrec[spot] = xk_ref[spot] + xrec[spot]
        y_send(0, step).start()

    def after_y(p, step):
        y_send(p, step).wait_recv()
        spot = target(step)
        mine = xrec[spot, minor] if p == 0 else pbown[spot]
        if step:
            yrec[p, spot] = mine + yrec[p, spot]
            z_send(p, step).start()
        else:
            last[p] = mine.astype(F32) + yrec[p, spot].astype(F32)

    def after_z(p):
        for step in range(1, far):
            z_send(p, step).wait_recv()
            last[p] += zrec[p, step - 1].astype(F32)

    if fused:
        for step in turn:
            x_send(step).start()
            y_send(1, step).start()

    do[...] = jnp.zeros_like(do)
    half = chunk // 2
    for c in range(count):
        for i, mask in enumerate((0, 2, 1, 3)):
            block = drec_ref[c, i]
            for part in range(2):
                low = pl.multiple_of((here ^ mask) * rows + c * chunk + part * half, half)
                for h in range(heads):
                    lane = part * cols + h * HD
                    do[h, pl.ds(low, half), 0:HD] = block[:, lane : lane + HD]
    qsum[...] = jnp.zeros_like(qsum)
    if fused:
        gpay[...] = jnp.zeros_like(gpay)
    idc_ref[...] = jnp.broadcast_to(idr_ref[...].astype(F32), (HP, length)).T.astype(jnp.int32)

    load_qkv.wait()
    if fused:
        load_pb.wait()

    def one_head(h):
        lanes = pl.ds(pl.multiple_of(h * HP, HP), HP)
        kt_ref[...] = dqkv[1, :, lanes].astype(F32).T.astype(BF)
        dka[...] = jnp.zeros_like(dka)
        dva[...] = jnp.zeros_like(dva)
        scale_sum = jnp.zeros((1, HP), F32)
        for t in range(tiles):
            seen, low = reach(t, length), t * TILE
            spot = slice(low, low + TILE)
            qt = dqkv[0, spot, lanes]
            dot_ = do[h, spot, :]
            delta = jnp.sum(
                dot_.astype(F32).T[:HD] * o_ref[h, :, spot].astype(F32), axis=0, keepdims=True
            )
            st = mm(dqkv[1, :seen, lanes], qt, 1, 1)
            p = jnp.exp(st - lse_ref[h, :, spot])
            visible = idc_ref[low:seen, 0:1] <= idr_ref[:, spot]
            pm = jnp.where(visible, p[low:], 0.0)
            p = jnp.concatenate([p[:low], pm], 0) if low else pm
            d_p = mm(dqkv[2, :seen, lanes], dot_, 1, 1)
            ds = (p * (d_p - delta)).astype(BF)
            dva[:seen, :] += mm(p.astype(BF), dot_, 1, 0)
            dka[:seen, :] += mm(ds, qt, 1, 0)
            dq = mm(kt_ref[:, :seen], ds, 1, 0).T
            scale_sum = scale_sum + jnp.sum(dq * qt.astype(F32), axis=0, keepdims=True)
            dqkv[0, spot, lanes] = (dq * vec_ref[4:5, :HP]).astype(BF)
        dqkv[1, :, lanes] = dka[...].astype(BF)
        dqkv[2, :, lanes] = dva[...].astype(BF)
        qsum[0:1, :] += scale_sum

    group = 2 * HD

    def weight_blocks(n, step):
        spot = target(step)
        low = pl.multiple_of(spot * 2 * depth, 16)
        lanes = slice(n * 2 * HP, (n + 1) * 2 * HP)
        dots = jnp.zeros((2 * depth, 1), F32)
        for i in range(3):
            g = mm(normt[pl.ds(low, 2 * depth), :], dqkv[i, :, lanes], 1, 0)
            dots = dots + jnp.sum(
                g * wpad[i, pl.ds(low, 2 * depth), lanes].astype(F32), axis=1, keepdims=True
            )
            g = g.astype(BF)
            for side in range(2):
                for h in range(2):
                    lane = i * group + h * HD
                    gpay[n, spot, side, :, lane : lane + HD] = g[
                        side * depth : (side + 1) * depth, h * HP : h * HP + HD
                    ]
        flat = jnp.broadcast_to(dots, (2 * depth, HP)).T[0:1, :]
        lvec[n, pl.ds(spot * 2, 1), :] = flat[:, :depth]
        lvec[n, pl.ds(spot * 2 + 1, 1), :] = flat[:, depth:]

    def gy_send(n, step):
        spot = target(step)
        return remote(
            gpay.at[n, spot, 1 - minor], gyrec.at[n, spot], sgy.at[n, step], rgy.at[n, step], across
        )

    def gz_send(n, step):
        return remote(
            gyrec.at[n, target(step)], gzrec.at[n, step - 1],
            sgz.at[n, step], rgz.at[n, step], along(step),
        )

    def weight_pair(n):
        @pl.loop(0, far)
        def _(j):
            step = lax.rem(j + 1, far)
            weight_blocks(n, step)
            gy_send(n, step).start()

    def gz_start(n, step):
        gy_send(n, step).wait_recv()
        spot = target(step)
        mine = gpay[n, spot, minor]
        if step:
            gyrec[n, spot] = mine + gyrec[n, spot]
            gz_send(n, step).start()
        else:
            ownsum[n] = mine.astype(F32) + gyrec[n, spot].astype(F32)

    @pl.loop(0, heads)
    def _(h):
        one_head(h)
        if fused:
            for n in range(far):

                @pl.when(h == n)
                def _(n=n):
                    after_x(turn[n])
                    after_y(1, turn[n])
                    if n:
                        after_y(0, turn[n - 1])
                    if n == 1:
                        for copy in loads[:2]:
                            copy.wait()
                        weight_pair(0)
                    if n == 2:
                        for step in turn:
                            gz_start(0, step)

    if not fused:
        for copy in loads[:2]:
            copy.wait()

    def part(mask, c):
        spot = pl.ds(pl.multiple_of((here ^ mask) * rows + c * chunk, chunk), chunk)
        total = mm(dqkv[0, spot, :], wpad[0], 1, 1)
        total = total + mm(dqkv[1, spot, :], wpad[1], 1, 1)
        return total + mm(dqkv[2, spot, :], wpad[2], 1, 1)

    def c_far(c):
        return remote(fo.at[c], crec.at[c], sfo.at[c], rfo.at[c], at(1))

    def x_far(c):
        return remote(fs.at[c], frec.at[c], sfs.at[c], rfs.at[c], at(2))

    def c_near(c):
        return remote(fo.at[c], nrec.at[c], sno.at[c], rno.at[c], at(1))

    def far_chunk(c):
        fo[c] = part(3, c).astype(BF)
        c_far(c).start()

    def far_sum(c):
        own = part(2, c)
        c_far(c).wait_recv()
        fs[c] = (own + crec[c].astype(F32)).astype(BF)

    def hop(n, where):
        return remote(ar.at[n], arec.at[n], sar.at[n], rar.at[n], where)

    def z_hop(step):
        return remote(ar.at[3], arec.at[3 + step], sar.at[3 + step], rar.at[3 + step], along(step))

    if fused:
        far_chunk(0)
        far_sum(0)
        x_far(0).start()
        after_y(0, turn[far - 1])
        weight_pair(1)
        ar[0] = jnp.zeros_like(ar[0])
        ar[0, 0:6, :] = early_ref[0:6, :]
        ar[0, 6:7, 0:HP] = qsum[0:1, :]
        ar[0, 8:16, 0:depth] = lvec[0] + lvec[1]
        hop(0, at(1)).start()
        for c in range(1, count):
            far_chunk(c)
        gz_start(1, turn[0])
        gz_start(1, turn[1])
        hop(0, at(1)).wait_recv()
        ar[1] = ar[0] + arec[0]
        hop(1, at(2)).start()
        for c in range(1, count):
            far_sum(c)
            x_far(c).start()
        after_z(1)
        for piece in range(2):
            last_half = last[1, piece * packed : (piece + 1) * packed, cols:]
            lastsend[:, piece * cols : (piece + 1) * cols] = last_half.astype(BF)
        cross = remote(lastsend, lastrec, sl, rl, at(2))
        cross.start()
    else:
        for c in range(count):
            far_chunk(c)
            far_sum(c)
            x_far(c).start()

        @pl.loop(0, 3)
        def _(i):
            for j in range(width // chunk):
                dq_out[i, j * chunk : (j + 1) * chunk, :] = mm(
                    normt[j * chunk : (j + 1) * chunk, :], dqkv[i], 1, 0
                )

    if not fused:
        sums_ref[...] = jnp.zeros_like(sums_ref)
        sums_ref[0:6, :] = early_ref[0:6, :]
        sums_ref[6:7, 0:HP] = qsum[0:1, :]

    for c in range(count):
        c_far(c).wait_send()
        fo[c] = part(1, c).astype(BF)
        c_near(c).start()
    if fused:
        gz_start(1, turn[2])
        gz_start(1, turn[3])
        hop(1, at(2)).wait_recv()
        ar[2] = ar[1] + arec[1]
        hop(2, across).start()
        after_z(0)
        dup_ref[...] = last[0, :, :cols]
        ddown_ref[...] = last[0, :, cols:]
    for copy in loads[2:]:
        copy.wait()
    near = [part(0, c) for c in range(1)]
    if fused:
        hop(2, across).wait_recv()
        ar[3] = ar[2] + arec[2]
        for step in range(1, far):
            z_hop(step).start()
        cross.wait_recv()
        arrived = jnp.concatenate([lastrec[:, :cols], lastrec[:, cols:]], axis=0)
        dout_ref[...] = last[1, :, :cols] + arrived.astype(F32)

    for c in range(count):
        d_normed = near[c] if c < len(near) else part(0, c)
        c_near(c).wait_recv()
        x_far(c).wait_recv()
        d_normed = d_normed + nrec[c].astype(F32) + frec[c].astype(F32)
        spot = slice(c * chunk, (c + 1) * chunk)
        v = tok[spot, :].astype(F32)
        inverse = lax.rsqrt(jnp.mean(v * v, axis=-1, keepdims=True) + EPSILON)
        hat = v * inverse
        scaled = d_normed * vec_ref[0:1, :]
        dtok_ref[spot, :] = (
            dhid[spot, :]
            + inverse * (scaled - hat * jnp.mean(scaled * hat, axis=-1, keepdims=True))
        ).astype(BF)
    if fused:
        for n in range(2):
            for step in range(1, far):
                gz_send(n, step).wait_recv()
                ownsum[n] += gzrec[n, step - 1].astype(F32)
            for i, ref in enumerate((dq_out, dk_out, dv_out)):
                ref[:, n * group : (n + 1) * group] = ownsum[n, :, i * group : (i + 1) * group]
        aorder[major] = ar[3]
        for step in range(1, far):
            z_hop(step).wait_recv()
            aorder[lax.rem(major + far - step, far)] = arec[3 + step]
        sums_ref[...] = (aorder[0] + aorder[1]) + (aorder[2] + aorder[3])
    else:
        dk_out[...] = jnp.zeros_like(dk_out)
        dv_out[...] = jnp.zeros_like(dv_out)
        dout_ref[...] = jnp.zeros_like(dout_ref)
        dup_ref[...] = jnp.zeros_like(dup_ref)
        ddown_ref[...] = jnp.zeros_like(ddown_ref)

    for c in range(count):
        x_far(c).wait_send()
        c_near(c).wait_send()
    if fused:
        for step in range(far):
            x_send(step).wait_send()
            for p in range(2):
                gy_send(p, step).wait_send()
                y_send(p, step).wait_send()
            if step:
                gz_send(0, step).wait_send()
                gz_send(1, step).wait_send()
                z_hop(step).wait_send()
                for p in range(2):
                    z_send(p, step).wait_send()
        cross.wait_send()
        hop(0, at(1)).wait_send()
        hop(1, at(2)).wait_send()
        hop(2, across).wait_send()


def backward(dp, far, o, lse, drec, vectors, idr, xk, early, qkv, xg, pb,
             tokens, d_hidden, normt, wpad):
    heads, _, length = o.shape
    rows, width = tokens.shape
    cols, wide = heads * HD, heads * HP
    depth = width // dp
    packed = depth // 2
    count = rows // TILE
    fused = far > 0
    far_n = max(far, 1)
    vmem = pl.BlockSpec(memory_space=pltpu.VMEM)
    hbm = pl.BlockSpec(memory_space=pl.ANY)
    sem = pltpu.SemaphoreType.DMA
    tiny = jax.ShapeDtypeStruct((8, 128), F32)
    shard = jax.ShapeDtypeStruct((depth, cols), F32) if fused else tiny
    whole = shard if fused else jax.ShapeDtypeStruct((3, width, wide), F32)

    def buf(*shape, dtype=BF, only=True):
        return pltpu.VMEM(shape if fused or not only else (8, 128), dtype)

    pair = 2 * cols
    return pl.pallas_call(
        lambda *refs: back_kernel(dp, far, *refs),
        out_shape=[jax.ShapeDtypeStruct((rows, width), BF), whole, shard, shard, shard, shard,
                   shard, jax.ShapeDtypeStruct((16, width), F32)],
        in_specs=[vmem] * 7 + [hbm] * 7,
        out_specs=[vmem] * 8,
        scratch_shapes=[
            buf(heads, length, HP, only=False),
            buf(length, HP, dtype=F32, only=False),
            buf(length, HP, dtype=F32, only=False),
            buf(HP, length, only=False),
            buf(length, HP, dtype=jnp.int32, only=False),
            buf(3, length, wide, only=False),
            buf(rows, width, only=False),
            buf(rows, width, dtype=F32, only=False),
            buf(width, length, only=False),
            buf(3, width, wide, only=False),
            buf(far_n, 2, depth, pair),
            buf(far_n, depth, pair),
            buf(2, far_n, depth, pair),
            buf(2, far_n - 1, depth, pair),
            buf(2, depth, pair, dtype=F32),
            buf(packed, pair),
            buf(packed, pair),
            buf(2, far_n, 2, depth, 4 * HP),
            buf(2, far_n, depth, 4 * HP),
            buf(2, far_n - 1, depth, 4 * HP),
            buf(2, depth, 4 * HP, dtype=F32),
            buf(count, TILE, width, only=False),
            buf(count, TILE, width, only=False),
            buf(count, TILE, width, only=False),
            buf(count, TILE, width, only=False),
            buf(count, TILE, width, only=False),
            buf(8, HP, dtype=F32, only=False),
            buf(2, dp, depth, dtype=F32),
            buf(4, 16, width, dtype=F32),
            buf(3 + far_n, 16, width, dtype=F32),
            buf(far_n, 16, width, dtype=F32),
            sem((6,)),
            sem((far_n,)), sem((far_n,)),
            sem((2, far_n)), sem((2, far_n)), sem((2, far_n)), sem((2, far_n)),
            sem, sem,
            sem((2, far_n)), sem((2, far_n)), sem((2, far_n)), sem((2, far_n)),
            sem((count,)), sem((count,)), sem((count,)), sem((count,)), sem((count,)), sem((count,)),
            sem((3 + far_n,)), sem((3 + far_n,)),
        ],
        compiler_params=pltpu.CompilerParams(
            vmem_limit_bytes=62 << 20, collective_id=3, has_side_effects=True
        ),
    )(o, lse, drec, vectors, idr, xk, early, qkv, xg, pb,
      tokens, d_hidden, normt, wpad)


def finish_kernel(dp, cols, scale_ref, sums_ref, vec_ref, *refs):
    moves, outs, held = refs[:8], refs[8:21], refs[21:29]
    row, sem = refs[29:]
    width = vec_ref.shape[1]
    depth = width // dp
    places = (0, 1, 3, 4, 5, 7, 9, 11)
    enter = [pltpu.make_async_copy(moves[i], held[i], sem.at[i]) for i in range(8)]
    leave = [pltpu.make_async_copy(held[i], outs[places[i]], sem.at[8 + i]) for i in range(8)]
    for copy in enter:
        copy.start()
    outs[6][...] = sums_ref[6, 0:HP] * scale_ref[0, :]
    outs[8][...] = sums_ref[0, :]
    outs[12][...] = sums_ref[1, :]
    row[...] = jnp.zeros_like(row)
    for i in range(width // cols):
        row[0:1, i * cols : (i + 1) * cols] = sums_ref[2 + i : 3 + i, :cols]
    for i in range(dp):
        spot = slice(i * depth, (i + 1) * depth)
        row[1:2, spot] = sums_ref[8 + i : 9 + i, :depth] / vec_ref[0:1, spot]
    outs[10][...] = row[0, :]
    outs[2][...] = row[1, :]
    for come, go in zip(enter, leave):
        come.wait()
        go.start()
    for copy in leave:
        copy.wait()


def finish(dp, cols, scale, sums, vectors, moves):
    width = vectors.shape[1]
    vmem = pl.BlockSpec(memory_space=pltpu.VMEM)
    hbm = pl.BlockSpec(memory_space=pl.ANY)
    row = jax.ShapeDtypeStruct((width,), F32)
    like = [jax.ShapeDtypeStruct(v.shape, v.dtype) for v in moves]
    shapes = like[:2] + [row] + like[2:5] + [jax.ShapeDtypeStruct((HP,), F32)]
    shapes += [like[5], row, like[6], row, like[7], row]
    small = (2, 6, 8, 10, 12)
    return pl.pallas_call(
        lambda *refs: finish_kernel(dp, cols, *refs),
        out_shape=shapes,
        in_specs=[vmem] * 3 + [hbm] * 8,
        out_specs=[vmem if i in small else hbm for i in range(13)],
        scratch_shapes=[pltpu.VMEM(v.shape, v.dtype) for v in moves]
        + [pltpu.VMEM((8, width), F32), pltpu.SemaphoreType.DMA((16,))],
        compiler_params=pltpu.CompilerParams(vmem_limit_bytes=60 << 20),
    )(scale, sums, vectors, *moves)


def swap(v, axis, size, mask):
    return lax.ppermute(v, axis, [(i, i ^ mask) for i in range(size)])


def gather_dp(shard):
    return lax.all_gather(shard, "dp", axis=0, tiled=True)


def scatter_dp(grad, size):
    return lax.psum_scatter(grad, "dp", scatter_dimension=0, tiled=True)


def pad_heads(w):
    rows, cols = w.shape
    w = w.reshape(rows, cols // HD, HD)
    return jnp.pad(w, ((0, 0), (0, 0), (0, HP - HD))).reshape(rows, cols // HD * HP)


def trim_heads(w):
    rows, cols = w.shape
    return w.reshape(rows, cols // HP, HP)[:, :, :HD].reshape(rows, cols // HP * HD)


def body(dp, tensor, tokens, cotangent, block_ids, attn_gain, w_query, w_key, w_value,
         query_scale, w_out, mlp_gain, w_up, b_up, w_down, b_down):
    assert tensor == 4
    here = lax.axis_index("tensor")
    rows, width = tokens.shape
    length = rows * tensor
    cols = w_query.shape[1]
    heads = cols // HD
    order = [here, here ^ 2, here ^ 1, here ^ 3]

    softplus = jnp.log1p(jnp.exp(query_scale))
    factor = jnp.pad(SCORE_BASE / math.sqrt(HD) * softplus, (0, HP - HD))
    b_rel = jnp.concatenate([lax.dynamic_slice(b_up, (at * cols,), (cols,)) for at in order])
    repeat = jnp.pad(jnp.tile(factor, heads), (0, width - heads * HP))
    vectors = jnp.concatenate([attn_gain, mlp_gain, b_rel, b_down, repeat]).reshape(5, width)

    far = dp // 2 if dp == 8 else 0
    matrices = (w_query, w_key, w_value, w_out.T, w_up, w_down.T)
    if not far:
        pair = [jnp.concatenate([w, swap(w, "tensor", tensor, 2)], axis=1) for w in matrices[3:]]
        half = gather_dp(jnp.concatenate(pair, axis=1)).reshape(width, 3, 2 * cols)
        both = jnp.concatenate([half, swap(half, "tensor", tensor, 1)], axis=2)
        full = gather_dp(jnp.concatenate(matrices[:3], axis=1))
        first = jnp.stack([pad_heads(full[:, i * cols : (i + 1) * cols]) for i in range(3)])
        matrices = (first,) + matrices[1:]
    qkv, normed_t, padded, attended, lse, got, pairs, wide = front(
        dp, far, tokens, vectors, block_ids, cols, matrices
    )
    if not far:
        wide = both[:, 0]
        pairs = both[:, 1:].reshape(width, 2, 4, cols).transpose(2, 0, 1, 3)
        pairs = pairs.reshape(4, width, 2 * cols)

    output, d_hidden, received, xk, xg, pb, early = middle(
        tokens, cotangent, got.reshape(4 * cols, rows), vectors, wide, pairs
    )
    depth = width // dp
    if far:
        xk, xg, pb = (v.reshape(far, 2, depth, 2 * cols) for v in (xk, xg, pb))
    d_tokens, s_q, s_k, s_v, s_out, s_up, s_down, sums = backward(
        dp, far, attended, lse, received, vectors, block_ids, xk, early,
        qkv, xg, pb, tokens, d_hidden, normed_t, padded,
    )
    slope = jax.nn.sigmoid(query_scale) / softplus
    if far:
        scale = jnp.pad(slope, (0, HP - HD))[None, :]
        final = list(
            finish(
                dp, cols, scale, sums, vectors,
                (output, d_tokens, s_q, s_k, s_v, s_out, s_up, s_down),
            )
        )
        final[6] = final[6][:HD]
        final[7], final[11] = final[7].T, final[11].T
        return tuple(final)
    else:
        dots = lax.psum(jnp.sum(s_q * padded.astype(F32), axis=(0, 2)), ("dp", "tensor"))
        sums = lax.psum(sums, ("dp", "tensor"))
        s_qkv = scatter_dp(jnp.concatenate([trim_heads(g) for g in s_q], axis=1), dp)
        s_q, s_k, s_v = (s_qkv[:, i * cols : (i + 1) * cols] for i in range(3))
        both = xk.astype(F32) + swap(xg, "tensor", tensor, 2).astype(F32)
        both = scatter_dp(both, dp)
        s_up, s_down = both[:, :cols], both[:, cols:].T
        both = scatter_dp(pb.astype(F32), dp)
        s_out = (both[:, :cols] + swap(both[:, cols:], "tensor", tensor, 2)).T
    d_scale = sums[6, :HD] * slope
    return (
        output,
        d_tokens,
        dots / attn_gain,
        s_q,
        s_k,
        s_v,
        d_scale,
        s_out,
        sums[0],
        s_up,
        sums[2:6, :cols].reshape(4 * cols),
        s_down,
        sums[1],
    )


def solution(mesh):
    weight, turned, whole = P("dp", "tensor"), P("tensor", "dp"), P()
    positions = P(("dp", "tensor"), None)
    return jax.shard_map(
        lambda *args: body(mesh.shape["dp"], mesh.shape["tensor"], *args),
        mesh=mesh,
        in_specs=(positions, positions, P("dp", None), whole, weight, weight, weight, whole,
                  turned, whole, weight, whole, turned, whole),
        out_specs=(positions, positions, whole, weight, weight, weight, whole, turned, whole,
                   weight, whole, turned, whole),
        check_vma=False,
    )
```

```python
import math

import jax
import jax.numpy as jnp
from jax import lax
from jax.experimental import pallas as pl
from jax.experimental.pallas import tpu as pltpu
from jax.sharding import PartitionSpec as P

HD = 80
HP = 128
TILE = 256
BLOCK_MOST = 256
EPSILON = 1e-06
SCORE_BASE = 1.442695041
MASKED = -1e30
BF = jnp.bfloat16
F32 = jnp.float32


def mm(a, b, ca, cb):
    return lax.dot_general(a, b, (((ca,), (cb,)), ((), ())), preferred_element_type=F32)


def reach(tile, length):
    return min((tile + 1) * TILE + BLOCK_MOST, length)


MESH = pl.DeviceIdType.MESH
PARTNERS = (2, 1, 3)
SLOT = {0: 0, 2: 1, 1: 2, 3: 3}


def remote(src, dst, send, recv, where):
    return pltpu.make_async_remote_copy(
        src_ref=src, dst_ref=dst, send_sem=send, recv_sem=recv, device_id=where, device_id_type=MESH
    )


def greet(peers):
    barrier = pltpu.get_barrier_semaphore()
    for where in peers:
        pl.semaphore_signal(barrier, inc=1, device_id=where, device_id_type=MESH)
    pl.semaphore_wait(barrier, len(peers))


def front_kernel(
    dp, far, tok_ref, vec_ref, idr_ref, wq_ref, wk_ref, wv_ref, wo_ref, wu_ref, wd_ref,
    qkv_out, normt_out, wpad_out, att_out, lse_ref, got_out, both_out, wide_out,
    norm, normt, wpad, qkv, att, got, vt_ref, idc_ref, fac, w1_ref, w2_ref, z1, y1, x2, pair,
    sx, rx, sc, rc, sf, rf, sz1, rz1, sy1, ry1, sx2, rx2, sz2, rz2, sy2, ry2, sc2, rc2,
    sx3, rx3, sc3, rc3, st_, rt_, so,
):
    here, me = lax.axis_index("tensor"), lax.axis_index("dp")
    rows, width = tok_ref.shape
    length = norm.shape[0]
    tiles = length // TILE
    heads = qkv.shape[2] // HP
    cols = heads * HD
    depth = width // dp
    packed = depth // 2
    fused = far > 0
    major, minor = me // 2, me % 2

    def at(mask):
        return (me, here ^ mask)

    def xor(mask):
        return here ^ mask

    across = (me ^ 1, here)

    def along(step):
        return (lax.rem(major + step, far) * 2 + minor, here)

    def source(step):
        return lax.rem(major + far - step, far)

    peers = [at(mask) for mask in PARTNERS]
    if fused:
        peers += [across] + [along(step) for step in range(1, far)]
    greet(peers)

    def z_first(w, step):
        return remote(
            w1_ref.at[w], z1.at[step, w], sz1.at[step, w], rz1.at[step, w], along(step)
        )

    def y_first(w, step):
        src = w1_ref.at[w] if isinstance(step, int) and step == 0 else z1.at[step, w]
        return remote(src, y1.at[step, w], sy1.at[step, w], ry1.at[step, w], across)

    swap_two = remote(w2_ref, x2, sx2, rx2, at(2)) if fused else None
    if fused:
        for w, ref in enumerate((wq_ref, wk_ref, wv_ref)):
            w1_ref[w, :, :cols] = ref[:packed, :]
            w1_ref[w, :, cols:] = ref[packed:, :]
            for step in range(1, far):
                z_first(w, step).start()
            y_first(w, 0).start()
        pair[0, :, :cols] = wu_ref[...]
        pair[0, :, cols:] = wd_ref[...]
        pair[1, :, :cols] = wo_ref[...]
        w2_ref[:, :cols] = wo_ref[:packed, :]
        w2_ref[:, cols:] = wo_ref[packed:, :]
        swap_two.start()

    chunk = TILE
    count = rows // chunk

    @pl.loop(0, count)
    def _(c):
        low = pl.multiple_of(c * chunk, chunk)
        v = tok_ref[pl.ds(low, chunk), :].astype(F32)
        hat = v * lax.rsqrt(jnp.mean(v * v, axis=-1, keepdims=True) + EPSILON)
        norm[pl.ds(pl.multiple_of(here * rows + low, chunk), chunk), :] = (
            hat * vec_ref[0:1, :]
        ).astype(BF)

    def rows_of(mask, c):
        return norm.at[pl.ds(pl.multiple_of((here ^ mask) * rows + c * chunk, chunk), chunk), :]

    def send_x(c):
        return remote(rows_of(0, c), rows_of(0, c), sx.at[c], rx.at[c], at(2))

    def send_c(c):
        return remote(rows_of(0, c), rows_of(0, c), sc.at[c], rc.at[c], at(1))

    def forward(c):
        return remote(rows_of(2, c), rows_of(2, c), sf.at[c], rf.at[c], at(1))

    for c in range(count):
        send_x(c).start()
        send_c(c).start()
    idc_ref[...] = jnp.broadcast_to(idr_ref[...].astype(F32), (HP, length)).T.astype(jnp.int32)
    fac[...] = jnp.ones_like(fac)
    fac[0:1, :] = vec_ref[4:5, : heads * HP]

    def project(w, mask, c):
        low = pl.multiple_of(xor(mask) * rows + c * chunk, chunk)
        x = norm[pl.ds(low, chunk), :]
        y = mm(x, wpad[w], 1, 0)
        qkv[w, pl.ds(low, chunk), :] = (y * fac[pl.ds(w, 1), :]).astype(BF)

        @pl.when(w == 2)
        def _():
            normt[:, pl.ds(low, chunk)] = x.astype(F32).T.astype(BF)

    def rows_two(index):
        return pl.ds(pl.multiple_of(index * depth, 16), depth)

    def index_of(step, side):
        return source(step) * 2 + (minor if side == 0 else 1 - minor)

    def block_two(p, index):
        if p == 0:
            return both_out.at[0, rows_two(index), :]
        return wide_out.at[rows_two(index), pl.ds(0, 2 * cols)]

    def held_two(p, step, side):
        return pair.at[p] if step == 0 and side == 0 else block_two(p, index_of(step, side))

    def z_second(p, step):
        return remote(
            pair.at[p], block_two(p, me), sz2.at[p, step], rz2.at[p, step], along(step)
        )

    def y_second(p, step):
        return remote(
            held_two(p, step, 0), block_two(p, index_of(step, 0)),
            sy2.at[p, step], ry2.at[p, step], across,
        )

    def c_second(p, step, side):
        index = index_of(step, side)
        if p == 0:
            dst = both_out.at[2, rows_two(index), :]
        else:
            dst = wide_out.at[rows_two(index), pl.ds(2 * cols, 2 * cols)]
        return remote(
            held_two(p, step, side), dst, sc2.at[p, step, side], rc2.at[p, step, side], at(1)
        )

    def x_second(step, side):
        return remote(
            held_two(0, step, side), both_out.at[1, rows_two(index_of(step, side)), :],
            sx3.at[step, side], rx3.at[step, side], at(2),
        )

    def c_third(step, side):
        spot = rows_two(index_of(step, side))
        return remote(
            both_out.at[1, spot, :], both_out.at[3, spot, :],
            sc3.at[step, side], rc3.at[step, side], at(1),
        )

    def own_two(p):
        return pltpu.make_async_copy(pair.at[p], block_two(p, me), so.at[8 + p])

    def start_second(p):
        for step in range(1, far):
            z_second(p, step).start()
        y_second(p, 0).start()
        own_two(p).start()

    def spread(p, step, side):
        c_second(p, step, side).start()
        if p == 0:
            x_second(step, side).start()

    def after_z(p):
        for step in range(1, far):
            z_second(p, step).wait_recv()
            y_second(p, step).start()
            spread(p, step, 0)

    def after_y(p, step):
        y_second(p, step).wait_recv()
        spread(p, step, 1)

    if fused:
        start_second(0)
        spread(0, 0, 0)
        swap_two.wait_recv()
        for part in range(2):
            pair[1, part * packed : (part + 1) * packed, cols:] = x2[
                :, part * cols : (part + 1) * cols
            ]
        start_second(1)
        spread(1, 0, 0)

    if not fused:
        wpad[...] = wq_ref[...]
        for c in range(count):
            send_c(c).wait_recv()

        @pl.loop(0, 3)
        def _(w):
            @pl.loop(0, 2 * count)
            def _(j):
                project(w, j // count, lax.rem(j, count))

    else:
        wpad[...] = jnp.zeros_like(wpad)

        def unpack(w, block, device):
            for part in range(2):
                low = pl.multiple_of(device * depth + part * packed, 16)
                for h in range(heads):
                    lane = part * cols + h * HD
                    wpad[w, pl.ds(low, packed), h * HP : h * HP + HD] = block[:, lane : lane + HD]

        @pl.loop(0, 3)
        def _(w):
            unpack(w, w1_ref[w], me)

            @pl.loop(1, far)
            def _(step):
                z_first(w, step).wait_recv()
                y_first(w, step).start()
                unpack(w, z1[step, w], source(step) * 2 + minor)

            @pl.loop(0, far)
            def _(step):
                y_first(w, step).wait_recv()
                unpack(w, y1[step, w], source(step) * 2 + 1 - minor)

            @pl.when(w == 0)
            def _():
                for c in range(count):
                    send_c(c).wait_recv()

            @pl.loop(0, 2 * count)
            def _(j):
                project(w, j // count, lax.rem(j, count))

            @pl.when(w == 1)
            def _():
                after_y(0, 0)

        after_z(0)

    @pl.loop(0, count)
    def _(c):
        send_x(c).wait_recv()
        forward(c).start()

        @pl.loop(0, 3)
        def _(w):
            project(w, 2, c)

    @pl.loop(0, count)
    def _(c):
        forward(c).wait_recv()

        @pl.loop(0, 3)
        def _(w):
            project(w, 3, c)

    keep = [
        pltpu.make_async_copy(normt, normt_out, so.at[0]),
        pltpu.make_async_copy(wpad, wpad_out, so.at[1]),
        pltpu.make_async_copy(qkv, qkv_out, so.at[2]),
    ]
    for copy in keep:
        copy.start()

    def trade(h, mask):
        spot = pl.ds(pl.multiple_of((here ^ mask) * rows, HP), rows)
        return remote(
            att.at[h, :, spot], got.at[SLOT[mask], h], st_.at[mask, h], rt_.at[mask, h], at(mask)
        )

    sub = lax.broadcasted_iota(jnp.int32, (HP, length), 0)

    @pl.loop(0, heads)
    def _(h):
        lanes = pl.ds(pl.multiple_of(h * HP, HP), HP)
        vt_ref[...] = jnp.where(sub == HD, 1.0, qkv[2, :, lanes].astype(F32).T).astype(BF)

        def scores(t):
            seen, low = reach(t, length), t * TILE
            st = mm(qkv[1, :seen, lanes], qkv[0, low : low + TILE, lanes], 1, 1)
            visible = idc_ref[low:seen, 0:1] <= idr_ref[:, low : low + TILE]
            masked = jnp.where(visible, st[low:], MASKED)
            return jnp.concatenate([st[:low], masked], 0) if low else masked

        st = scores(0)
        for t in range(tiles):
            later = scores(t + 1) if t + 1 < tiles else None
            seen, low = st.shape[0], t * TILE
            group = jnp.max(st.reshape(seen // 64, 64, TILE), axis=0)
            highest = jnp.max(group, axis=0, keepdims=True)
            weights = jnp.exp(st - highest).astype(BF)
            ot = mm(vt_ref[:, :seen], weights, 1, 0)
            summed = ot[HD : HD + 1, :]
            att[h, :, low : low + TILE] = (ot[:HD] * (1.0 / summed)).astype(BF)
            lse_ref[h, :, low : low + TILE] = highest + jnp.log(summed)
            st = later
        for mask in PARTNERS:
            trade(h, mask).start()
        if fused:
            for n in range(heads):

                @pl.when(h == n)
                def _(n=n):
                    if n == 0:
                        after_y(0, 1)
                    if n == 1:
                        after_y(0, 2)
                        after_y(0, 3)
                    if n == 2:
                        after_z(1)
                        after_y(1, 0)

    got[0] = att[:, :, pl.ds(pl.multiple_of(here * rows, HP), rows)]
    keep.append(pltpu.make_async_copy(att, att_out, so.at[5]))
    keep[-1].start()
    if fused:
        for step in range(far):
            x_second(step, 0).wait_recv()
            c_third(step, 0).start()
        for step in range(1, far):
            after_y(1, step)
        for step in range(far):
            x_second(step, 1).wait_recv()
            c_third(step, 1).start()
    for h in range(heads):
        for mask in PARTNERS:
            trade(h, mask).wait_recv()
    keep.append(pltpu.make_async_copy(got, got_out, so.at[6]))
    keep[-1].start()

    for c in range(count):
        send_x(c).wait_send()
        send_c(c).wait_send()
        forward(c).wait_send()
    for h in range(heads):
        for mask in PARTNERS:
            trade(h, mask).wait_send()
    if fused:
        swap_two.wait_send()
        for w in range(3):
            for step in range(far):
                if step:
                    z_first(w, step).wait_send()
                y_first(w, step).wait_send()
        for p in range(2):
            own_two(p).wait()
            for step in range(far):
                if step:
                    z_second(p, step).wait_send()
                y_second(p, step).wait_send()
                for side in range(2):
                    c_second(p, step, side).wait()
                    if p == 0:
                        x_second(step, side).wait_send()
                        c_third(step, side).wait()
    for copy in keep:
        copy.wait()


def front(dp, far, tokens, vectors, idr, cols, matrices):
    rows, width = tokens.shape
    length = idr.shape[1]
    heads = cols // HD
    wide = heads * HP
    packed = width // dp // 2
    count = rows // TILE
    vmem = pl.BlockSpec(memory_space=pltpu.VMEM)
    hbm = pl.BlockSpec(memory_space=pl.ANY)
    sem = pltpu.SemaphoreType.DMA
    far_n = max(far, 1)
    fused = far > 0
    small = (packed, 2 * cols) if fused else (16, 128)
    return pl.pallas_call(
        lambda *refs: front_kernel(dp, far, *refs),
        out_shape=[
            jax.ShapeDtypeStruct((3, length, wide), BF),
            jax.ShapeDtypeStruct((width, length), BF),
            jax.ShapeDtypeStruct((3, width, wide), BF),
            jax.ShapeDtypeStruct((heads, HD, length), BF),
            jax.ShapeDtypeStruct((heads, 1, length), F32),
            jax.ShapeDtypeStruct((4, heads, HD, rows), BF),
            jax.ShapeDtypeStruct((4, width, 2 * cols) if fused else (16, 128), BF),
            jax.ShapeDtypeStruct((width, 4 * cols) if fused else (16, 128), BF),
        ],
        in_specs=[vmem] * 9,
        out_specs=[hbm] * 4 + [vmem] + [hbm] * 3,
        scratch_shapes=[
            pltpu.VMEM((length, width), BF),
            pltpu.VMEM((width, length), BF),
            pltpu.VMEM((3, width, wide), BF),
            pltpu.VMEM((3, length, wide), BF),
            pltpu.VMEM((heads, HD, length), BF),
            pltpu.VMEM((4, heads, HD, rows), BF),
            pltpu.VMEM((HP, length), BF),
            pltpu.VMEM((length, HP), jnp.int32),
            pltpu.VMEM((8, wide), F32),
            pltpu.VMEM((3,) + small, BF),
            pltpu.VMEM(small, BF),
            pltpu.VMEM((far_n, 3) + small, BF),
            pltpu.VMEM((far_n, 3) + small, BF),
            pltpu.VMEM(small, BF),
            pltpu.VMEM((2, 2 * packed, 2 * cols) if fused else (2, 16, 128), BF),
            sem((count,)), sem((count,)), sem((count,)), sem((count,)), sem((count,)), sem((count,)),
            sem((far_n, 3)), sem((far_n, 3)), sem((far_n, 3)), sem((far_n, 3)),
            sem, sem,
            sem((2, far_n)), sem((2, far_n)), sem((2, far_n)), sem((2, far_n)),
            sem((2, far_n, 2)), sem((2, far_n, 2)),
            sem((far_n, 2)), sem((far_n, 2)), sem((far_n, 2)), sem((far_n, 2)),
            sem((4, heads)), sem((4, heads)),
            sem((12,)),
        ],
        compiler_params=pltpu.CompilerParams(
            vmem_limit_bytes=60 << 20, collective_id=1, has_side_effects=True
        ),
    )(tokens, vectors, idr, *matrices)


def mid_kernel(
    tok_ref, cot_ref, got_ref, vec_ref, wide_ref, both_ref,
    out_ref, dhid_ref, drec_out, xk_out, xg_out, pb_out, early_ref,
    w, both, att, n2, act, dpre, branch, hid, give, grec, db, drec, kept, bs,
    ss, rs, sg, rg, so,
):
    here, me = lax.axis_index("tensor"), lax.axis_index("dp")
    rows, width = tok_ref.shape
    wide = w.shape[1]
    cols = wide // 4
    pair = 2 * cols
    chunk = TILE
    half = chunk // 2
    count = rows // chunk

    def at(mask):
        return (me, here ^ mask)

    loads = [
        pltpu.make_async_copy(both_ref, both, so.at[1]),
        pltpu.make_async_copy(wide_ref, w.at[0], so.at[0]),
    ]
    for copy in loads:
        copy.start()
    greet([at(mask) for mask in PARTNERS])
    att[...] = got_ref[...].astype(F32).T.astype(BF)
    early_ref[...] = jnp.zeros_like(early_ref)
    bs[...] = jnp.zeros_like(bs)
    loads[0].wait()

    @pl.loop(0, width // chunk)
    def _(j):
        spot = pl.ds(pl.multiple_of(j * chunk, chunk), chunk)
        for i in range(4):
            w[1, spot, i * cols : (i + 1) * cols] = both[i, spot, :cols]
            w[2, spot, i * cols : (i + 1) * cols] = both[i, spot, cols:]

    loads[1].wait()

    def trade(c, mask):
        return remote(
            db.at[c, SLOT[mask]], drec.at[c, SLOT[mask]],
            ss.at[c, mask], rs.at[c, mask], at(mask),
        )

    @pl.loop(0, count)
    def _(c):
        low = pl.multiple_of(c * chunk, chunk)
        spot = pl.ds(low, chunk)
        hidden = tok_ref[spot, :].astype(F32) + mm(att[spot, :], w[0], 1, 1)
        hid[spot, :] = hidden
        cot = cot_ref[spot, :]
        d_act = mm(cot, w[2], 1, 0)
        inverse = lax.rsqrt(jnp.mean(hidden * hidden, axis=-1, keepdims=True) + EPSILON)
        hat = hidden * inverse
        normed = (hat * vec_ref[1:2, :]).astype(BF)
        n2[spot, :] = normed
        pre = mm(normed, w[1], 1, 0) + vec_ref[2:3, :]
        sig = jax.nn.sigmoid(pre)
        act[spot, :] = (pre * sig).astype(BF)
        d_pre = (d_act * sig * (1.0 + pre * (1.0 - sig))).astype(BF)
        dpre[spot, :] = d_pre
        d_n2 = mm(d_pre, w[1], 1, 1)
        scaled = d_n2 * vec_ref[1:2, :]
        cot_f32 = cot.astype(F32)
        d_hidden = cot_f32 + inverse * (
            scaled - hat * jnp.mean(scaled * hat, axis=-1, keepdims=True)
        )
        dhid_ref[spot, :] = d_hidden
        br = d_hidden.astype(BF)
        branch[spot, :] = br
        d_att = mm(br, w[0], 1, 0).astype(BF)
        for i in range(4):
            for part in range(2):
                db[c, i, :, part * cols : (part + 1) * cols] = d_att[
                    part * half : (part + 1) * half, i * cols : (i + 1) * cols
                ]
        for mask in PARTNERS:
            trade(c, mask).start()
        drec[c, 0] = db[c, 0]
        early_ref[0:1, :] += jnp.sum(d_n2 * hat, axis=0, keepdims=True)
        early_ref[1:2, :] += jnp.sum(cot_f32, axis=0, keepdims=True)
        bs[0:1, :] += jnp.sum(d_pre.astype(F32), axis=0, keepdims=True)

    pieces = ((branch, att), (n2, dpre), (cot_ref, act))

    def hand(i):
        return remote(give.at[i], grec.at[i], sg.at[i], rg.at[i], at(1))

    for i in range(3):

        @pl.loop(0, width // chunk)
        def _(j):
            spot = pl.ds(pl.multiple_of(j * chunk, chunk), chunk)
            left, right = pieces[i]
            g = mm(left[:, spot], right[...], 0, 0).astype(BF)
            give[i, spot, :] = g[:, pair:]
            if i == 0:
                kept[2, spot, :] = g[:, :pair]
            else:
                lane = (i - 1) * cols
                kept[0, spot, lane : lane + cols] = g[:, :cols]
                kept[1, spot, lane : lane + cols] = g[:, cols:pair]

        hand(i).start()

    for i in range(4):
        place = here ^ (0, 2, 1, 3)[i]
        early_ref[pl.ds(2 + place, 1), 0:cols] = bs[0:1, i * cols : (i + 1) * cols]

    @pl.loop(0, count)
    def _(c):
        spot = pl.ds(pl.multiple_of(c * chunk, chunk), chunk)
        out_ref[spot, :] = (hid[spot, :] + mm(act[spot, :], w[2], 1, 1) + vec_ref[3:4, :]).astype(BF)

    for i in range(3):
        hand(i).wait_recv()

        @pl.loop(0, width // chunk)
        def _(j):
            spot = pl.ds(pl.multiple_of(j * chunk, chunk), chunk)
            came = grec[i, spot, :]
            if i == 0:
                kept[2, spot, :] += came
            else:
                lane = (i - 1) * cols
                kept[0, spot, lane : lane + cols] += came[:, :cols]
                kept[1, spot, lane : lane + cols] += came[:, cols:]

        if i == 0:
            keep = [pltpu.make_async_copy(kept.at[2], pb_out, so.at[3])]
            keep[0].start()
    keep.append(pltpu.make_async_copy(kept.at[0], xk_out, so.at[4]))
    keep.append(pltpu.make_async_copy(kept.at[1], xg_out, so.at[5]))
    for copy in keep[1:]:
        copy.start()
    for c in range(count):
        for mask in PARTNERS:
            trade(c, mask).wait_recv()
    keep.append(pltpu.make_async_copy(drec, drec_out, so.at[6]))
    keep[-1].start()
    for c in range(count):
        for mask in PARTNERS:
            trade(c, mask).wait_send()
    for i in range(3):
        hand(i).wait_send()
    for copy in keep:
        copy.wait()


def middle(tokens, cotangent, got, vectors, wide, both):
    rows, width = tokens.shape
    all_cols = wide.shape[1]
    cols = all_cols // 4
    count = rows // TILE
    vmem = pl.BlockSpec(memory_space=pltpu.VMEM)
    hbm = pl.BlockSpec(memory_space=pl.ANY)
    sem = pltpu.SemaphoreType.DMA
    blocks = (count, 4, TILE // 2, 2 * cols)
    halves = jax.ShapeDtypeStruct((width, 2 * cols), BF)
    return pl.pallas_call(
        mid_kernel,
        out_shape=[
            jax.ShapeDtypeStruct((rows, width), BF),
            jax.ShapeDtypeStruct((rows, width), F32),
            jax.ShapeDtypeStruct(blocks, BF),
            halves,
            halves,
            halves,
            jax.ShapeDtypeStruct((16, width), F32),
        ],
        in_specs=[vmem] * 4 + [hbm] * 2,
        out_specs=[vmem, vmem, hbm, hbm, hbm, hbm, vmem],
        scratch_shapes=[
            pltpu.VMEM((3, width, all_cols), BF),
            pltpu.VMEM((4, width, 2 * cols), BF),
            pltpu.VMEM((rows, all_cols), BF),
            pltpu.VMEM((rows, width), BF),
            pltpu.VMEM((rows, all_cols), BF),
            pltpu.VMEM((rows, all_cols), BF),
            pltpu.VMEM((rows, width), BF),
            pltpu.VMEM((rows, width), F32),
            pltpu.VMEM((3, width, 2 * cols), BF),
            pltpu.VMEM((3, width, 2 * cols), BF),
            pltpu.VMEM(blocks, BF),
            pltpu.VMEM(blocks, BF),
            pltpu.VMEM((3, width, 2 * cols), BF),
            pltpu.VMEM((8, all_cols), F32),
            sem((count, 4)), sem((count, 4)), sem((3,)), sem((3,)), sem((8,)),
        ],
        compiler_params=pltpu.CompilerParams(
            vmem_limit_bytes=60 << 20, collective_id=2, has_side_effects=True
        ),
    )(tokens, cotangent, got, vectors, wide, both)


def back_kernel(
    dp, far, o_ref, lse_ref, drec_ref, vec_ref, idr_ref, xk_ref, early_ref,
    qkv_hbm, xg_ref, pb_ref, tok_hbm, dhid_hbm, normt_hbm, wpad_hbm,
    dtok_ref, dq_out, dk_out, dv_out, dout_ref, dup_ref, ddown_ref, sums_ref,
    do, dka, dva, kt_ref, idc_ref, dqkv, tok, dhid, normt, wpad,
    xrec, pbown, yrec, zrec, last, lastsend, lastrec,
    gpay, gyrec, gzrec, ownsum, near, fo, crec, fs, frec, nrec, qsum, lvec, ar, arec, aorder,
    so, sxa, rxa, sy, ry, sz, rz, sl, rl, sgy, rgy, sgz, rgz, sfo, rfo, sfs, rfs, sno, rno, sar, rar,
):
    here, me = lax.axis_index("tensor"), lax.axis_index("dp")
    heads, _, length = o_ref.shape
    rows, width = tok.shape
    cols = heads * HD
    tiles = length // TILE
    depth = width // dp
    packed = depth // 2
    fused = far > 0
    major, minor = me // 2, me % 2
    chunk = TILE
    count = rows // chunk

    def at(mask):
        return (me, here ^ mask)

    across = (me ^ 1, here)

    def along(step):
        return (lax.rem(major + step, far) * 2 + minor, here)

    def target(step):
        return lax.rem(major + step, far)

    loads = [
        pltpu.make_async_copy(src, dst, so.at[i])
        for i, (src, dst) in enumerate(
            ((wpad_hbm, wpad), (normt_hbm, normt), (tok_hbm, tok), (dhid_hbm, dhid))
        )
    ]
    load_qkv = pltpu.make_async_copy(qkv_hbm, dqkv, so.at[4])
    load_qkv.start()
    if fused:
        load_pb = pltpu.make_async_copy(pb_ref.at[:, minor], pbown, so.at[5])
        load_pb.start()
    for copy in loads:
        copy.start()
    peers = [at(2), at(1)]
    if fused:
        peers += [across] + [along(step) for step in range(1, far)]
    greet(peers)

    turn = list(range(1, far)) + [0]

    def x_send(step):
        spot = target(step)
        return remote(xg_ref.at[spot], xrec.at[spot], sxa.at[step], rxa.at[step], at(2))

    def y_send(p, step):
        spot = target(step)
        src = xrec.at[spot, 1 - minor] if p == 0 else pb_ref.at[spot, 1 - minor]
        return remote(src, yrec.at[p, spot], sy.at[p, step], ry.at[p, step], across)

    def z_send(p, step):
        return remote(
            yrec.at[p, target(step)], zrec.at[p, step - 1],
            sz.at[p, step], rz.at[p, step], along(step),
        )

    def after_x(step):
        x_send(step).wait_recv()
        spot = target(step)
        xrec[spot] = xk_ref[spot] + xrec[spot]
        y_send(0, step).start()

    def after_y(p, step):
        y_send(p, step).wait_recv()
        spot = target(step)
        mine = xrec[spot, minor] if p == 0 else pbown[spot]

        @pl.when(step != 0)
        def _():
            yrec[p, spot] = mine + yrec[p, spot]
            z_send(p, step).start()

        @pl.when(step == 0)
        def _():
            last[p] = mine.astype(F32) + yrec[p, spot].astype(F32)

    def after_z(p):
        for step in range(1, far):
            z_send(p, step).wait_recv()
            last[p] += zrec[p, step - 1].astype(F32)

    if fused:
        for step in turn:
            x_send(step).start()
            y_send(1, step).start()

    do[...] = jnp.zeros_like(do)
    half = chunk // 2
    for c in range(count):
        for i, mask in enumerate((0, 2, 1, 3)):
            block = drec_ref[c, i]
            for part in range(2):
                low = pl.multiple_of((here ^ mask) * rows + c * chunk + part * half, half)
                for h in range(heads):
                    lane = part * cols + h * HD
                    do[h, pl.ds(low, half), 0:HD] = block[:, lane : lane + HD]
    qsum[...] = jnp.zeros_like(qsum)
    if fused:
        gpay[...] = jnp.zeros_like(gpay)
    idc_ref[...] = jnp.broadcast_to(idr_ref[...].astype(F32), (HP, length)).T.astype(jnp.int32)

    load_qkv.wait()
    if fused:
        load_pb.wait()

    def one_head(h):
        lanes = pl.ds(pl.multiple_of(h * HP, HP), HP)
        kt_ref[...] = dqkv[1, :, lanes].astype(F32).T.astype(BF)
        dka[...] = jnp.zeros_like(dka)
        dva[...] = jnp.zeros_like(dva)
        scale_sum = jnp.zeros((1, HP), F32)
        for t in range(tiles):
            seen, low = reach(t, length), t * TILE
            spot = slice(low, low + TILE)
            qt = dqkv[0, spot, lanes]
            dot_ = do[h, spot, :]
            delta = jnp.sum(
                dot_.astype(F32).T[:HD] * o_ref[h, :, spot].astype(F32), axis=0, keepdims=True
            )
            st = mm(dqkv[1, :seen, lanes], qt, 1, 1)
            p = jnp.exp(st - lse_ref[h, :, spot])
            visible = idc_ref[low:seen, 0:1] <= idr_ref[:, spot]
            pm = jnp.where(visible, p[low:], 0.0)
            p = jnp.concatenate([p[:low], pm], 0) if low else pm
            d_p = mm(dqkv[2, :seen, lanes], dot_, 1, 1)
            ds = (p * (d_p - delta)).astype(BF)
            dva[:seen, :] += mm(p.astype(BF), dot_, 1, 0)
            dka[:seen, :] += mm(ds, qt, 1, 0)
            dq = mm(kt_ref[:, :seen], ds, 1, 0).T
            scale_sum = scale_sum + jnp.sum(dq * qt.astype(F32), axis=0, keepdims=True)
            dqkv[0, spot, lanes] = (dq * vec_ref[4:5, :HP]).astype(BF)
        dqkv[1, :, lanes] = dka[...].astype(BF)
        dqkv[2, :, lanes] = dva[...].astype(BF)
        qsum[0:1, :] += scale_sum

    group = 2 * HD

    def weight_blocks(n, step):
        spot = target(step)
        low = pl.multiple_of(spot * 2 * depth, 16)
        lanes = slice(n * 2 * HP, (n + 1) * 2 * HP)
        dots = jnp.zeros((2 * depth, 1), F32)
        for i in range(3):
            g = mm(normt[pl.ds(low, 2 * depth), :], dqkv[i, :, lanes], 1, 0)
            dots = dots + jnp.sum(
                g * wpad[i, pl.ds(low, 2 * depth), lanes].astype(F32), axis=1, keepdims=True
            )
            g = g.astype(BF)
            for side in range(2):
                for h in range(2):
                    lane = i * group + h * HD
                    gpay[n, spot, side, :, lane : lane + HD] = g[
                        side * depth : (side + 1) * depth, h * HP : h * HP + HD
                    ]
        flat = jnp.broadcast_to(dots, (2 * depth, HP)).T[0:1, :]
        lvec[n, pl.ds(spot * 2, 1), :] = flat[:, :depth]
        lvec[n, pl.ds(spot * 2 + 1, 1), :] = flat[:, depth:]

    def gy_send(n, step):
        spot = target(step)
        return remote(
            gpay.at[n, spot, 1 - minor], gyrec.at[n, spot], sgy.at[n, step], rgy.at[n, step], across
        )

    def gz_send(n, step):
        return remote(
            gyrec.at[n, target(step)], gzrec.at[n, step - 1],
            sgz.at[n, step], rgz.at[n, step], along(step),
        )

    def weight_pair(n):
        @pl.loop(0, far)
        def _(j):
            step = lax.rem(j + 1, far)
            weight_blocks(n, step)
            gy_send(n, step).start()

    def gz_start(n, step):
        gy_send(n, step).wait_recv()
        spot = target(step)
        mine = gpay[n, spot, minor]

        @pl.when(step != 0)
        def _():
            gyrec[n, spot] = mine + gyrec[n, spot]
            gz_send(n, step).start()

        @pl.when(step == 0)
        def _():
            ownsum[n] = mine.astype(F32) + gyrec[n, spot].astype(F32)

    @pl.loop(0, heads)
    def _(h):
        one_head(h)
        if fused:
            after_x(lax.rem(h + 1, far))

            @pl.when(h < 2)
            def _():
                @pl.loop(0, 2)
                def _(k):
                    after_y(1, lax.rem(2 * h + k + 1, far))

            @pl.when(h > 0)
            def _():
                after_y(0, h)

            @pl.when(h == 1)
            def _():
                for copy in loads[:2]:
                    copy.wait()
                weight_pair(0)

            @pl.when(h == 2)
            def _():
                @pl.loop(0, far)
                def _(j):
                    gz_start(0, lax.rem(j + 1, far))

    if not fused:
        for copy in loads[:2]:
            copy.wait()

    def part(mask, c):
        spot = pl.ds(pl.multiple_of((here ^ mask) * rows + c * chunk, chunk), chunk)
        total = mm(dqkv[0, spot, :], wpad[0], 1, 1)
        total = total + mm(dqkv[1, spot, :], wpad[1], 1, 1)
        return total + mm(dqkv[2, spot, :], wpad[2], 1, 1)

    def c_far(c):
        return remote(fo.at[c], crec.at[c], sfo.at[c], rfo.at[c], at(1))

    def x_far(c):
        return remote(fs.at[c], frec.at[c], sfs.at[c], rfs.at[c], at(2))

    def c_near(c):
        return remote(fo.at[c], nrec.at[c], sno.at[c], rno.at[c], at(1))

    def far_chunk(c):
        fo[c] = part(3, c).astype(BF)
        c_far(c).start()

    def far_sum(c):
        own = part(2, c)
        c_far(c).wait_recv()
        fs[c] = (own + crec[c].astype(F32)).astype(BF)

    def hop(n, where):
        return remote(ar.at[n], arec.at[n], sar.at[n], rar.at[n], where)

    def z_hop(step):
        return remote(ar.at[3], arec.at[3 + step], sar.at[3 + step], rar.at[3 + step], along(step))

    if fused:
        far_chunk(0)
        far_sum(0)
        x_far(0).start()
        after_y(0, turn[far - 1])
        weight_pair(1)
        ar[0] = jnp.zeros_like(ar[0])
        ar[0, 0:6, :] = early_ref[0:6, :]
        ar[0, 6:7, 0:HP] = qsum[0:1, :]
        ar[0, 8:16, 0:depth] = lvec[0] + lvec[1]
        hop(0, at(1)).start()
        for c in range(1, count):
            far_chunk(c)

        @pl.loop(1, 3)
        def _(step):
            gz_start(1, step)

        hop(0, at(1)).wait_recv()
        ar[1] = ar[0] + arec[0]
        hop(1, at(2)).start()
        for c in range(1, count):
            far_sum(c)
            x_far(c).start()
        after_z(1)
        for piece in range(2):
            last_half = last[1, piece * packed : (piece + 1) * packed, cols:]
            lastsend[:, piece * cols : (piece + 1) * cols] = last_half.astype(BF)
        cross = remote(lastsend, lastrec, sl, rl, at(2))
        cross.start()
    else:
        for c in range(count):
            far_chunk(c)
            far_sum(c)
            x_far(c).start()

        @pl.loop(0, 3)
        def _(i):
            for j in range(width // chunk):
                dq_out[i, j * chunk : (j + 1) * chunk, :] = mm(
                    normt[j * chunk : (j + 1) * chunk, :], dqkv[i], 1, 0
                )

    if not fused:
        sums_ref[...] = jnp.zeros_like(sums_ref)
        sums_ref[0:6, :] = early_ref[0:6, :]
        sums_ref[6:7, 0:HP] = qsum[0:1, :]

    @pl.loop(0, count)
    def _(c):
        c_far(c).wait_send()
        fo[c] = part(1, c).astype(BF)
        c_near(c).start()

    if fused:

        @pl.loop(0, 2)
        def _(j):
            gz_start(1, lax.rem(j + 3, far))

        hop(1, at(2)).wait_recv()
        ar[2] = ar[1] + arec[1]
        hop(2, across).start()
        after_z(0)
        dup_ref[...] = last[0, :, :cols]
        ddown_ref[...] = last[0, :, cols:]
    for copy in loads[2:]:
        copy.wait()

    @pl.loop(0, count)
    def _(c):
        near[c] = part(0, c)

    if fused:
        hop(2, across).wait_recv()
        ar[3] = ar[2] + arec[2]
        for step in range(1, far):
            z_hop(step).start()
        cross.wait_recv()
        arrived = jnp.concatenate([lastrec[:, :cols], lastrec[:, cols:]], axis=0)
        dout_ref[...] = last[1, :, :cols] + arrived.astype(F32)

    @pl.loop(0, count)
    def _(c):
        c_near(c).wait_recv()
        x_far(c).wait_recv()
        d_normed = near[c] + nrec[c].astype(F32) + frec[c].astype(F32)
        spot = pl.ds(pl.multiple_of(c * chunk, chunk), chunk)
        v = tok[spot, :].astype(F32)
        inverse = lax.rsqrt(jnp.mean(v * v, axis=-1, keepdims=True) + EPSILON)
        hat = v * inverse
        scaled = d_normed * vec_ref[0:1, :]
        dtok_ref[spot, :] = (
            dhid[spot, :]
            + inverse * (scaled - hat * jnp.mean(scaled * hat, axis=-1, keepdims=True))
        ).astype(BF)

    if fused:
        for n in range(2):
            for step in range(1, far):
                gz_send(n, step).wait_recv()
                ownsum[n] += gzrec[n, step - 1].astype(F32)
            for i, ref in enumerate((dq_out, dk_out, dv_out)):
                ref[:, n * group : (n + 1) * group] = ownsum[n, :, i * group : (i + 1) * group]
        aorder[major] = ar[3]
        for step in range(1, far):
            z_hop(step).wait_recv()
            aorder[lax.rem(major + far - step, far)] = arec[3 + step]
        sums_ref[...] = (aorder[0] + aorder[1]) + (aorder[2] + aorder[3])
    else:
        dk_out[...] = jnp.zeros_like(dk_out)
        dv_out[...] = jnp.zeros_like(dv_out)
        dout_ref[...] = jnp.zeros_like(dout_ref)
        dup_ref[...] = jnp.zeros_like(dup_ref)
        ddown_ref[...] = jnp.zeros_like(ddown_ref)

    for c in range(count):
        x_far(c).wait_send()
        c_near(c).wait_send()
    if fused:
        for step in range(far):
            x_send(step).wait_send()
            for p in range(2):
                gy_send(p, step).wait_send()
                y_send(p, step).wait_send()
            if step:
                gz_send(0, step).wait_send()
                gz_send(1, step).wait_send()
                z_hop(step).wait_send()
                for p in range(2):
                    z_send(p, step).wait_send()
        cross.wait_send()
        hop(0, at(1)).wait_send()
        hop(1, at(2)).wait_send()
        hop(2, across).wait_send()


def backward(dp, far, o, lse, drec, vectors, idr, xk, early, qkv, xg, pb,
             tokens, d_hidden, normt, wpad):
    heads, _, length = o.shape
    rows, width = tokens.shape
    cols, wide = heads * HD, heads * HP
    depth = width // dp
    packed = depth // 2
    count = rows // TILE
    fused = far > 0
    far_n = max(far, 1)
    vmem = pl.BlockSpec(memory_space=pltpu.VMEM)
    hbm = pl.BlockSpec(memory_space=pl.ANY)
    sem = pltpu.SemaphoreType.DMA
    tiny = jax.ShapeDtypeStruct((8, 128), F32)
    shard = jax.ShapeDtypeStruct((depth, cols), F32) if fused else tiny
    whole = shard if fused else jax.ShapeDtypeStruct((3, width, wide), F32)

    def buf(*shape, dtype=BF, only=True):
        return pltpu.VMEM(shape if fused or not only else (8, 128), dtype)

    pair = 2 * cols
    return pl.pallas_call(
        lambda *refs: back_kernel(dp, far, *refs),
        out_shape=[jax.ShapeDtypeStruct((rows, width), BF), whole, shard, shard, shard, shard,
                   shard, jax.ShapeDtypeStruct((16, width), F32)],
        in_specs=[vmem] * 7 + [hbm] * 7,
        out_specs=[vmem] * 8,
        scratch_shapes=[
            buf(heads, length, HP, only=False),
            buf(length, HP, dtype=F32, only=False),
            buf(length, HP, dtype=F32, only=False),
            buf(HP, length, only=False),
            buf(length, HP, dtype=jnp.int32, only=False),
            buf(3, length, wide, only=False),
            buf(rows, width, only=False),
            buf(rows, width, dtype=F32, only=False),
            buf(width, length, only=False),
            buf(3, width, wide, only=False),
            buf(far_n, 2, depth, pair),
            buf(far_n, depth, pair),
            buf(2, far_n, depth, pair),
            buf(2, far_n - 1, depth, pair),
            buf(2, depth, pair, dtype=F32),
            buf(packed, pair),
            buf(packed, pair),
            buf(2, far_n, 2, depth, 4 * HP),
            buf(2, far_n, depth, 4 * HP),
            buf(2, far_n - 1, depth, 4 * HP),
            buf(2, depth, 4 * HP, dtype=F32),
            buf(count, TILE, width, dtype=F32, only=False),
            buf(count, TILE, width, only=False),
            buf(count, TILE, width, only=False),
            buf(count, TILE, width, only=False),
            buf(count, TILE, width, only=False),
            buf(count, TILE, width, only=False),
            buf(8, HP, dtype=F32, only=False),
            buf(2, dp, depth, dtype=F32),
            buf(4, 16, width, dtype=F32),
            buf(3 + far_n, 16, width, dtype=F32),
            buf(far_n, 16, width, dtype=F32),
            sem((6,)),
            sem((far_n,)), sem((far_n,)),
            sem((2, far_n)), sem((2, far_n)), sem((2, far_n)), sem((2, far_n)),
            sem, sem,
            sem((2, far_n)), sem((2, far_n)), sem((2, far_n)), sem((2, far_n)),
            sem((count,)), sem((count,)), sem((count,)), sem((count,)), sem((count,)), sem((count,)),
            sem((3 + far_n,)), sem((3 + far_n,)),
        ],
        compiler_params=pltpu.CompilerParams(
            vmem_limit_bytes=62 << 20, collective_id=3, has_side_effects=True
        ),
    )(o, lse, drec, vectors, idr, xk, early, qkv, xg, pb,
      tokens, d_hidden, normt, wpad)


def finish_kernel(dp, cols, scale_ref, sums_ref, vec_ref, *refs):
    moves, outs, held = refs[:8], refs[8:21], refs[21:29]
    row, sem = refs[29:]
    width = vec_ref.shape[1]
    depth = width // dp
    places = (0, 1, 3, 4, 5, 7, 9, 11)
    enter = [pltpu.make_async_copy(moves[i], held[i], sem.at[i]) for i in range(8)]
    leave = [pltpu.make_async_copy(held[i], outs[places[i]], sem.at[8 + i]) for i in range(8)]
    for copy in enter:
        copy.start()
    outs[6][...] = sums_ref[6, 0:HP] * scale_ref[0, :]
    outs[8][...] = sums_ref[0, :]
    outs[12][...] = sums_ref[1, :]
    row[...] = jnp.zeros_like(row)
    for i in range(width // cols):
        row[0:1, i * cols : (i + 1) * cols] = sums_ref[2 + i : 3 + i, :cols]
    for i in range(dp):
        spot = slice(i * depth, (i + 1) * depth)
        row[1:2, spot] = sums_ref[8 + i : 9 + i, :depth] / vec_ref[0:1, spot]
    outs[10][...] = row[0, :]
    outs[2][...] = row[1, :]
    for come, go in zip(enter, leave):
        come.wait()
        go.start()
    for copy in leave:
        copy.wait()


def finish(dp, cols, scale, sums, vectors, moves):
    width = vectors.shape[1]
    vmem = pl.BlockSpec(memory_space=pltpu.VMEM)
    hbm = pl.BlockSpec(memory_space=pl.ANY)
    row = jax.ShapeDtypeStruct((width,), F32)
    like = [jax.ShapeDtypeStruct(v.shape, v.dtype) for v in moves]
    shapes = like[:2] + [row] + like[2:5] + [jax.ShapeDtypeStruct((HP,), F32)]
    shapes += [like[5], row, like[6], row, like[7], row]
    small = (2, 6, 8, 10, 12)
    return pl.pallas_call(
        lambda *refs: finish_kernel(dp, cols, *refs),
        out_shape=shapes,
        in_specs=[vmem] * 3 + [hbm] * 8,
        out_specs=[vmem if i in small else hbm for i in range(13)],
        scratch_shapes=[pltpu.VMEM(v.shape, v.dtype) for v in moves]
        + [pltpu.VMEM((8, width), F32), pltpu.SemaphoreType.DMA((16,))],
        compiler_params=pltpu.CompilerParams(vmem_limit_bytes=60 << 20),
    )(scale, sums, vectors, *moves)


def swap(v, axis, size, mask):
    return lax.ppermute(v, axis, [(i, i ^ mask) for i in range(size)])


def gather_dp(shard):
    return lax.all_gather(shard, "dp", axis=0, tiled=True)


def scatter_dp(grad, size):
    return lax.psum_scatter(grad, "dp", scatter_dimension=0, tiled=True)


def pad_heads(w):
    rows, cols = w.shape
    w = w.reshape(rows, cols // HD, HD)
    return jnp.pad(w, ((0, 0), (0, 0), (0, HP - HD))).reshape(rows, cols // HD * HP)


def trim_heads(w):
    rows, cols = w.shape
    return w.reshape(rows, cols // HP, HP)[:, :, :HD].reshape(rows, cols // HP * HD)


def body(dp, tensor, tokens, cotangent, block_ids, attn_gain, w_query, w_key, w_value,
         query_scale, w_out, mlp_gain, w_up, b_up, w_down, b_down):
    assert tensor == 4
    here = lax.axis_index("tensor")
    rows, width = tokens.shape
    length = rows * tensor
    cols = w_query.shape[1]
    heads = cols // HD
    order = [here, here ^ 2, here ^ 1, here ^ 3]

    softplus = jnp.log1p(jnp.exp(query_scale))
    factor = jnp.pad(SCORE_BASE / math.sqrt(HD) * softplus, (0, HP - HD))
    b_rel = jnp.concatenate([lax.dynamic_slice(b_up, (at * cols,), (cols,)) for at in order])
    repeat = jnp.pad(jnp.tile(factor, heads), (0, width - heads * HP))
    vectors = jnp.concatenate([attn_gain, mlp_gain, b_rel, b_down, repeat]).reshape(5, width)

    far = dp // 2 if dp == 8 else 0
    matrices = (w_query, w_key, w_value, w_out.T, w_up, w_down.T)
    if not far:
        pair = [jnp.concatenate([w, swap(w, "tensor", tensor, 2)], axis=1) for w in matrices[3:]]
        half = gather_dp(jnp.concatenate(pair, axis=1)).reshape(width, 3, 2 * cols)
        both = jnp.concatenate([half, swap(half, "tensor", tensor, 1)], axis=2)
        full = gather_dp(jnp.concatenate(matrices[:3], axis=1))
        first = jnp.stack([pad_heads(full[:, i * cols : (i + 1) * cols]) for i in range(3)])
        matrices = (first,) + matrices[1:]
    qkv, normed_t, padded, attended, lse, got, pairs, wide = front(
        dp, far, tokens, vectors, block_ids, cols, matrices
    )
    if not far:
        wide = both[:, 0]
        pairs = both[:, 1:].reshape(width, 2, 4, cols).transpose(2, 0, 1, 3)
        pairs = pairs.reshape(4, width, 2 * cols)

    output, d_hidden, received, xk, xg, pb, early = middle(
        tokens, cotangent, got.reshape(4 * cols, rows), vectors, wide, pairs
    )
    depth = width // dp
    if far:
        xk, xg, pb = (v.reshape(far, 2, depth, 2 * cols) for v in (xk, xg, pb))
    d_tokens, s_q, s_k, s_v, s_out, s_up, s_down, sums = backward(
        dp, far, attended, lse, received, vectors, block_ids, xk, early,
        qkv, xg, pb, tokens, d_hidden, normed_t, padded,
    )
    slope = jax.nn.sigmoid(query_scale) / softplus
    if far:
        scale = jnp.pad(slope, (0, HP - HD))[None, :]
        final = list(
            finish(
                dp, cols, scale, sums, vectors,
                (output, d_tokens, s_q, s_k, s_v, s_out, s_up, s_down),
            )
        )
        final[6] = final[6][:HD]
        final[7], final[11] = final[7].T, final[11].T
        return tuple(final)
    else:
        dots = lax.psum(jnp.sum(s_q * padded.astype(F32), axis=(0, 2)), ("dp", "tensor"))
        sums = lax.psum(sums, ("dp", "tensor"))
        s_qkv = scatter_dp(jnp.concatenate([trim_heads(g) for g in s_q], axis=1), dp)
        s_q, s_k, s_v = (s_qkv[:, i * cols : (i + 1) * cols] for i in range(3))
        both = xk.astype(F32) + swap(xg, "tensor", tensor, 2).astype(F32)
        both = scatter_dp(both, dp)
        s_up, s_down = both[:, :cols], both[:, cols:].T
        both = scatter_dp(pb.astype(F32), dp)
        s_out = (both[:, :cols] + swap(both[:, cols:], "tensor", tensor, 2)).T
    d_scale = sums[6, :HD] * slope
    return (
        output,
        d_tokens,
        dots / attn_gain,
        s_q,
        s_k,
        s_v,
        d_scale,
        s_out,
        sums[0],
        s_up,
        sums[2:6, :cols].reshape(4 * cols),
        s_down,
        sums[1],
    )


def solution(mesh):
    weight, turned, whole = P("dp", "tensor"), P("tensor", "dp"), P()
    positions = P(("dp", "tensor"), None)
    return jax.shard_map(
        lambda *args: body(mesh.shape["dp"], mesh.shape["tensor"], *args),
        mesh=mesh,
        in_specs=(positions, positions, P("dp", None), whole, weight, weight, weight, whole,
                  turned, whole, weight, whole, turned, whole),
        out_specs=(positions, positions, whole, weight, weight, weight, whole, turned, whole,
                   weight, whole, turned, whole),
        check_vma=False,
    )
```

```python
import math

import jax
import jax.numpy as jnp
from jax import lax
from jax.experimental import pallas as pl
from jax.experimental.pallas import tpu as pltpu
from jax.sharding import PartitionSpec as P

HD = 80
HP = 128
TILE = 256
BLOCK_MOST = 256
EPSILON = 1e-06
SCORE_BASE = 1.442695041
MASKED = -1e30
BF = jnp.bfloat16
F32 = jnp.float32


def mm(a, b, ca, cb):
    return lax.dot_general(a, b, (((ca,), (cb,)), ((), ())), preferred_element_type=F32)


def reach(tile, length):
    return min((tile + 1) * TILE + BLOCK_MOST, length)


MESH = pl.DeviceIdType.MESH
PARTNERS = (2, 1, 3)
SLOT = {0: 0, 2: 1, 1: 2, 3: 3}


def remote(src, dst, send, recv, where):
    return pltpu.make_async_remote_copy(
        src_ref=src, dst_ref=dst, send_sem=send, recv_sem=recv, device_id=where, device_id_type=MESH
    )


def greet(peers):
    barrier = pltpu.get_barrier_semaphore()
    for where in peers:
        pl.semaphore_signal(barrier, inc=1, device_id=where, device_id_type=MESH)
    pl.semaphore_wait(barrier, len(peers))


def front_kernel(
    dp, far, tok_ref, vec_ref, idr_ref, wq_ref, wk_ref, wv_ref, wo_ref, wu_ref, wd_ref,
    qkv_out, normt_out, wpad_out, att_out, lse_ref, got_out, both_out, wide_out,
    norm, normt, wpad, qkv, att, got, vt_ref, idc_ref, fac, w1_ref, w2_ref, z1, y1, x2, pair,
    sx, rx, sc, rc, sf, rf, sz1, rz1, sy1, ry1, sx2, rx2, sz2, rz2, sy2, ry2, sc2, rc2,
    sx3, rx3, sc3, rc3, st_, rt_, so,
):
    here, me = lax.axis_index("tensor"), lax.axis_index("dp")
    rows, width = tok_ref.shape
    length = norm.shape[0]
    tiles = length // TILE
    heads = qkv.shape[2] // HP
    cols = heads * HD
    depth = width // dp
    packed = depth // 2
    fused = far > 0
    major, minor = me // 2, me % 2

    def at(mask):
        return (me, here ^ mask)

    def xor(mask):
        return here ^ mask

    across = (me ^ 1, here)

    def along(step):
        return (lax.rem(major + step, far) * 2 + minor, here)

    def source(step):
        return lax.rem(major + far - step, far)

    peers = [at(mask) for mask in PARTNERS]
    if fused:
        peers += [across] + [along(step) for step in range(1, far)]
    greet(peers)

    def z_first(w, step):
        return remote(
            w1_ref.at[w], z1.at[step, w], sz1.at[step, w], rz1.at[step, w], along(step)
        )

    def y_first(w, step):
        src = w1_ref.at[w] if isinstance(step, int) and step == 0 else z1.at[step, w]
        return remote(src, y1.at[step, w], sy1.at[step, w], ry1.at[step, w], across)

    swap_two = remote(w2_ref, x2, sx2, rx2, at(2)) if fused else None
    if fused:
        for w, ref in enumerate((wq_ref, wk_ref, wv_ref)):
            w1_ref[w, :, :cols] = ref[:packed, :]
            w1_ref[w, :, cols:] = ref[packed:, :]
            for step in range(1, far):
                z_first(w, step).start()
            y_first(w, 0).start()
        pair[0, :, :cols] = wu_ref[...]
        pair[0, :, cols:] = wd_ref[...]
        pair[1, :, :cols] = wo_ref[...]
        w2_ref[:, :cols] = wo_ref[:packed, :]
        w2_ref[:, cols:] = wo_ref[packed:, :]
        swap_two.start()

    chunk = TILE
    count = rows // chunk

    @pl.loop(0, count)
    def _(c):
        low = pl.multiple_of(c * chunk, chunk)
        v = tok_ref[pl.ds(low, chunk), :].astype(F32)
        hat = v * lax.rsqrt(jnp.mean(v * v, axis=-1, keepdims=True) + EPSILON)
        norm[pl.ds(pl.multiple_of(here * rows + low, chunk), chunk), :] = (
            hat * vec_ref[0:1, :]
        ).astype(BF)

    def rows_of(mask, c):
        return norm.at[pl.ds(pl.multiple_of((here ^ mask) * rows + c * chunk, chunk), chunk), :]

    def send_x(c):
        return remote(rows_of(0, c), rows_of(0, c), sx.at[c], rx.at[c], at(2))

    def send_c(c):
        return remote(rows_of(0, c), rows_of(0, c), sc.at[c], rc.at[c], at(1))

    def forward(c):
        return remote(rows_of(2, c), rows_of(2, c), sf.at[c], rf.at[c], at(1))

    for c in range(count):
        send_x(c).start()
        send_c(c).start()
    idc_ref[...] = jnp.broadcast_to(idr_ref[...].astype(F32), (HP, length)).T.astype(jnp.int32)
    fac[...] = jnp.ones_like(fac)
    fac[0:1, :] = vec_ref[4:5, : heads * HP]

    def project(w, mask, c):
        low = pl.multiple_of(xor(mask) * rows + c * chunk, chunk)
        x = norm[pl.ds(low, chunk), :]
        y = mm(x, wpad[w], 1, 0)
        qkv[w, pl.ds(low, chunk), :] = (y * fac[pl.ds(w, 1), :]).astype(BF)

        @pl.when(w == 2)
        def _():
            normt[:, pl.ds(low, chunk)] = x.astype(F32).T.astype(BF)

    def rows_two(index):
        return pl.ds(pl.multiple_of(index * depth, 16), depth)

    def index_of(step, side):
        return source(step) * 2 + (minor if side == 0 else 1 - minor)

    def block_two(p, index):
        if p == 0:
            return both_out.at[0, rows_two(index), :]
        return wide_out.at[rows_two(index), pl.ds(0, 2 * cols)]

    def held_two(p, step, side):
        return pair.at[p] if step == 0 and side == 0 else block_two(p, index_of(step, side))

    def z_second(p, step):
        return remote(
            pair.at[p], block_two(p, me), sz2.at[p, step], rz2.at[p, step], along(step)
        )

    def y_second(p, step):
        return remote(
            held_two(p, step, 0), block_two(p, index_of(step, 0)),
            sy2.at[p, step], ry2.at[p, step], across,
        )

    def c_second(p, step, side):
        index = index_of(step, side)
        if p == 0:
            dst = both_out.at[2, rows_two(index), :]
        else:
            dst = wide_out.at[rows_two(index), pl.ds(2 * cols, 2 * cols)]
        return remote(
            held_two(p, step, side), dst, sc2.at[p, step, side], rc2.at[p, step, side], at(1)
        )

    def x_second(step, side):
        return remote(
            held_two(0, step, side), both_out.at[1, rows_two(index_of(step, side)), :],
            sx3.at[step, side], rx3.at[step, side], at(2),
        )

    def c_third(step, side):
        spot = rows_two(index_of(step, side))
        return remote(
            both_out.at[1, spot, :], both_out.at[3, spot, :],
            sc3.at[step, side], rc3.at[step, side], at(1),
        )

    def own_two(p):
        return pltpu.make_async_copy(pair.at[p], block_two(p, me), so.at[8 + p])

    def start_second(p):
        for step in range(1, far):
            z_second(p, step).start()
        y_second(p, 0).start()
        own_two(p).start()

    def spread(p, step, side):
        c_second(p, step, side).start()
        if p == 0:
            x_second(step, side).start()

    def after_z(p):
        for step in range(1, far):
            z_second(p, step).wait_recv()
            y_second(p, step).start()
            spread(p, step, 0)

    def after_y(p, step):
        y_second(p, step).wait_recv()
        spread(p, step, 1)

    if fused:
        start_second(0)
        spread(0, 0, 0)
        swap_two.wait_recv()
        for part in range(2):
            pair[1, part * packed : (part + 1) * packed, cols:] = x2[
                :, part * cols : (part + 1) * cols
            ]
        start_second(1)
        spread(1, 0, 0)

    if not fused:
        wpad[...] = wq_ref[...]
        for c in range(count):
            send_c(c).wait_recv()

        @pl.loop(0, 3)
        def _(w):
            @pl.loop(0, 2 * count)
            def _(j):
                project(w, j // count, lax.rem(j, count))

    else:
        wpad[...] = jnp.zeros_like(wpad)

        def unpack(w, block, device):
            for part in range(2):
                low = pl.multiple_of(device * depth + part * packed, 16)
                for h in range(heads):
                    lane = part * cols + h * HD
                    wpad[w, pl.ds(low, packed), h * HP : h * HP + HD] = block[:, lane : lane + HD]

        @pl.loop(0, 3)
        def _(w):
            unpack(w, w1_ref[w], me)

            @pl.loop(1, far)
            def _(step):
                z_first(w, step).wait_recv()
                y_first(w, step).start()
                unpack(w, z1[step, w], source(step) * 2 + minor)

            @pl.loop(0, far)
            def _(step):
                y_first(w, step).wait_recv()
                unpack(w, y1[step, w], source(step) * 2 + 1 - minor)

            @pl.when(w == 0)
            def _():
                for c in range(count):
                    send_c(c).wait_recv()

            @pl.loop(0, 2 * count)
            def _(j):
                project(w, j // count, lax.rem(j, count))

            @pl.when(w == 1)
            def _():
                after_y(0, 0)

        after_z(0)

    @pl.loop(0, count)
    def _(c):
        send_x(c).wait_recv()
        forward(c).start()

        @pl.loop(0, 3)
        def _(w):
            project(w, 2, c)

    @pl.loop(0, count)
    def _(c):
        forward(c).wait_recv()

        @pl.loop(0, 3)
        def _(w):
            project(w, 3, c)

    keep = [
        pltpu.make_async_copy(normt, normt_out, so.at[0]),
        pltpu.make_async_copy(wpad, wpad_out, so.at[1]),
        pltpu.make_async_copy(qkv, qkv_out, so.at[2]),
    ]
    for copy in keep:
        copy.start()

    def trade(h, mask):
        spot = pl.ds(pl.multiple_of((here ^ mask) * rows, HP), rows)
        return remote(
            att.at[h, :, spot], got.at[SLOT[mask], h], st_.at[mask, h], rt_.at[mask, h], at(mask)
        )

    sub = lax.broadcasted_iota(jnp.int32, (HP, length), 0)

    @pl.loop(0, heads)
    def _(h):
        lanes = pl.ds(pl.multiple_of(h * HP, HP), HP)
        vt_ref[...] = jnp.where(sub == HD, 1.0, qkv[2, :, lanes].astype(F32).T).astype(BF)

        def scores(t):
            seen, low = reach(t, length), t * TILE
            st = mm(qkv[1, :seen, lanes], qkv[0, low : low + TILE, lanes], 1, 1)
            visible = idc_ref[low:seen, 0:1] <= idr_ref[:, low : low + TILE]
            masked = jnp.where(visible, st[low:], MASKED)
            return jnp.concatenate([st[:low], masked], 0) if low else masked

        st = scores(0)
        for t in range(tiles):
            later = scores(t + 1) if t + 1 < tiles else None
            seen, low = st.shape[0], t * TILE
            group = jnp.max(st.reshape(seen // 64, 64, TILE), axis=0)
            highest = jnp.max(group, axis=0, keepdims=True)
            weights = jnp.exp(st - highest).astype(BF)
            ot = mm(vt_ref[:, :seen], weights, 1, 0)
            summed = ot[HD : HD + 1, :]
            att[h, :, low : low + TILE] = (ot[:HD] * (1.0 / summed)).astype(BF)
            lse_ref[h, :, low : low + TILE] = highest + jnp.log(summed)
            st = later
        for mask in PARTNERS:
            trade(h, mask).start()
        if fused:
            for n in range(heads):

                @pl.when(h == n)
                def _(n=n):
                    if n == 0:
                        after_y(0, 1)
                    if n == 1:
                        after_y(0, 2)
                        after_y(0, 3)
                    if n == 2:
                        after_z(1)
                        after_y(1, 0)

    got[0] = att[:, :, pl.ds(pl.multiple_of(here * rows, HP), rows)]
    keep.append(pltpu.make_async_copy(att, att_out, so.at[5]))
    keep[-1].start()
    if fused:
        for step in range(far):
            x_second(step, 0).wait_recv()
            c_third(step, 0).start()
        for step in range(1, far):
            after_y(1, step)
        for step in range(far):
            x_second(step, 1).wait_recv()
            c_third(step, 1).start()
    for h in range(heads):
        for mask in PARTNERS:
            trade(h, mask).wait_recv()
    keep.append(pltpu.make_async_copy(got, got_out, so.at[6]))
    keep[-1].start()

    for c in range(count):
        send_x(c).wait_send()
        send_c(c).wait_send()
        forward(c).wait_send()
    for h in range(heads):
        for mask in PARTNERS:
            trade(h, mask).wait_send()
    if fused:
        swap_two.wait_send()
        for w in range(3):
            for step in range(far):
                if step:
                    z_first(w, step).wait_send()
                y_first(w, step).wait_send()
        for p in range(2):
            own_two(p).wait()
            for step in range(far):
                if step:
                    z_second(p, step).wait_send()
                y_second(p, step).wait_send()
                for side in range(2):
                    c_second(p, step, side).wait()
                    if p == 0:
                        x_second(step, side).wait_send()
                        c_third(step, side).wait()
    for copy in keep:
        copy.wait()


def front(dp, far, tokens, vectors, idr, cols, matrices):
    rows, width = tokens.shape
    length = idr.shape[1]
    heads = cols // HD
    wide = heads * HP
    packed = width // dp // 2
    count = rows // TILE
    vmem = pl.BlockSpec(memory_space=pltpu.VMEM)
    hbm = pl.BlockSpec(memory_space=pl.ANY)
    sem = pltpu.SemaphoreType.DMA
    far_n = max(far, 1)
    fused = far > 0
    small = (packed, 2 * cols) if fused else (16, 128)
    return pl.pallas_call(
        lambda *refs: front_kernel(dp, far, *refs),
        out_shape=[
            jax.ShapeDtypeStruct((3, length, wide), BF),
            jax.ShapeDtypeStruct((width, length), BF),
            jax.ShapeDtypeStruct((3, width, wide), BF),
            jax.ShapeDtypeStruct((heads, HD, length), BF),
            jax.ShapeDtypeStruct((heads, 1, length), F32),
            jax.ShapeDtypeStruct((4, heads, HD, rows), BF),
            jax.ShapeDtypeStruct((4, width, 2 * cols) if fused else (16, 128), BF),
            jax.ShapeDtypeStruct((width, 4 * cols) if fused else (16, 128), BF),
        ],
        in_specs=[vmem] * 9,
        out_specs=[hbm] * 4 + [vmem] + [hbm] * 3,
        scratch_shapes=[
            pltpu.VMEM((length, width), BF),
            pltpu.VMEM((width, length), BF),
            pltpu.VMEM((3, width, wide), BF),
            pltpu.VMEM((3, length, wide), BF),
            pltpu.VMEM((heads, HD, length), BF),
            pltpu.VMEM((4, heads, HD, rows), BF),
            pltpu.VMEM((HP, length), BF),
            pltpu.VMEM((length, HP), jnp.int32),
            pltpu.VMEM((8, wide), F32),
            pltpu.VMEM((3,) + small, BF),
            pltpu.VMEM(small, BF),
            pltpu.VMEM((far_n, 3) + small, BF),
            pltpu.VMEM((far_n, 3) + small, BF),
            pltpu.VMEM(small, BF),
            pltpu.VMEM((2, 2 * packed, 2 * cols) if fused else (2, 16, 128), BF),
            sem((count,)), sem((count,)), sem((count,)), sem((count,)), sem((count,)), sem((count,)),
            sem((far_n, 3)), sem((far_n, 3)), sem((far_n, 3)), sem((far_n, 3)),
            sem, sem,
            sem((2, far_n)), sem((2, far_n)), sem((2, far_n)), sem((2, far_n)),
            sem((2, far_n, 2)), sem((2, far_n, 2)),
            sem((far_n, 2)), sem((far_n, 2)), sem((far_n, 2)), sem((far_n, 2)),
            sem((4, heads)), sem((4, heads)),
            sem((12,)),
        ],
        compiler_params=pltpu.CompilerParams(
            vmem_limit_bytes=60 << 20, collective_id=1, has_side_effects=True
        ),
    )(tokens, vectors, idr, *matrices)


def mid_kernel(
    tok_ref, cot_ref, got_ref, vec_ref, wide_ref, both_ref,
    out_ref, dhid_ref, drec_out, xk_out, xg_out, pb_out, early_ref,
    w, both, att, n2, act, dpre, branch, hid, give, grec, db, drec, kept, bs,
    ss, rs, sg, rg, so,
):
    here, me = lax.axis_index("tensor"), lax.axis_index("dp")
    rows, width = tok_ref.shape
    wide = w.shape[1]
    cols = wide // 4
    pair = 2 * cols
    chunk = TILE
    half = chunk // 2
    count = rows // chunk

    def at(mask):
        return (me, here ^ mask)

    loads = [
        pltpu.make_async_copy(both_ref, both, so.at[1]),
        pltpu.make_async_copy(wide_ref, w.at[0], so.at[0]),
    ]
    for copy in loads:
        copy.start()
    greet([at(mask) for mask in PARTNERS])
    att[...] = got_ref[...].astype(F32).T.astype(BF)
    early_ref[...] = jnp.zeros_like(early_ref)
    bs[...] = jnp.zeros_like(bs)
    loads[0].wait()

    @pl.loop(0, width // chunk)
    def _(j):
        spot = pl.ds(pl.multiple_of(j * chunk, chunk), chunk)
        for i in range(4):
            w[1, spot, i * cols : (i + 1) * cols] = both[i, spot, :cols]
            w[2, spot, i * cols : (i + 1) * cols] = both[i, spot, cols:]

    loads[1].wait()

    def trade(c, mask):
        return remote(
            db.at[c, SLOT[mask]], drec.at[c, SLOT[mask]],
            ss.at[c, mask], rs.at[c, mask], at(mask),
        )

    @pl.loop(0, count)
    def _(c):
        low = pl.multiple_of(c * chunk, chunk)
        spot = pl.ds(low, chunk)
        hidden = tok_ref[spot, :].astype(F32) + mm(att[spot, :], w[0], 1, 1)
        hid[spot, :] = hidden
        cot = cot_ref[spot, :]
        d_act = mm(cot, w[2], 1, 0)
        inverse = lax.rsqrt(jnp.mean(hidden * hidden, axis=-1, keepdims=True) + EPSILON)
        hat = hidden * inverse
        normed = (hat * vec_ref[1:2, :]).astype(BF)
        n2[spot, :] = normed
        pre = mm(normed, w[1], 1, 0) + vec_ref[2:3, :]
        sig = jax.nn.sigmoid(pre)
        act[spot, :] = (pre * sig).astype(BF)
        d_pre = (d_act * sig * (1.0 + pre * (1.0 - sig))).astype(BF)
        dpre[spot, :] = d_pre
        d_n2 = mm(d_pre, w[1], 1, 1)
        scaled = d_n2 * vec_ref[1:2, :]
        cot_f32 = cot.astype(F32)
        d_hidden = cot_f32 + inverse * (
            scaled - hat * jnp.mean(scaled * hat, axis=-1, keepdims=True)
        )
        dhid_ref[spot, :] = d_hidden
        br = d_hidden.astype(BF)
        branch[spot, :] = br
        d_att = mm(br, w[0], 1, 0).astype(BF)
        for i in range(4):
            for part in range(2):
                db[c, i, :, part * cols : (part + 1) * cols] = d_att[
                    part * half : (part + 1) * half, i * cols : (i + 1) * cols
                ]
        for mask in PARTNERS:
            trade(c, mask).start()
        drec[c, 0] = db[c, 0]
        early_ref[0:1, :] += jnp.sum(d_n2 * hat, axis=0, keepdims=True)
        early_ref[1:2, :] += jnp.sum(cot_f32, axis=0, keepdims=True)
        bs[0:1, :] += jnp.sum(d_pre.astype(F32), axis=0, keepdims=True)

    pieces = ((branch, att), (n2, dpre), (cot_ref, act))

    def hand(i):
        return remote(give.at[i], grec.at[i], sg.at[i], rg.at[i], at(1))

    for i in range(3):

        @pl.loop(0, width // chunk)
        def _(j):
            spot = pl.ds(pl.multiple_of(j * chunk, chunk), chunk)
            left, right = pieces[i]
            g = mm(left[:, spot], right[...], 0, 0).astype(BF)
            give[i, spot, :] = g[:, pair:]
            if i == 0:
                kept[2, spot, :] = g[:, :pair]
            else:
                lane = (i - 1) * cols
                kept[0, spot, lane : lane + cols] = g[:, :cols]
                kept[1, spot, lane : lane + cols] = g[:, cols:pair]

        hand(i).start()

    for i in range(4):
        place = here ^ (0, 2, 1, 3)[i]
        early_ref[pl.ds(2 + place, 1), 0:cols] = bs[0:1, i * cols : (i + 1) * cols]

    @pl.loop(0, count)
    def _(c):
        spot = pl.ds(pl.multiple_of(c * chunk, chunk), chunk)
        out_ref[spot, :] = (hid[spot, :] + mm(act[spot, :], w[2], 1, 1) + vec_ref[3:4, :]).astype(BF)

    for i in range(3):
        hand(i).wait_recv()

        @pl.loop(0, width // chunk)
        def _(j):
            spot = pl.ds(pl.multiple_of(j * chunk, chunk), chunk)
            came = grec[i, spot, :]
            if i == 0:
                kept[2, spot, :] += came
            else:
                lane = (i - 1) * cols
                kept[0, spot, lane : lane + cols] += came[:, :cols]
                kept[1, spot, lane : lane + cols] += came[:, cols:]

        if i == 0:
            keep = [pltpu.make_async_copy(kept.at[2], pb_out, so.at[3])]
            keep[0].start()
    keep.append(pltpu.make_async_copy(kept.at[0], xk_out, so.at[4]))
    keep.append(pltpu.make_async_copy(kept.at[1], xg_out, so.at[5]))
    for copy in keep[1:]:
        copy.start()
    for c in range(count):
        for mask in PARTNERS:
            trade(c, mask).wait_recv()
    keep.append(pltpu.make_async_copy(drec, drec_out, so.at[6]))
    keep[-1].start()
    for c in range(count):
        for mask in PARTNERS:
            trade(c, mask).wait_send()
    for i in range(3):
        hand(i).wait_send()
    for copy in keep:
        copy.wait()


def middle(tokens, cotangent, got, vectors, wide, both):
    rows, width = tokens.shape
    all_cols = wide.shape[1]
    cols = all_cols // 4
    count = rows // TILE
    vmem = pl.BlockSpec(memory_space=pltpu.VMEM)
    hbm = pl.BlockSpec(memory_space=pl.ANY)
    sem = pltpu.SemaphoreType.DMA
    blocks = (count, 4, TILE // 2, 2 * cols)
    halves = jax.ShapeDtypeStruct((width, 2 * cols), BF)
    return pl.pallas_call(
        mid_kernel,
        out_shape=[
            jax.ShapeDtypeStruct((rows, width), BF),
            jax.ShapeDtypeStruct((rows, width), F32),
            jax.ShapeDtypeStruct(blocks, BF),
            halves,
            halves,
            halves,
            jax.ShapeDtypeStruct((16, width), F32),
        ],
        in_specs=[vmem] * 4 + [hbm] * 2,
        out_specs=[vmem, vmem, hbm, hbm, hbm, hbm, vmem],
        scratch_shapes=[
            pltpu.VMEM((3, width, all_cols), BF),
            pltpu.VMEM((4, width, 2 * cols), BF),
            pltpu.VMEM((rows, all_cols), BF),
            pltpu.VMEM((rows, width), BF),
            pltpu.VMEM((rows, all_cols), BF),
            pltpu.VMEM((rows, all_cols), BF),
            pltpu.VMEM((rows, width), BF),
            pltpu.VMEM((rows, width), F32),
            pltpu.VMEM((3, width, 2 * cols), BF),
            pltpu.VMEM((3, width, 2 * cols), BF),
            pltpu.VMEM(blocks, BF),
            pltpu.VMEM(blocks, BF),
            pltpu.VMEM((3, width, 2 * cols), BF),
            pltpu.VMEM((8, all_cols), F32),
            sem((count, 4)), sem((count, 4)), sem((3,)), sem((3,)), sem((8,)),
        ],
        compiler_params=pltpu.CompilerParams(
            vmem_limit_bytes=60 << 20, collective_id=2, has_side_effects=True
        ),
    )(tokens, cotangent, got, vectors, wide, both)


def back_kernel(
    dp, far, o_ref, lse_ref, drec_ref, vec_ref, idr_ref, xk_ref, early_ref,
    qkv_hbm, xg_ref, pb_ref, tok_hbm, dhid_hbm, normt_hbm, wpad_hbm,
    dtok_ref, dq_out, dk_out, dv_out, dout_ref, dup_ref, ddown_ref, sums_ref,
    do, dka, dva, kt_ref, idc_ref, dqkv, tok, dhid, normt, wpad,
    xrec, pbown, yrec, zrec, last, lastsend, lastrec,
    gpay, gyrec, gzrec, ownsum, near, fo, crec, fs, frec, nrec, qsum, lvec, ar, arec, aorder, er, erec, eorder,
    so, sxa, rxa, sy, ry, sz, rz, sl, rl, sgy, rgy, sgz, rgz, sfo, rfo, sfs, rfs, sno, rno, sar, rar, ser, rer,
):
    here, me = lax.axis_index("tensor"), lax.axis_index("dp")
    heads, _, length = o_ref.shape
    rows, width = tok.shape
    cols = heads * HD
    tiles = length // TILE
    depth = width // dp
    packed = depth // 2
    fused = far > 0
    major, minor = me // 2, me % 2
    chunk = TILE
    count = rows // chunk

    def at(mask):
        return (me, here ^ mask)

    across = (me ^ 1, here)

    def along(step):
        return (lax.rem(major + step, far) * 2 + minor, here)

    def target(step):
        return lax.rem(major + step, far)

    loads = [
        pltpu.make_async_copy(src, dst, so.at[i])
        for i, (src, dst) in enumerate(
            ((wpad_hbm, wpad), (normt_hbm, normt), (tok_hbm, tok), (dhid_hbm, dhid))
        )
    ]
    load_qkv = pltpu.make_async_copy(qkv_hbm, dqkv, so.at[4])
    load_qkv.start()
    if fused:
        load_pb = pltpu.make_async_copy(pb_ref.at[:, minor], pbown, so.at[5])
        load_pb.start()
    for copy in loads:
        copy.start()
    peers = [at(2), at(1)]
    if fused:
        peers += [across] + [along(step) for step in range(1, far)]
    greet(peers)

    turn = list(range(1, far)) + [0]

    def x_send(step):
        spot = target(step)
        return remote(xg_ref.at[spot], xrec.at[spot], sxa.at[step], rxa.at[step], at(2))

    def y_send(p, step):
        spot = target(step)
        src = xrec.at[spot, 1 - minor] if p == 0 else pb_ref.at[spot, 1 - minor]
        return remote(src, yrec.at[p, spot], sy.at[p, step], ry.at[p, step], across)

    def z_send(p, step):
        return remote(
            yrec.at[p, target(step)], zrec.at[p, step - 1],
            sz.at[p, step], rz.at[p, step], along(step),
        )

    def after_x(step):
        x_send(step).wait_recv()
        spot = target(step)
        xrec[spot] = xk_ref[spot] + xrec[spot]
        y_send(0, step).start()

    def after_y(p, step):
        y_send(p, step).wait_recv()
        spot = target(step)
        mine = xrec[spot, minor] if p == 0 else pbown[spot]

        @pl.when(step != 0)
        def _():
            yrec[p, spot] = mine + yrec[p, spot]
            z_send(p, step).start()

        @pl.when(step == 0)
        def _():
            last[p] = mine.astype(F32) + yrec[p, spot].astype(F32)

    def after_z(p):
        for step in range(1, far):
            z_send(p, step).wait_recv()
            last[p] += zrec[p, step - 1].astype(F32)

    def e_hop(n, where):
        return remote(er.at[n], erec.at[n], ser.at[n], rer.at[n], where)

    def e_last():
        return remote(er.at[3], erec.at[2], ser.at[2], rer.at[2], at(2))

    def e_z(step):
        return remote(er.at[2], erec.at[3 + step], ser.at[3 + step], rer.at[3 + step], along(step))

    def early_hop(h):
        @pl.when(h == 0)
        def _():
            e_hop(0, at(1)).wait_recv()
            er[1] = er[0] + erec[0]
            e_hop(1, across).start()

        @pl.when(h == 1)
        def _():
            e_hop(1, across).wait_recv()
            er[2] = er[1] + erec[1]
            for step in range(1, far):
                e_z(step).start()

        @pl.when(h == 2)
        def _():
            eorder[major] = er[2]
            for step in range(1, far):
                e_z(step).wait_recv()
                eorder[lax.rem(major + far - step, far)] = erec[3 + step]
            er[3] = (eorder[0] + eorder[1]) + (eorder[2] + eorder[3])
            e_last().start()

    if fused:
        er[0] = early_ref[0:8, :]
        e_hop(0, at(1)).start()
        for step in turn:
            x_send(step).start()
            y_send(1, step).start()

    do[...] = jnp.zeros_like(do)
    half = chunk // 2
    for c in range(count):
        for i, mask in enumerate((0, 2, 1, 3)):
            block = drec_ref[c, i]
            for part in range(2):
                low = pl.multiple_of((here ^ mask) * rows + c * chunk + part * half, half)
                for h in range(heads):
                    lane = part * cols + h * HD
                    do[h, pl.ds(low, half), 0:HD] = block[:, lane : lane + HD]
    qsum[...] = jnp.zeros_like(qsum)
    if fused:
        gpay[...] = jnp.zeros_like(gpay)
    idc_ref[...] = jnp.broadcast_to(idr_ref[...].astype(F32), (HP, length)).T.astype(jnp.int32)

    load_qkv.wait()
    if fused:
        load_pb.wait()

    def one_head(h):
        lanes = pl.ds(pl.multiple_of(h * HP, HP), HP)
        kt_ref[...] = dqkv[1, :, lanes].astype(F32).T.astype(BF)
        dka[...] = jnp.zeros_like(dka)
        dva[...] = jnp.zeros_like(dva)
        scale_sum = jnp.zeros((1, HP), F32)
        for t in range(tiles):
            seen, low = reach(t, length), t * TILE
            spot = slice(low, low + TILE)
            qt = dqkv[0, spot, lanes]
            dot_ = do[h, spot, :]
            delta = jnp.sum(
                dot_.astype(F32).T[:HD] * o_ref[h, :, spot].astype(F32), axis=0, keepdims=True
            )
            st = mm(dqkv[1, :seen, lanes], qt, 1, 1)
            p = jnp.exp(st - lse_ref[h, :, spot])
            visible = idc_ref[low:seen, 0:1] <= idr_ref[:, spot]
            pm = jnp.where(visible, p[low:], 0.0)
            p = jnp.concatenate([p[:low], pm], 0) if low else pm
            d_p = mm(dqkv[2, :seen, lanes], dot_, 1, 1)
            ds = (p * (d_p - delta)).astype(BF)
            dva[:seen, :] += mm(p.astype(BF), dot_, 1, 0)
            dka[:seen, :] += mm(ds, qt, 1, 0)
            dq = mm(kt_ref[:, :seen], ds, 1, 0).T
            scale_sum = scale_sum + jnp.sum(dq * qt.astype(F32), axis=0, keepdims=True)
            dqkv[0, spot, lanes] = (dq * vec_ref[4:5, :HP]).astype(BF)
        dqkv[1, :, lanes] = dka[...].astype(BF)
        dqkv[2, :, lanes] = dva[...].astype(BF)
        qsum[0:1, :] += scale_sum

    group = 2 * HD

    def weight_blocks(n, step):
        spot = target(step)
        low = pl.multiple_of(spot * 2 * depth, 16)
        lanes = slice(n * 2 * HP, (n + 1) * 2 * HP)
        dots = jnp.zeros((2 * depth, 1), F32)
        for i in range(3):
            g = mm(normt[pl.ds(low, 2 * depth), :], dqkv[i, :, lanes], 1, 0)
            dots = dots + jnp.sum(
                g * wpad[i, pl.ds(low, 2 * depth), lanes].astype(F32), axis=1, keepdims=True
            )
            g = g.astype(BF)
            for side in range(2):
                for h in range(2):
                    lane = i * group + h * HD
                    gpay[n, spot, side, :, lane : lane + HD] = g[
                        side * depth : (side + 1) * depth, h * HP : h * HP + HD
                    ]
        flat = jnp.broadcast_to(dots, (2 * depth, HP)).T[0:1, :]
        lvec[n, pl.ds(spot * 2, 1), :] = flat[:, :depth]
        lvec[n, pl.ds(spot * 2 + 1, 1), :] = flat[:, depth:]

    def gy_send(n, step):
        spot = target(step)
        return remote(
            gpay.at[n, spot, 1 - minor], gyrec.at[n, spot], sgy.at[n, step], rgy.at[n, step], across
        )

    def gz_send(n, step):
        return remote(
            gyrec.at[n, target(step)], gzrec.at[n, step - 1],
            sgz.at[n, step], rgz.at[n, step], along(step),
        )

    def weight_pair(n):
        @pl.loop(0, far)
        def _(j):
            step = lax.rem(j + 1, far)
            weight_blocks(n, step)
            gy_send(n, step).start()

    def gz_start(n, step):
        gy_send(n, step).wait_recv()
        spot = target(step)
        mine = gpay[n, spot, minor]

        @pl.when(step != 0)
        def _():
            gyrec[n, spot] = mine + gyrec[n, spot]
            gz_send(n, step).start()

        @pl.when(step == 0)
        def _():
            ownsum[n] = mine.astype(F32) + gyrec[n, spot].astype(F32)

    @pl.loop(0, heads)
    def _(h):
        one_head(h)
        if fused:
            early_hop(h)
            after_x(lax.rem(h + 1, far))

            @pl.when(h < 2)
            def _():
                @pl.loop(0, 2)
                def _(k):
                    after_y(1, lax.rem(2 * h + k + 1, far))

            @pl.when(h == 1)
            def _():
                for copy in loads[:2]:
                    copy.wait()
                weight_pair(0)

            @pl.when(h > 0)
            def _():
                after_y(0, h)

    if not fused:
        for copy in loads[:2]:
            copy.wait()

    def part(mask, c):
        spot = pl.ds(pl.multiple_of((here ^ mask) * rows + c * chunk, chunk), chunk)
        total = mm(dqkv[0, spot, :], wpad[0], 1, 1)
        total = total + mm(dqkv[1, spot, :], wpad[1], 1, 1)
        return total + mm(dqkv[2, spot, :], wpad[2], 1, 1)

    def c_far(c):
        return remote(fo.at[c], crec.at[c], sfo.at[c], rfo.at[c], at(1))

    def x_far(c):
        return remote(fs.at[c], frec.at[c], sfs.at[c], rfs.at[c], at(2))

    def c_near(c):
        return remote(fo.at[c], nrec.at[c], sno.at[c], rno.at[c], at(1))

    def far_chunk(c):
        fo[c] = part(3, c).astype(BF)
        c_far(c).start()

    def far_sum(c):
        own = part(2, c)
        c_far(c).wait_recv()
        fs[c] = (own + crec[c].astype(F32)).astype(BF)

    def hop(n, where):
        return remote(ar.at[n], arec.at[n], sar.at[n], rar.at[n], where)

    def z_hop(step):
        return remote(ar.at[3], arec.at[3 + step], sar.at[3 + step], rar.at[3 + step], along(step))

    if fused:
        far_chunk(0)
        far_sum(0)
        x_far(0).start()

        @pl.loop(0, far)
        def _(j):
            gz_start(0, lax.rem(j + 1, far))

        after_y(0, turn[far - 1])
        weight_pair(1)
        for index in range(dp):
            spot = slice(index * depth, (index + 1) * depth)
            ar[0, :, spot] = lvec[0, index : index + 1, :] + lvec[1, index : index + 1, :]
        ar[0, :, width:] = qsum[0:1, :]
        hop(0, at(1)).start()
        for c in range(1, count):
            far_chunk(c)

        @pl.loop(1, 3)
        def _(step):
            gz_start(1, step)

        hop(0, at(1)).wait_recv()
        ar[1] = ar[0] + arec[0]
        hop(1, at(2)).start()
        for c in range(1, count):
            far_sum(c)
            x_far(c).start()
        after_z(1)
        for piece in range(2):
            last_half = last[1, piece * packed : (piece + 1) * packed, cols:]
            lastsend[:, piece * cols : (piece + 1) * cols] = last_half.astype(BF)
        cross = remote(lastsend, lastrec, sl, rl, at(2))
        cross.start()
    else:
        for c in range(count):
            far_chunk(c)
            far_sum(c)
            x_far(c).start()

        @pl.loop(0, 3)
        def _(i):
            for j in range(width // chunk):
                dq_out[i, j * chunk : (j + 1) * chunk, :] = mm(
                    normt[j * chunk : (j + 1) * chunk, :], dqkv[i], 1, 0
                )

    if not fused:
        sums_ref[...] = jnp.zeros_like(sums_ref)
        sums_ref[0:6, :] = early_ref[0:6, :]
        sums_ref[6:7, 0:HP] = qsum[0:1, :]

    @pl.loop(0, count)
    def _(c):
        c_far(c).wait_send()
        fo[c] = part(1, c).astype(BF)
        c_near(c).start()

    if fused:

        @pl.loop(0, 2)
        def _(j):
            gz_start(1, lax.rem(j + 3, far))

        hop(1, at(2)).wait_recv()
        ar[2] = ar[1] + arec[1]
        hop(2, across).start()
        after_z(0)
        dup_ref[...] = last[0, :, :cols]
        ddown_ref[...] = last[0, :, cols:]
    for copy in loads[2:]:
        copy.wait()

    @pl.loop(0, count)
    def _(c):
        near[c] = part(0, c)

    if fused:
        hop(2, across).wait_recv()
        ar[3] = ar[2] + arec[2]
        for step in range(1, far):
            z_hop(step).start()
        cross.wait_recv()
        arrived = jnp.concatenate([lastrec[:, :cols], lastrec[:, cols:]], axis=0)
        dout_ref[...] = last[1, :, :cols] + arrived.astype(F32)

    @pl.loop(0, count)
    def _(c):
        c_near(c).wait_recv()
        x_far(c).wait_recv()
        d_normed = near[c] + nrec[c].astype(F32) + frec[c].astype(F32)
        spot = pl.ds(pl.multiple_of(c * chunk, chunk), chunk)
        v = tok[spot, :].astype(F32)
        inverse = lax.rsqrt(jnp.mean(v * v, axis=-1, keepdims=True) + EPSILON)
        hat = v * inverse
        scaled = d_normed * vec_ref[0:1, :]
        dtok_ref[spot, :] = (
            dhid[spot, :]
            + inverse * (scaled - hat * jnp.mean(scaled * hat, axis=-1, keepdims=True))
        ).astype(BF)

    if fused:
        for n in range(2):
            for step in range(1, far):
                gz_send(n, step).wait_recv()
                ownsum[n] += gzrec[n, step - 1].astype(F32)
            for i, ref in enumerate((dq_out, dk_out, dv_out)):
                ref[:, n * group : (n + 1) * group] = ownsum[n, :, i * group : (i + 1) * group]
        aorder[major] = ar[3]
        for step in range(1, far):
            z_hop(step).wait_recv()
            aorder[lax.rem(major + far - step, far)] = arec[3 + step]
        total = (aorder[0] + aorder[1]) + (aorder[2] + aorder[3])
        e_last().wait_recv()
        sums_ref[...] = jnp.zeros_like(sums_ref)
        sums_ref[0:8, :] = er[3] + erec[2]
        sums_ref[6:7, 0:HP] = total[:, width:]
        sums_ref[7:8, :] = total[:, :width]
    else:
        dk_out[...] = jnp.zeros_like(dk_out)
        dv_out[...] = jnp.zeros_like(dv_out)
        dout_ref[...] = jnp.zeros_like(dout_ref)
        dup_ref[...] = jnp.zeros_like(dup_ref)
        ddown_ref[...] = jnp.zeros_like(ddown_ref)

    for c in range(count):
        x_far(c).wait_send()
        c_near(c).wait_send()
    if fused:
        for step in range(far):
            x_send(step).wait_send()
            for p in range(2):
                gy_send(p, step).wait_send()
                y_send(p, step).wait_send()
            if step:
                gz_send(0, step).wait_send()
                gz_send(1, step).wait_send()
                z_hop(step).wait_send()
                e_z(step).wait_send()
                for p in range(2):
                    z_send(p, step).wait_send()
        cross.wait_send()
        hop(0, at(1)).wait_send()
        hop(1, at(2)).wait_send()
        hop(2, across).wait_send()
        e_hop(0, at(1)).wait_send()
        e_hop(1, across).wait_send()
        e_last().wait_send()


def backward(dp, far, o, lse, drec, vectors, idr, xk, early, qkv, xg, pb,
             tokens, d_hidden, normt, wpad):
    heads, _, length = o.shape
    rows, width = tokens.shape
    cols, wide = heads * HD, heads * HP
    depth = width // dp
    packed = depth // 2
    count = rows // TILE
    fused = far > 0
    far_n = max(far, 1)
    vmem = pl.BlockSpec(memory_space=pltpu.VMEM)
    hbm = pl.BlockSpec(memory_space=pl.ANY)
    sem = pltpu.SemaphoreType.DMA
    tiny = jax.ShapeDtypeStruct((8, 128), F32)
    shard = jax.ShapeDtypeStruct((depth, cols), F32) if fused else tiny
    whole = shard if fused else jax.ShapeDtypeStruct((3, width, wide), F32)

    def buf(*shape, dtype=BF, only=True):
        return pltpu.VMEM(shape if fused or not only else (8, 128), dtype)

    pair = 2 * cols
    return pl.pallas_call(
        lambda *refs: back_kernel(dp, far, *refs),
        out_shape=[jax.ShapeDtypeStruct((rows, width), BF), whole, shard, shard, shard, shard,
                   shard, jax.ShapeDtypeStruct((16, width), F32)],
        in_specs=[vmem] * 7 + [hbm] * 7,
        out_specs=[vmem] * 8,
        scratch_shapes=[
            buf(heads, length, HP, only=False),
            buf(length, HP, dtype=F32, only=False),
            buf(length, HP, dtype=F32, only=False),
            buf(HP, length, only=False),
            buf(length, HP, dtype=jnp.int32, only=False),
            buf(3, length, wide, only=False),
            buf(rows, width, only=False),
            buf(rows, width, dtype=F32, only=False),
            buf(width, length, only=False),
            buf(3, width, wide, only=False),
            buf(far_n, 2, depth, pair),
            buf(far_n, depth, pair),
            buf(2, far_n, depth, pair),
            buf(2, far_n - 1, depth, pair),
            buf(2, depth, pair, dtype=F32),
            buf(packed, pair),
            buf(packed, pair),
            buf(2, far_n, 2, depth, 4 * HP),
            buf(2, far_n, depth, 4 * HP),
            buf(2, far_n - 1, depth, 4 * HP),
            buf(2, depth, 4 * HP, dtype=F32),
            buf(count, TILE, width, dtype=F32, only=False),
            buf(count, TILE, width, only=False),
            buf(count, TILE, width, only=False),
            buf(count, TILE, width, only=False),
            buf(count, TILE, width, only=False),
            buf(count, TILE, width, only=False),
            buf(8, HP, dtype=F32, only=False),
            buf(2, dp, depth, dtype=F32),
            buf(4, 1, width + HP, dtype=F32),
            buf(3 + far_n, 1, width + HP, dtype=F32),
            buf(far_n, 1, width + HP, dtype=F32),
            buf(4, 8, width, dtype=F32),
            buf(3 + far_n, 8, width, dtype=F32),
            buf(far_n, 8, width, dtype=F32),
            sem((6,)),
            sem((far_n,)), sem((far_n,)),
            sem((2, far_n)), sem((2, far_n)), sem((2, far_n)), sem((2, far_n)),
            sem, sem,
            sem((2, far_n)), sem((2, far_n)), sem((2, far_n)), sem((2, far_n)),
            sem((count,)), sem((count,)), sem((count,)), sem((count,)), sem((count,)), sem((count,)),
            sem((3 + far_n,)), sem((3 + far_n,)), sem((3 + far_n,)), sem((3 + far_n,)),
        ],
        compiler_params=pltpu.CompilerParams(
            vmem_limit_bytes=62 << 20, collective_id=3, has_side_effects=True
        ),
    )(o, lse, drec, vectors, idr, xk, early, qkv, xg, pb,
      tokens, d_hidden, normt, wpad)


def finish_kernel(dp, cols, scale_ref, sums_ref, vec_ref, *refs):
    moves, outs, held = refs[:8], refs[8:21], refs[21:29]
    row, sem = refs[29:]
    width = vec_ref.shape[1]
    places = (0, 1, 3, 4, 5, 7, 9, 11)
    enter = [pltpu.make_async_copy(moves[i], held[i], sem.at[i]) for i in range(8)]
    leave = [pltpu.make_async_copy(held[i], outs[places[i]], sem.at[8 + i]) for i in range(8)]
    for copy in enter:
        copy.start()
    outs[6][...] = sums_ref[6, 0:HP] * scale_ref[0, :]
    outs[8][...] = sums_ref[0, :]
    outs[12][...] = sums_ref[1, :]
    row[...] = jnp.zeros_like(row)
    for i in range(width // cols):
        row[0:1, i * cols : (i + 1) * cols] = sums_ref[2 + i : 3 + i, :cols]
    row[1:2, :] = sums_ref[7:8, :] / vec_ref[0:1, :]
    outs[10][...] = row[0, :]
    outs[2][...] = row[1, :]
    for come, go in zip(enter, leave):
        come.wait()
        go.start()
    for copy in leave:
        copy.wait()


def finish(dp, cols, scale, sums, vectors, moves):
    width = vectors.shape[1]
    vmem = pl.BlockSpec(memory_space=pltpu.VMEM)
    hbm = pl.BlockSpec(memory_space=pl.ANY)
    row = jax.ShapeDtypeStruct((width,), F32)
    like = [jax.ShapeDtypeStruct(v.shape, v.dtype) for v in moves]
    shapes = like[:2] + [row] + like[2:5] + [jax.ShapeDtypeStruct((HP,), F32)]
    shapes += [like[5], row, like[6], row, like[7], row]
    small = (2, 6, 8, 10, 12)
    return pl.pallas_call(
        lambda *refs: finish_kernel(dp, cols, *refs),
        out_shape=shapes,
        in_specs=[vmem] * 3 + [hbm] * 8,
        out_specs=[vmem if i in small else hbm for i in range(13)],
        scratch_shapes=[pltpu.VMEM(v.shape, v.dtype) for v in moves]
        + [pltpu.VMEM((8, width), F32), pltpu.SemaphoreType.DMA((16,))],
        compiler_params=pltpu.CompilerParams(vmem_limit_bytes=60 << 20),
    )(scale, sums, vectors, *moves)


def swap(v, axis, size, mask):
    return lax.ppermute(v, axis, [(i, i ^ mask) for i in range(size)])


def gather_dp(shard):
    return lax.all_gather(shard, "dp", axis=0, tiled=True)


def scatter_dp(grad, size):
    return lax.psum_scatter(grad, "dp", scatter_dimension=0, tiled=True)


def pad_heads(w):
    rows, cols = w.shape
    w = w.reshape(rows, cols // HD, HD)
    return jnp.pad(w, ((0, 0), (0, 0), (0, HP - HD))).reshape(rows, cols // HD * HP)


def trim_heads(w):
    rows, cols = w.shape
    return w.reshape(rows, cols // HP, HP)[:, :, :HD].reshape(rows, cols // HP * HD)


def body(dp, tensor, tokens, cotangent, block_ids, attn_gain, w_query, w_key, w_value,
         query_scale, w_out, mlp_gain, w_up, b_up, w_down, b_down):
    assert tensor == 4
    here = lax.axis_index("tensor")
    rows, width = tokens.shape
    length = rows * tensor
    cols = w_query.shape[1]
    heads = cols // HD
    order = [here, here ^ 2, here ^ 1, here ^ 3]

    softplus = jnp.log1p(jnp.exp(query_scale))
    factor = jnp.pad(SCORE_BASE / math.sqrt(HD) * softplus, (0, HP - HD))
    b_rel = jnp.concatenate([lax.dynamic_slice(b_up, (at * cols,), (cols,)) for at in order])
    repeat = jnp.pad(jnp.tile(factor, heads), (0, width - heads * HP))
    vectors = jnp.concatenate([attn_gain, mlp_gain, b_rel, b_down, repeat]).reshape(5, width)

    far = dp // 2 if dp == 8 else 0
    matrices = (w_query, w_key, w_value, w_out.T, w_up, w_down.T)
    if not far:
        pair = [jnp.concatenate([w, swap(w, "tensor", tensor, 2)], axis=1) for w in matrices[3:]]
        half = gather_dp(jnp.concatenate(pair, axis=1)).reshape(width, 3, 2 * cols)
        both = jnp.concatenate([half, swap(half, "tensor", tensor, 1)], axis=2)
        full = gather_dp(jnp.concatenate(matrices[:3], axis=1))
        first = jnp.stack([pad_heads(full[:, i * cols : (i + 1) * cols]) for i in range(3)])
        matrices = (first,) + matrices[1:]
    qkv, normed_t, padded, attended, lse, got, pairs, wide = front(
        dp, far, tokens, vectors, block_ids, cols, matrices
    )
    if not far:
        wide = both[:, 0]
        pairs = both[:, 1:].reshape(width, 2, 4, cols).transpose(2, 0, 1, 3)
        pairs = pairs.reshape(4, width, 2 * cols)

    output, d_hidden, received, xk, xg, pb, early = middle(
        tokens, cotangent, got.reshape(4 * cols, rows), vectors, wide, pairs
    )
    depth = width // dp
    if far:
        xk, xg, pb = (v.reshape(far, 2, depth, 2 * cols) for v in (xk, xg, pb))
    d_tokens, s_q, s_k, s_v, s_out, s_up, s_down, sums = backward(
        dp, far, attended, lse, received, vectors, block_ids, xk, early,
        qkv, xg, pb, tokens, d_hidden, normed_t, padded,
    )
    slope = jax.nn.sigmoid(query_scale) / softplus
    if far:
        scale = jnp.pad(slope, (0, HP - HD))[None, :]
        final = list(
            finish(
                dp, cols, scale, sums, vectors,
                (output, d_tokens, s_q, s_k, s_v, s_out, s_up, s_down),
            )
        )
        final[6] = final[6][:HD]
        final[7], final[11] = final[7].T, final[11].T
        return tuple(final)
    else:
        dots = lax.psum(jnp.sum(s_q * padded.astype(F32), axis=(0, 2)), ("dp", "tensor"))
        sums = lax.psum(sums, ("dp", "tensor"))
        s_qkv = scatter_dp(jnp.concatenate([trim_heads(g) for g in s_q], axis=1), dp)
        s_q, s_k, s_v = (s_qkv[:, i * cols : (i + 1) * cols] for i in range(3))
        both = xk.astype(F32) + swap(xg, "tensor", tensor, 2).astype(F32)
        both = scatter_dp(both, dp)
        s_up, s_down = both[:, :cols], both[:, cols:].T
        both = scatter_dp(pb.astype(F32), dp)
        s_out = (both[:, :cols] + swap(both[:, cols:], "tensor", tensor, 2)).T
    d_scale = sums[6, :HD] * slope
    return (
        output,
        d_tokens,
        dots / attn_gain,
        s_q,
        s_k,
        s_v,
        d_scale,
        s_out,
        sums[0],
        s_up,
        sums[2:6, :cols].reshape(4 * cols),
        s_down,
        sums[1],
    )


def solution(mesh):
    weight, turned, whole = P("dp", "tensor"), P("tensor", "dp"), P()
    positions = P(("dp", "tensor"), None)
    return jax.shard_map(
        lambda *args: body(mesh.shape["dp"], mesh.shape["tensor"], *args),
        mesh=mesh,
        in_specs=(positions, positions, P("dp", None), whole, weight, weight, weight, whole,
                  turned, whole, weight, whole, turned, whole),
        out_specs=(positions, positions, whole, weight, weight, weight, whole, turned, whole,
                   weight, whole, turned, whole),
        check_vma=False,
    )
```

```python
import math

import jax
import jax.numpy as jnp
from jax import lax
from jax.experimental import pallas as pl
from jax.experimental.pallas import tpu as pltpu
from jax.sharding import PartitionSpec as P

HD = 80
HP = 128
TILE = 256
BLOCK_MOST = 256
EPSILON = 1e-06
SCORE_BASE = 1.442695041
MASKED = -1e30
BF = jnp.bfloat16
F32 = jnp.float32


def mm(a, b, ca, cb):
    return lax.dot_general(a, b, (((ca,), (cb,)), ((), ())), preferred_element_type=F32)


def reach(tile, length):
    return min((tile + 1) * TILE + BLOCK_MOST, length)


MESH = pl.DeviceIdType.MESH
PARTNERS = (2, 1, 3)
SLOT = {0: 0, 2: 1, 1: 2, 3: 3}


def remote(src, dst, send, recv, where):
    return pltpu.make_async_remote_copy(
        src_ref=src, dst_ref=dst, send_sem=send, recv_sem=recv, device_id=where, device_id_type=MESH
    )


def greet(peers):
    barrier = pltpu.get_barrier_semaphore()
    for where in peers:
        pl.semaphore_signal(barrier, inc=1, device_id=where, device_id_type=MESH)
    pl.semaphore_wait(barrier, len(peers))


def front_kernel(
    dp, far, tok_ref, vec_ref, idr_ref, wq_ref, wk_ref, wv_ref, wo_ref, wu_ref, wd_ref,
    qkv_out, normt_out, wpad_out, att_out, lse_ref, got_out, both_out, wide_out,
    norm, normt, wpad, qkv, att, got, vt_ref, idc_ref, fac, w1_ref, w2_ref, z1, y1, x2, pair,
    sx, rx, sc, rc, sf, rf, sz1, rz1, sy1, ry1, sx2, rx2, sz2, rz2, sy2, ry2, sc2, rc2,
    sx3, rx3, sc3, rc3, st_, rt_, so,
):
    here, me = lax.axis_index("tensor"), lax.axis_index("dp")
    rows, width = tok_ref.shape
    length = norm.shape[0]
    tiles = length // TILE
    heads = qkv.shape[2] // HP
    cols = heads * HD
    depth = width // dp
    packed = depth // 2
    fused = far > 0
    major, minor = me // 2, me % 2

    def at(mask):
        return (me, here ^ mask)

    def xor(mask):
        return here ^ mask

    across = (me ^ 1, here)

    def along(step):
        return (lax.rem(major + step, far) * 2 + minor, here)

    def source(step):
        return lax.rem(major + far - step, far)

    peers = [at(mask) for mask in PARTNERS]
    if fused:
        peers += [across] + [along(step) for step in range(1, far)]
    greet(peers)

    def z_first(w, step):
        return remote(
            w1_ref.at[w], z1.at[step, w], sz1.at[step, w], rz1.at[step, w], along(step)
        )

    def y_first(w, step):
        src = w1_ref.at[w] if isinstance(step, int) and step == 0 else z1.at[step, w]
        return remote(src, y1.at[step, w], sy1.at[step, w], ry1.at[step, w], across)

    swap_two = remote(w2_ref, x2, sx2, rx2, at(2)) if fused else None
    if fused:
        for w, ref in enumerate((wq_ref, wk_ref, wv_ref)):
            w1_ref[w, :, :cols] = ref[:packed, :]
            w1_ref[w, :, cols:] = ref[packed:, :]
            for step in range(1, far):
                z_first(w, step).start()
            y_first(w, 0).start()
        pair[0, :, :cols] = wu_ref[...]
        pair[0, :, cols:] = wd_ref[...]
        pair[1, :, :cols] = wo_ref[...]
        w2_ref[:, :cols] = wo_ref[:packed, :]
        w2_ref[:, cols:] = wo_ref[packed:, :]
        swap_two.start()

    chunk = TILE
    count = rows // chunk

    @pl.loop(0, count)
    def _(c):
        low = pl.multiple_of(c * chunk, chunk)
        v = tok_ref[pl.ds(low, chunk), :].astype(F32)
        hat = v * lax.rsqrt(jnp.mean(v * v, axis=-1, keepdims=True) + EPSILON)
        norm[pl.ds(pl.multiple_of(here * rows + low, chunk), chunk), :] = (
            hat * vec_ref[0:1, :]
        ).astype(BF)

    def rows_of(mask, c):
        return norm.at[pl.ds(pl.multiple_of((here ^ mask) * rows + c * chunk, chunk), chunk), :]

    def send_x(c):
        return remote(rows_of(0, c), rows_of(0, c), sx.at[c], rx.at[c], at(2))

    def send_c(c):
        return remote(rows_of(0, c), rows_of(0, c), sc.at[c], rc.at[c], at(1))

    def forward(c):
        return remote(rows_of(2, c), rows_of(2, c), sf.at[c], rf.at[c], at(1))

    for c in range(count):
        send_x(c).start()
        send_c(c).start()
    idc_ref[...] = jnp.broadcast_to(idr_ref[...].astype(F32), (HP, length)).T.astype(jnp.int32)
    fac[...] = jnp.ones_like(fac)
    fac[0:1, :] = vec_ref[4:5, : heads * HP]

    def project(w, mask, c):
        low = pl.multiple_of(xor(mask) * rows + c * chunk, chunk)
        x = norm[pl.ds(low, chunk), :]
        y = mm(x, wpad[w], 1, 0)
        qkv[w, pl.ds(low, chunk), :] = (y * fac[pl.ds(w, 1), :]).astype(BF)

        @pl.when(w == 2)
        def _():
            normt[:, pl.ds(low, chunk)] = x.astype(F32).T.astype(BF)

    def rows_two(index):
        return pl.ds(pl.multiple_of(index * depth, 16), depth)

    def index_of(step, side):
        return source(step) * 2 + (minor if side == 0 else 1 - minor)

    def block_two(p, index):
        if p == 0:
            return both_out.at[0, rows_two(index), :]
        return wide_out.at[rows_two(index), pl.ds(0, 2 * cols)]

    def held_two(p, step, side):
        return pair.at[p] if step == 0 and side == 0 else block_two(p, index_of(step, side))

    def z_second(p, step):
        return remote(
            pair.at[p], block_two(p, me), sz2.at[p, step], rz2.at[p, step], along(step)
        )

    def y_second(p, step):
        return remote(
            held_two(p, step, 0), block_two(p, index_of(step, 0)),
            sy2.at[p, step], ry2.at[p, step], across,
        )

    def c_second(p, step, side):
        index = index_of(step, side)
        if p == 0:
            dst = both_out.at[2, rows_two(index), :]
        else:
            dst = wide_out.at[rows_two(index), pl.ds(2 * cols, 2 * cols)]
        return remote(
            held_two(p, step, side), dst, sc2.at[p, step, side], rc2.at[p, step, side], at(1)
        )

    def x_second(step, side):
        return remote(
            held_two(0, step, side), both_out.at[1, rows_two(index_of(step, side)), :],
            sx3.at[step, side], rx3.at[step, side], at(2),
        )

    def c_third(step, side):
        spot = rows_two(index_of(step, side))
        return remote(
            both_out.at[1, spot, :], both_out.at[3, spot, :],
            sc3.at[step, side], rc3.at[step, side], at(1),
        )

    def own_two(p):
        return pltpu.make_async_copy(pair.at[p], block_two(p, me), so.at[8 + p])

    def start_second(p):
        for step in range(1, far):
            z_second(p, step).start()
        y_second(p, 0).start()
        own_two(p).start()

    def spread(p, step, side):
        c_second(p, step, side).start()
        if p == 0:
            x_second(step, side).start()

    def after_z(p):
        for step in range(1, far):
            z_second(p, step).wait_recv()
            y_second(p, step).start()
            spread(p, step, 0)

    def after_y(p, step):
        y_second(p, step).wait_recv()
        spread(p, step, 1)

    if fused:
        start_second(0)
        spread(0, 0, 0)
        swap_two.wait_recv()
        for part in range(2):
            pair[1, part * packed : (part + 1) * packed, cols:] = x2[
                :, part * cols : (part + 1) * cols
            ]
        start_second(1)
        spread(1, 0, 0)

    if not fused:
        wpad[...] = wq_ref[...]
        for c in range(count):
            send_c(c).wait_recv()

        @pl.loop(0, 3)
        def _(w):
            @pl.loop(0, 2 * count)
            def _(j):
                project(w, j // count, lax.rem(j, count))

    else:
        wpad[...] = jnp.zeros_like(wpad)

        def unpack(w, block, device):
            for part in range(2):
                low = pl.multiple_of(device * depth + part * packed, 16)
                for h in range(heads):
                    lane = part * cols + h * HD
                    wpad[w, pl.ds(low, packed), h * HP : h * HP + HD] = block[:, lane : lane + HD]

        @pl.loop(0, 3)
        def _(w):
            unpack(w, w1_ref[w], me)

            @pl.loop(1, far)
            def _(step):
                z_first(w, step).wait_recv()
                y_first(w, step).start()
                unpack(w, z1[step, w], source(step) * 2 + minor)

            @pl.loop(0, far)
            def _(step):
                y_first(w, step).wait_recv()
                unpack(w, y1[step, w], source(step) * 2 + 1 - minor)

            @pl.when(w == 0)
            def _():
                for c in range(count):
                    send_c(c).wait_recv()

            @pl.loop(0, 2 * count)
            def _(j):
                project(w, j // count, lax.rem(j, count))

            @pl.when(w == 1)
            def _():
                after_y(0, 0)

        after_z(0)

    @pl.loop(0, count)
    def _(c):
        send_x(c).wait_recv()
        forward(c).start()

        @pl.loop(0, 3)
        def _(w):
            project(w, 2, c)

    @pl.loop(0, count)
    def _(c):
        forward(c).wait_recv()

        @pl.loop(0, 3)
        def _(w):
            project(w, 3, c)

    keep = [
        pltpu.make_async_copy(normt, normt_out, so.at[0]),
        pltpu.make_async_copy(wpad, wpad_out, so.at[1]),
        pltpu.make_async_copy(qkv, qkv_out, so.at[2]),
    ]
    for copy in keep:
        copy.start()

    def trade(h, mask):
        spot = pl.ds(pl.multiple_of((here ^ mask) * rows, HP), rows)
        return remote(
            att.at[h, :, spot], got.at[SLOT[mask], h], st_.at[mask, h], rt_.at[mask, h], at(mask)
        )

    sub = lax.broadcasted_iota(jnp.int32, (HP, length), 0)

    @pl.loop(0, heads)
    def _(h):
        lanes = pl.ds(pl.multiple_of(h * HP, HP), HP)
        vt_ref[...] = jnp.where(sub == HD, 1.0, qkv[2, :, lanes].astype(F32).T).astype(BF)

        def scores(t):
            seen, low = reach(t, length), t * TILE
            st = mm(qkv[1, :seen, lanes], qkv[0, low : low + TILE, lanes], 1, 1)
            visible = idc_ref[low:seen, 0:1] <= idr_ref[:, low : low + TILE]
            masked = jnp.where(visible, st[low:], MASKED)
            return jnp.concatenate([st[:low], masked], 0) if low else masked

        st = scores(0)
        for t in range(tiles):
            later = scores(t + 1) if t + 1 < tiles else None
            seen, low = st.shape[0], t * TILE
            group = jnp.max(st.reshape(seen // 64, 64, TILE), axis=0)
            highest = jnp.max(group, axis=0, keepdims=True)
            weights = jnp.exp(st - highest).astype(BF)
            ot = mm(vt_ref[:, :seen], weights, 1, 0)
            summed = ot[HD : HD + 1, :]
            att[h, :, low : low + TILE] = (ot[:HD] * (1.0 / summed)).astype(BF)
            lse_ref[h, :, low : low + TILE] = highest + jnp.log(summed)
            st = later
        for mask in PARTNERS:
            trade(h, mask).start()
        if fused:
            for n in range(heads):

                @pl.when(h == n)
                def _(n=n):
                    if n == 0:
                        after_y(0, 1)
                    if n == 1:
                        after_y(0, 2)
                        after_y(0, 3)
                    if n == 2:
                        after_z(1)
                        after_y(1, 0)

    got[0] = att[:, :, pl.ds(pl.multiple_of(here * rows, HP), rows)]
    keep.append(pltpu.make_async_copy(att, att_out, so.at[5]))
    keep[-1].start()
    if fused:
        for step in range(far):
            x_second(step, 0).wait_recv()
            c_third(step, 0).start()
        for step in range(1, far):
            after_y(1, step)
        for step in range(far):
            x_second(step, 1).wait_recv()
            c_third(step, 1).start()
    for h in range(heads):
        for mask in PARTNERS:
            trade(h, mask).wait_recv()
    keep.append(pltpu.make_async_copy(got, got_out, so.at[6]))
    keep[-1].start()

    for c in range(count):
        send_x(c).wait_send()
        send_c(c).wait_send()
        forward(c).wait_send()
    for h in range(heads):
        for mask in PARTNERS:
            trade(h, mask).wait_send()
    if fused:
        swap_two.wait_send()
        for w in range(3):
            for step in range(far):
                if step:
                    z_first(w, step).wait_send()
                y_first(w, step).wait_send()
        for p in range(2):
            own_two(p).wait()
            for step in range(far):
                if step:
                    z_second(p, step).wait_send()
                y_second(p, step).wait_send()
                for side in range(2):
                    c_second(p, step, side).wait()
                    if p == 0:
                        x_second(step, side).wait_send()
                        c_third(step, side).wait()
    for copy in keep:
        copy.wait()


def front(dp, far, tokens, vectors, idr, cols, matrices):
    rows, width = tokens.shape
    length = idr.shape[1]
    heads = cols // HD
    wide = heads * HP
    packed = width // dp // 2
    count = rows // TILE
    vmem = pl.BlockSpec(memory_space=pltpu.VMEM)
    hbm = pl.BlockSpec(memory_space=pl.ANY)
    sem = pltpu.SemaphoreType.DMA
    far_n = max(far, 1)
    fused = far > 0
    small = (packed, 2 * cols) if fused else (16, 128)
    return pl.pallas_call(
        lambda *refs: front_kernel(dp, far, *refs),
        out_shape=[
            jax.ShapeDtypeStruct((3, length, wide), BF),
            jax.ShapeDtypeStruct((width, length), BF),
            jax.ShapeDtypeStruct((3, width, wide), BF),
            jax.ShapeDtypeStruct((heads, HD, length), BF),
            jax.ShapeDtypeStruct((heads, 1, length), F32),
            jax.ShapeDtypeStruct((4, heads, HD, rows), BF),
            jax.ShapeDtypeStruct((4, width, 2 * cols) if fused else (16, 128), BF),
            jax.ShapeDtypeStruct((width, 4 * cols) if fused else (16, 128), BF),
        ],
        in_specs=[vmem] * 9,
        out_specs=[hbm] * 4 + [vmem] + [hbm] * 3,
        scratch_shapes=[
            pltpu.VMEM((length, width), BF),
            pltpu.VMEM((width, length), BF),
            pltpu.VMEM((3, width, wide), BF),
            pltpu.VMEM((3, length, wide), BF),
            pltpu.VMEM((heads, HD, length), BF),
            pltpu.VMEM((4, heads, HD, rows), BF),
            pltpu.VMEM((HP, length), BF),
            pltpu.VMEM((length, HP), jnp.int32),
            pltpu.VMEM((8, wide), F32),
            pltpu.VMEM((3,) + small, BF),
            pltpu.VMEM(small, BF),
            pltpu.VMEM((far_n, 3) + small, BF),
            pltpu.VMEM((far_n, 3) + small, BF),
            pltpu.VMEM(small, BF),
            pltpu.VMEM((2, 2 * packed, 2 * cols) if fused else (2, 16, 128), BF),
            sem((count,)), sem((count,)), sem((count,)), sem((count,)), sem((count,)), sem((count,)),
            sem((far_n, 3)), sem((far_n, 3)), sem((far_n, 3)), sem((far_n, 3)),
            sem, sem,
            sem((2, far_n)), sem((2, far_n)), sem((2, far_n)), sem((2, far_n)),
            sem((2, far_n, 2)), sem((2, far_n, 2)),
            sem((far_n, 2)), sem((far_n, 2)), sem((far_n, 2)), sem((far_n, 2)),
            sem((4, heads)), sem((4, heads)),
            sem((12,)),
        ],
        compiler_params=pltpu.CompilerParams(
            vmem_limit_bytes=60 << 20, collective_id=1, has_side_effects=True
        ),
    )(tokens, vectors, idr, *matrices)


def mid_kernel(
    tok_ref, cot_ref, got_ref, vec_ref, wide_ref, both_ref,
    out_ref, dhid_ref, drec_out, xk_out, xg_out, pb_out, early_ref,
    w, both, att, n2, act, dpre, branch, hid, give, grec, db, drec, kept, bs,
    ss, rs, sg, rg, so,
):
    here, me = lax.axis_index("tensor"), lax.axis_index("dp")
    rows, width = tok_ref.shape
    wide = w.shape[1]
    cols = wide // 4
    pair = 2 * cols
    chunk = TILE
    half = chunk // 2
    count = rows // chunk

    def at(mask):
        return (me, here ^ mask)

    loads = [
        pltpu.make_async_copy(both_ref, both, so.at[1]),
        pltpu.make_async_copy(wide_ref, w.at[0], so.at[0]),
    ]
    for copy in loads:
        copy.start()
    greet([at(mask) for mask in PARTNERS])
    att[...] = got_ref[...].astype(F32).T.astype(BF)
    early_ref[...] = jnp.zeros_like(early_ref)
    bs[...] = jnp.zeros_like(bs)
    loads[0].wait()

    @pl.loop(0, width // chunk)
    def _(j):
        spot = pl.ds(pl.multiple_of(j * chunk, chunk), chunk)
        for i in range(4):
            w[1, spot, i * cols : (i + 1) * cols] = both[i, spot, :cols]
            w[2, spot, i * cols : (i + 1) * cols] = both[i, spot, cols:]

    loads[1].wait()

    def trade(c, mask):
        return remote(
            db.at[c, SLOT[mask]], drec.at[c, SLOT[mask]],
            ss.at[c, mask], rs.at[c, mask], at(mask),
        )

    @pl.loop(0, count)
    def _(c):
        low = pl.multiple_of(c * chunk, chunk)
        spot = pl.ds(low, chunk)
        hidden = tok_ref[spot, :].astype(F32) + mm(att[spot, :], w[0], 1, 1)
        hid[spot, :] = hidden
        cot = cot_ref[spot, :]
        d_act = mm(cot, w[2], 1, 0)
        inverse = lax.rsqrt(jnp.mean(hidden * hidden, axis=-1, keepdims=True) + EPSILON)
        hat = hidden * inverse
        normed = (hat * vec_ref[1:2, :]).astype(BF)
        n2[spot, :] = normed
        pre = mm(normed, w[1], 1, 0) + vec_ref[2:3, :]
        sig = jax.nn.sigmoid(pre)
        act[spot, :] = (pre * sig).astype(BF)
        d_pre = (d_act * sig * (1.0 + pre * (1.0 - sig))).astype(BF)
        dpre[spot, :] = d_pre
        d_n2 = mm(d_pre, w[1], 1, 1)
        scaled = d_n2 * vec_ref[1:2, :]
        cot_f32 = cot.astype(F32)
        d_hidden = cot_f32 + inverse * (
            scaled - hat * jnp.mean(scaled * hat, axis=-1, keepdims=True)
        )
        dhid_ref[spot, :] = d_hidden
        br = d_hidden.astype(BF)
        branch[spot, :] = br
        d_att = mm(br, w[0], 1, 0).astype(BF)
        for i in range(4):
            for part in range(2):
                db[c, i, :, part * cols : (part + 1) * cols] = d_att[
                    part * half : (part + 1) * half, i * cols : (i + 1) * cols
                ]
        for mask in PARTNERS:
            trade(c, mask).start()
        drec[c, 0] = db[c, 0]
        early_ref[0:1, :] += jnp.sum(d_n2 * hat, axis=0, keepdims=True)
        early_ref[1:2, :] += jnp.sum(cot_f32, axis=0, keepdims=True)
        bs[0:1, :] += jnp.sum(d_pre.astype(F32), axis=0, keepdims=True)

    pieces = ((branch, att), (n2, dpre), (cot_ref, act))

    def hand(i):
        return remote(give.at[i], grec.at[i], sg.at[i], rg.at[i], at(1))

    for i in range(3):

        @pl.loop(0, width // chunk)
        def _(j):
            spot = pl.ds(pl.multiple_of(j * chunk, chunk), chunk)
            left, right = pieces[i]
            g = mm(left[:, spot], right[...], 0, 0).astype(BF)
            give[i, spot, :] = g[:, pair:]
            if i == 0:
                kept[2, spot, :] = g[:, :pair]
            else:
                lane = (i - 1) * cols
                kept[0, spot, lane : lane + cols] = g[:, :cols]
                kept[1, spot, lane : lane + cols] = g[:, cols:pair]

        hand(i).start()

    for i in range(4):
        place = here ^ (0, 2, 1, 3)[i]
        early_ref[pl.ds(2 + place, 1), 0:cols] = bs[0:1, i * cols : (i + 1) * cols]

    @pl.loop(0, count)
    def _(c):
        spot = pl.ds(pl.multiple_of(c * chunk, chunk), chunk)
        out_ref[spot, :] = (hid[spot, :] + mm(act[spot, :], w[2], 1, 1) + vec_ref[3:4, :]).astype(BF)

    for i in range(3):
        hand(i).wait_recv()

        @pl.loop(0, width // chunk)
        def _(j):
            spot = pl.ds(pl.multiple_of(j * chunk, chunk), chunk)
            came = grec[i, spot, :]
            if i == 0:
                kept[2, spot, :] += came
            else:
                lane = (i - 1) * cols
                kept[0, spot, lane : lane + cols] += came[:, :cols]
                kept[1, spot, lane : lane + cols] += came[:, cols:]

        if i == 0:
            keep = [pltpu.make_async_copy(kept.at[2], pb_out, so.at[3])]
            keep[0].start()
    keep.append(pltpu.make_async_copy(kept.at[0], xk_out, so.at[4]))
    keep.append(pltpu.make_async_copy(kept.at[1], xg_out, so.at[5]))
    for copy in keep[1:]:
        copy.start()
    for c in range(count):
        for mask in PARTNERS:
            trade(c, mask).wait_recv()
    keep.append(pltpu.make_async_copy(drec, drec_out, so.at[6]))
    keep[-1].start()
    for c in range(count):
        for mask in PARTNERS:
            trade(c, mask).wait_send()
    for i in range(3):
        hand(i).wait_send()
    for copy in keep:
        copy.wait()


def middle(tokens, cotangent, got, vectors, wide, both):
    rows, width = tokens.shape
    all_cols = wide.shape[1]
    cols = all_cols // 4
    count = rows // TILE
    vmem = pl.BlockSpec(memory_space=pltpu.VMEM)
    hbm = pl.BlockSpec(memory_space=pl.ANY)
    sem = pltpu.SemaphoreType.DMA
    blocks = (count, 4, TILE // 2, 2 * cols)
    halves = jax.ShapeDtypeStruct((width, 2 * cols), BF)
    return pl.pallas_call(
        mid_kernel,
        out_shape=[
            jax.ShapeDtypeStruct((rows, width), BF),
            jax.ShapeDtypeStruct((rows, width), F32),
            jax.ShapeDtypeStruct(blocks, BF),
            halves,
            halves,
            halves,
            jax.ShapeDtypeStruct((16, width), F32),
        ],
        in_specs=[vmem] * 4 + [hbm] * 2,
        out_specs=[vmem, vmem, hbm, hbm, hbm, hbm, vmem],
        scratch_shapes=[
            pltpu.VMEM((3, width, all_cols), BF),
            pltpu.VMEM((4, width, 2 * cols), BF),
            pltpu.VMEM((rows, all_cols), BF),
            pltpu.VMEM((rows, width), BF),
            pltpu.VMEM((rows, all_cols), BF),
            pltpu.VMEM((rows, all_cols), BF),
            pltpu.VMEM((rows, width), BF),
            pltpu.VMEM((rows, width), F32),
            pltpu.VMEM((3, width, 2 * cols), BF),
            pltpu.VMEM((3, width, 2 * cols), BF),
            pltpu.VMEM(blocks, BF),
            pltpu.VMEM(blocks, BF),
            pltpu.VMEM((3, width, 2 * cols), BF),
            pltpu.VMEM((8, all_cols), F32),
            sem((count, 4)), sem((count, 4)), sem((3,)), sem((3,)), sem((8,)),
        ],
        compiler_params=pltpu.CompilerParams(
            vmem_limit_bytes=60 << 20, collective_id=2, has_side_effects=True
        ),
    )(tokens, cotangent, got, vectors, wide, both)


def back_kernel(
    dp, far, o_ref, lse_ref, drec_ref, vec_ref, idr_ref, xk_ref, early_ref,
    qkv_hbm, xg_ref, pb_ref, tok_hbm, dhid_hbm, normt_hbm, wpad_hbm,
    dtok_ref, dq_out, dk_out, dv_out, dout_ref, dup_ref, ddown_ref, sums_ref,
    do, dka, dva, kt_ref, idc_ref, dqkv, tok, dhid, normt, wpad,
    xrec, pbown, yrec, zrec, last, lastsend, lastrec,
    gpay, gyrec, gzrec, ownsum, near, fo, crec, fs, frec, nrec, qsum, lvec, ar, arec, aorder, er, erec, eorder,
    so, sxa, rxa, sy, ry, sz, rz, sl, rl, sgy, rgy, sgz, rgz, sfo, rfo, sfs, rfs, sno, rno, sar, rar, ser, rer,
):
    here, me = lax.axis_index("tensor"), lax.axis_index("dp")
    heads, _, length = o_ref.shape
    rows, width = tok.shape
    cols = heads * HD
    tiles = length // TILE
    depth = width // dp
    packed = depth // 2
    fused = far > 0
    major, minor = me // 2, me % 2
    chunk = TILE
    count = rows // chunk

    def at(mask):
        return (me, here ^ mask)

    across = (me ^ 1, here)

    def along(step):
        return (lax.rem(major + step, far) * 2 + minor, here)

    def target(step):
        return lax.rem(major + step, far)

    loads = [
        pltpu.make_async_copy(src, dst, so.at[i])
        for i, (src, dst) in enumerate(
            ((wpad_hbm, wpad), (normt_hbm, normt), (tok_hbm, tok), (dhid_hbm, dhid))
        )
    ]
    load_qkv = pltpu.make_async_copy(qkv_hbm, dqkv, so.at[4])
    load_qkv.start()
    if fused:
        load_pb = pltpu.make_async_copy(pb_ref.at[:, minor], pbown, so.at[5])
        load_pb.start()
    for copy in loads:
        copy.start()
    peers = [at(2), at(1)]
    if fused:
        peers += [across] + [along(step) for step in range(1, far)]
    greet(peers)

    turn = list(range(1, far)) + [0]

    def x_send(step):
        spot = target(step)
        return remote(xg_ref.at[spot], xrec.at[spot], sxa.at[step], rxa.at[step], at(2))

    def y_send(p, step):
        spot = target(step)
        src = xrec.at[spot, 1 - minor] if p == 0 else pb_ref.at[spot, 1 - minor]
        return remote(src, yrec.at[p, spot], sy.at[p, step], ry.at[p, step], across)

    def z_send(p, step):
        return remote(
            yrec.at[p, target(step)], zrec.at[p, step - 1],
            sz.at[p, step], rz.at[p, step], along(step),
        )

    def after_x(step):
        x_send(step).wait_recv()
        spot = target(step)
        xrec[spot] = xk_ref[spot] + xrec[spot]
        y_send(0, step).start()

    def after_y(p, step):
        y_send(p, step).wait_recv()
        spot = target(step)
        mine = xrec[spot, minor] if p == 0 else pbown[spot]

        @pl.when(step != 0)
        def _():
            yrec[p, spot] = mine + yrec[p, spot]
            z_send(p, step).start()

        @pl.when(step == 0)
        def _():
            last[p] = mine.astype(F32) + yrec[p, spot].astype(F32)

    def after_z(p):
        for step in range(1, far):
            z_send(p, step).wait_recv()
            last[p] += zrec[p, step - 1].astype(F32)

    def e_hop(n, where):
        return remote(er.at[n], erec.at[n], ser.at[n], rer.at[n], where)

    def e_last():
        return remote(er.at[3], erec.at[2], ser.at[2], rer.at[2], at(2))

    def e_z(step):
        return remote(er.at[2], erec.at[3 + step], ser.at[3 + step], rer.at[3 + step], along(step))

    def early_hop(h):
        @pl.when(h == 0)
        def _():
            e_hop(0, at(1)).wait_recv()
            er[1] = er[0] + erec[0]
            e_hop(1, across).start()

        @pl.when(h == 1)
        def _():
            e_hop(1, across).wait_recv()
            er[2] = er[1] + erec[1]
            for step in range(1, far):
                e_z(step).start()

        @pl.when(h == 2)
        def _():
            eorder[major] = er[2]
            for step in range(1, far):
                e_z(step).wait_recv()
                eorder[lax.rem(major + far - step, far)] = erec[3 + step]
            er[3] = (eorder[0] + eorder[1]) + (eorder[2] + eorder[3])
            e_last().start()

    if fused:
        er[0] = early_ref[0:8, :]
        e_hop(0, at(1)).start()
        for step in turn:
            x_send(step).start()
            y_send(1, step).start()

    do[...] = jnp.zeros_like(do)
    half = chunk // 2
    for c in range(count):
        for i, mask in enumerate((0, 2, 1, 3)):
            block = drec_ref[c, i]
            for part in range(2):
                low = pl.multiple_of((here ^ mask) * rows + c * chunk + part * half, half)
                for h in range(heads):
                    lane = part * cols + h * HD
                    do[h, pl.ds(low, half), 0:HD] = block[:, lane : lane + HD]
    qsum[...] = jnp.zeros_like(qsum)
    if fused:
        gpay[...] = jnp.zeros_like(gpay)
    idc_ref[...] = jnp.broadcast_to(idr_ref[...].astype(F32), (HP, length)).T.astype(jnp.int32)

    load_qkv.wait()
    if fused:
        load_pb.wait()

    def one_head(h):
        lanes = pl.ds(pl.multiple_of(h * HP, HP), HP)
        kt_ref[...] = dqkv[1, :, lanes].astype(F32).T.astype(BF)
        dka[...] = jnp.zeros_like(dka)
        dva[...] = jnp.zeros_like(dva)
        scale_sum = jnp.zeros((1, HP), F32)
        for t in range(tiles):
            seen, low = reach(t, length), t * TILE
            spot = slice(low, low + TILE)
            qt = dqkv[0, spot, lanes]
            dot_ = do[h, spot, :]
            delta = jnp.sum(
                dot_.astype(F32).T[:HD] * o_ref[h, :, spot].astype(F32), axis=0, keepdims=True
            )
            st = mm(dqkv[1, :seen, lanes], qt, 1, 1)
            p = jnp.exp(st - lse_ref[h, :, spot])
            visible = idc_ref[low:seen, 0:1] <= idr_ref[:, spot]
            pm = jnp.where(visible, p[low:], 0.0)
            p = jnp.concatenate([p[:low], pm], 0) if low else pm
            d_p = mm(dqkv[2, :seen, lanes], dot_, 1, 1)
            ds = (p * (d_p - delta)).astype(BF)
            dva[:seen, :] += mm(p.astype(BF), dot_, 1, 0)
            dka[:seen, :] += mm(ds, qt, 1, 0)
            dq = mm(kt_ref[:, :seen], ds, 1, 0).T
            scale_sum = scale_sum + jnp.sum(dq * qt.astype(F32), axis=0, keepdims=True)
            dqkv[0, spot, lanes] = (dq * vec_ref[4:5, :HP]).astype(BF)
        dqkv[1, :, lanes] = dka[...].astype(BF)
        dqkv[2, :, lanes] = dva[...].astype(BF)
        qsum[0:1, :] += scale_sum

    group = 2 * HD

    def weight_blocks(n, step):
        spot = target(step)
        low = pl.multiple_of(spot * 2 * depth, 16)
        lanes = slice(n * 2 * HP, (n + 1) * 2 * HP)
        dots = jnp.zeros((2 * depth, 1), F32)
        for i in range(3):
            g = mm(normt[pl.ds(low, 2 * depth), :], dqkv[i, :, lanes], 1, 0)
            dots = dots + jnp.sum(
                g * wpad[i, pl.ds(low, 2 * depth), lanes].astype(F32), axis=1, keepdims=True
            )
            g = g.astype(BF)
            for side in range(2):
                for h in range(2):
                    lane = i * group + h * HD
                    gpay[n, spot, side, :, lane : lane + HD] = g[
                        side * depth : (side + 1) * depth, h * HP : h * HP + HD
                    ]
        flat = jnp.broadcast_to(dots, (2 * depth, HP)).T[0:1, :]
        lvec[n, pl.ds(spot * 2, 1), :] = flat[:, :depth]
        lvec[n, pl.ds(spot * 2 + 1, 1), :] = flat[:, depth:]

    def gy_send(n, step):
        spot = target(step)
        return remote(
            gpay.at[n, spot, 1 - minor], gyrec.at[n, spot], sgy.at[n, step], rgy.at[n, step], across
        )

    def gz_send(n, step):
        return remote(
            gyrec.at[n, target(step)], gzrec.at[n, step - 1],
            sgz.at[n, step], rgz.at[n, step], along(step),
        )

    def weight_pair(n):
        @pl.loop(0, far)
        def _(j):
            step = lax.rem(j + 1, far)
            weight_blocks(n, step)
            gy_send(n, step).start()

    def gz_start(n, step):
        gy_send(n, step).wait_recv()
        spot = target(step)
        mine = gpay[n, spot, minor]

        @pl.when(step != 0)
        def _():
            gyrec[n, spot] = mine + gyrec[n, spot]
            gz_send(n, step).start()

        @pl.when(step == 0)
        def _():
            ownsum[n] = mine.astype(F32) + gyrec[n, spot].astype(F32)

    @pl.loop(0, heads)
    def _(h):
        one_head(h)
        if fused:
            early_hop(h)
            after_x(lax.rem(h + 1, far))

            @pl.when(h < 2)
            def _():
                @pl.loop(0, 2)
                def _(k):
                    after_y(1, lax.rem(2 * h + k + 1, far))

            @pl.when(h == 1)
            def _():
                for copy in loads[:2]:
                    copy.wait()
                weight_pair(0)

            @pl.when(h > 0)
            def _():
                after_y(0, h)

    if not fused:
        for copy in loads[:2]:
            copy.wait()

    def part(mask, c):
        spot = pl.ds(pl.multiple_of((here ^ mask) * rows + c * chunk, chunk), chunk)
        total = mm(dqkv[0, spot, :], wpad[0], 1, 1)
        total = total + mm(dqkv[1, spot, :], wpad[1], 1, 1)
        return total + mm(dqkv[2, spot, :], wpad[2], 1, 1)

    def c_far(c):
        return remote(fo.at[c], crec.at[c], sfo.at[c], rfo.at[c], at(1))

    def x_far(c):
        return remote(fs.at[c], frec.at[c], sfs.at[c], rfs.at[c], at(2))

    def c_near(c):
        return remote(fo.at[c], nrec.at[c], sno.at[c], rno.at[c], at(1))

    def far_chunk(c):
        fo[c] = part(3, c).astype(BF)
        c_far(c).start()

    def far_sum(c):
        own = part(2, c)
        c_far(c).wait_recv()
        fs[c] = (own + crec[c].astype(F32)).astype(BF)

    def hop(n, where):
        return remote(ar.at[n], arec.at[n], sar.at[n], rar.at[n], where)

    def z_hop(step):
        return remote(ar.at[3], arec.at[3 + step], sar.at[3 + step], rar.at[3 + step], along(step))

    if fused:
        far_chunk(0)
        far_sum(0)
        x_far(0).start()

        @pl.loop(0, far)
        def _(j):
            gz_start(0, lax.rem(j + 1, far))

        after_y(0, turn[far - 1])
        weight_pair(1)
        for index in range(dp):
            spot = slice(index * depth, (index + 1) * depth)
            ar[0, :, spot] = lvec[0, index : index + 1, :] + lvec[1, index : index + 1, :]
        ar[0, :, width:] = qsum[0:1, :]
        hop(0, at(1)).start()
        for c in range(1, count):
            far_chunk(c)

        @pl.loop(1, 3)
        def _(step):
            gz_start(1, step)

        hop(0, at(1)).wait_recv()
        ar[1] = ar[0] + arec[0]
        hop(1, at(2)).start()
        for c in range(1, count):
            far_sum(c)
            x_far(c).start()
        after_z(1)
        for piece in range(2):
            last_half = last[1, piece * packed : (piece + 1) * packed, cols:]
            lastsend[:, piece * cols : (piece + 1) * cols] = last_half.astype(BF)
        cross = remote(lastsend, lastrec, sl, rl, at(2))
        cross.start()
    else:
        for c in range(count):
            far_chunk(c)
            far_sum(c)
            x_far(c).start()

        @pl.loop(0, 3)
        def _(i):
            for j in range(width // chunk):
                dq_out[i, j * chunk : (j + 1) * chunk, :] = mm(
                    normt[j * chunk : (j + 1) * chunk, :], dqkv[i], 1, 0
                )

    if not fused:
        sums_ref[...] = jnp.zeros_like(sums_ref)
        sums_ref[0:6, :] = early_ref[0:6, :]
        sums_ref[6:7, 0:HP] = qsum[0:1, :]

    @pl.loop(0, count)
    def _(c):
        c_far(c).wait_send()
        fo[c] = part(1, c).astype(BF)
        c_near(c).start()

    if fused:

        @pl.loop(0, 2)
        def _(j):
            gz_start(1, lax.rem(j + 3, far))

        hop(1, at(2)).wait_recv()
        ar[2] = ar[1] + arec[1]
        hop(2, across).start()
        after_z(0)
        dup_ref[...] = last[0, :, :cols]
        ddown_ref[...] = last[0, :, cols:]
    for copy in loads[2:]:
        copy.wait()

    @pl.loop(0, count)
    def _(c):
        near[c] = part(0, c)

    if fused:
        hop(2, across).wait_recv()
        ar[3] = ar[2] + arec[2]
        for step in range(1, far):
            z_hop(step).start()
        cross.wait_recv()
        arrived = jnp.concatenate([lastrec[:, :cols], lastrec[:, cols:]], axis=0)
        dout_ref[...] = last[1, :, :cols] + arrived.astype(F32)

    @pl.loop(0, count)
    def _(c):
        c_near(c).wait_recv()
        x_far(c).wait_recv()
        d_normed = near[c] + nrec[c].astype(F32) + frec[c].astype(F32)
        spot = pl.ds(pl.multiple_of(c * chunk, chunk), chunk)
        v = tok[spot, :].astype(F32)
        inverse = lax.rsqrt(jnp.mean(v * v, axis=-1, keepdims=True) + EPSILON)
        hat = v * inverse
        scaled = d_normed * vec_ref[0:1, :]
        dtok_ref[spot, :] = (
            dhid[spot, :]
            + inverse * (scaled - hat * jnp.mean(scaled * hat, axis=-1, keepdims=True))
        ).astype(BF)

    if fused:
        for n in range(2):
            for step in range(1, far):
                gz_send(n, step).wait_recv()
                ownsum[n] += gzrec[n, step - 1].astype(F32)
            for i, ref in enumerate((dq_out, dk_out, dv_out)):
                ref[:, n * group : (n + 1) * group] = ownsum[n, :, i * group : (i + 1) * group]
        aorder[major] = ar[3]
        for step in range(1, far):
            z_hop(step).wait_recv()
            aorder[lax.rem(major + far - step, far)] = arec[3 + step]
        total = (aorder[0] + aorder[1]) + (aorder[2] + aorder[3])
        e_last().wait_recv()
        sums_ref[...] = jnp.zeros_like(sums_ref)
        sums_ref[0:8, :] = er[3] + erec[2]
        sums_ref[6:7, 0:HP] = total[:, width:]
        sums_ref[7:8, :] = total[:, :width]
    else:
        dk_out[...] = jnp.zeros_like(dk_out)
        dv_out[...] = jnp.zeros_like(dv_out)
        dout_ref[...] = jnp.zeros_like(dout_ref)
        dup_ref[...] = jnp.zeros_like(dup_ref)
        ddown_ref[...] = jnp.zeros_like(ddown_ref)

    for c in range(count):
        x_far(c).wait_send()
        c_near(c).wait_send()
    if fused:
        for step in range(far):
            x_send(step).wait_send()
            for p in range(2):
                gy_send(p, step).wait_send()
                y_send(p, step).wait_send()
            if step:
                gz_send(0, step).wait_send()
                gz_send(1, step).wait_send()
                z_hop(step).wait_send()
                e_z(step).wait_send()
                for p in range(2):
                    z_send(p, step).wait_send()
        cross.wait_send()
        hop(0, at(1)).wait_send()
        hop(1, at(2)).wait_send()
        hop(2, across).wait_send()
        e_hop(0, at(1)).wait_send()
        e_hop(1, across).wait_send()
        e_last().wait_send()


def backward(dp, far, o, lse, drec, vectors, idr, xk, early, qkv, xg, pb,
             tokens, d_hidden, normt, wpad):
    heads, _, length = o.shape
    rows, width = tokens.shape
    cols, wide = heads * HD, heads * HP
    depth = width // dp
    packed = depth // 2
    count = rows // TILE
    fused = far > 0
    far_n = max(far, 1)
    vmem = pl.BlockSpec(memory_space=pltpu.VMEM)
    hbm = pl.BlockSpec(memory_space=pl.ANY)
    sem = pltpu.SemaphoreType.DMA
    tiny = jax.ShapeDtypeStruct((8, 128), F32)
    shard = jax.ShapeDtypeStruct((depth, cols), F32) if fused else tiny
    whole = shard if fused else jax.ShapeDtypeStruct((3, width, wide), F32)

    def buf(*shape, dtype=BF, only=True):
        return pltpu.VMEM(shape if fused or not only else (8, 128), dtype)

    pair = 2 * cols
    return pl.pallas_call(
        lambda *refs: back_kernel(dp, far, *refs),
        out_shape=[jax.ShapeDtypeStruct((rows, width), BF), whole, shard, shard, shard, shard,
                   shard, jax.ShapeDtypeStruct((16, width), F32)],
        in_specs=[vmem] * 7 + [hbm] * 7,
        out_specs=[vmem] * 8,
        scratch_shapes=[
            buf(heads, length, HP, only=False),
            buf(length, HP, dtype=F32, only=False),
            buf(length, HP, dtype=F32, only=False),
            buf(HP, length, only=False),
            buf(length, HP, dtype=jnp.int32, only=False),
            buf(3, length, wide, only=False),
            buf(rows, width, only=False),
            buf(rows, width, dtype=F32, only=False),
            buf(width, length, only=False),
            buf(3, width, wide, only=False),
            buf(far_n, 2, depth, pair),
            buf(far_n, depth, pair),
            buf(2, far_n, depth, pair),
            buf(2, far_n - 1, depth, pair),
            buf(2, depth, pair, dtype=F32),
            buf(packed, pair),
            buf(packed, pair),
            buf(2, far_n, 2, depth, 4 * HP),
            buf(2, far_n, depth, 4 * HP),
            buf(2, far_n - 1, depth, 4 * HP),
            buf(2, depth, 4 * HP, dtype=F32),
            buf(count, TILE, width, dtype=F32, only=False),
            buf(count, TILE, width, only=False),
            buf(count, TILE, width, only=False),
            buf(count, TILE, width, only=False),
            buf(count, TILE, width, only=False),
            buf(count, TILE, width, only=False),
            buf(8, HP, dtype=F32, only=False),
            buf(2, dp, depth, dtype=F32),
            buf(4, 1, width + HP, dtype=F32),
            buf(3 + far_n, 1, width + HP, dtype=F32),
            buf(far_n, 1, width + HP, dtype=F32),
            buf(4, 8, width, dtype=F32),
            buf(3 + far_n, 8, width, dtype=F32),
            buf(far_n, 8, width, dtype=F32),
            sem((6,)),
            sem((far_n,)), sem((far_n,)),
            sem((2, far_n)), sem((2, far_n)), sem((2, far_n)), sem((2, far_n)),
            sem, sem,
            sem((2, far_n)), sem((2, far_n)), sem((2, far_n)), sem((2, far_n)),
            sem((count,)), sem((count,)), sem((count,)), sem((count,)), sem((count,)), sem((count,)),
            sem((3 + far_n,)), sem((3 + far_n,)), sem((3 + far_n,)), sem((3 + far_n,)),
        ],
        compiler_params=pltpu.CompilerParams(
            vmem_limit_bytes=62 << 20, collective_id=3, has_side_effects=True
        ),
    )(o, lse, drec, vectors, idr, xk, early, qkv, xg, pb,
      tokens, d_hidden, normt, wpad)


def finish_kernel(cols, sums_ref, vec_ref, *refs):
    moves, outs, held = refs[:8], refs[8:21], refs[21:29]
    row, sem = refs[29:]
    width = vec_ref.shape[1]
    places = (0, 1, 3, 4, 5, 7, 9, 11)
    enter = [pltpu.make_async_copy(moves[i], held[i], sem.at[i]) for i in range(8)]
    leave = [pltpu.make_async_copy(held[i], outs[places[i]], sem.at[8 + i]) for i in range(8)]
    for copy in enter:
        copy.start()
    outs[6][...] = sums_ref[6, 0:HP] * vec_ref[5, 0:HP]
    outs[8][...] = sums_ref[0, :]
    outs[12][...] = sums_ref[1, :]
    row[...] = jnp.zeros_like(row)
    for i in range(width // cols):
        row[0:1, i * cols : (i + 1) * cols] = sums_ref[2 + i : 3 + i, :cols]
    row[1:2, :] = sums_ref[7:8, :] / vec_ref[0:1, :]
    outs[10][...] = row[0, :]
    outs[2][...] = row[1, :]
    for come, go in zip(enter, leave):
        come.wait()
        go.start()
    for copy in leave:
        copy.wait()


def finish(cols, sums, vectors, moves):
    width = vectors.shape[1]
    vmem = pl.BlockSpec(memory_space=pltpu.VMEM)
    hbm = pl.BlockSpec(memory_space=pl.ANY)
    row = jax.ShapeDtypeStruct((width,), F32)
    like = [jax.ShapeDtypeStruct(v.shape, v.dtype) for v in moves]
    shapes = like[:2] + [row] + like[2:5] + [jax.ShapeDtypeStruct((HP,), F32)]
    shapes += [like[5], row, like[6], row, like[7], row]
    small = (2, 6, 8, 10, 12)
    return pl.pallas_call(
        lambda *refs: finish_kernel(cols, *refs),
        out_shape=shapes,
        in_specs=[vmem] * 2 + [hbm] * 8,
        out_specs=[vmem if i in small else hbm for i in range(13)],
        scratch_shapes=[pltpu.VMEM(v.shape, v.dtype) for v in moves]
        + [pltpu.VMEM((8, width), F32), pltpu.SemaphoreType.DMA((16,))],
        compiler_params=pltpu.CompilerParams(vmem_limit_bytes=60 << 20),
    )(sums, vectors, *moves)


def swap(v, axis, size, mask):
    return lax.ppermute(v, axis, [(i, i ^ mask) for i in range(size)])


def gather_dp(shard):
    return lax.all_gather(shard, "dp", axis=0, tiled=True)


def scatter_dp(grad, size):
    return lax.psum_scatter(grad, "dp", scatter_dimension=0, tiled=True)


def pad_heads(w):
    rows, cols = w.shape
    w = w.reshape(rows, cols // HD, HD)
    return jnp.pad(w, ((0, 0), (0, 0), (0, HP - HD))).reshape(rows, cols // HD * HP)


def trim_heads(w):
    rows, cols = w.shape
    return w.reshape(rows, cols // HP, HP)[:, :, :HD].reshape(rows, cols // HP * HD)


def body(dp, tensor, tokens, cotangent, block_ids, attn_gain, w_query, w_key, w_value,
         query_scale, w_out, mlp_gain, w_up, b_up, w_down, b_down):
    assert tensor == 4
    here = lax.axis_index("tensor")
    rows, width = tokens.shape
    length = rows * tensor
    cols = w_query.shape[1]
    heads = cols // HD
    order = [here, here ^ 2, here ^ 1, here ^ 3]

    softplus = jnp.log1p(jnp.exp(query_scale))
    factor = jnp.pad(SCORE_BASE / math.sqrt(HD) * softplus, (0, HP - HD))
    b_rel = jnp.concatenate([lax.dynamic_slice(b_up, (at * cols,), (cols,)) for at in order])
    repeat = jnp.pad(jnp.tile(factor, heads), (0, width - heads * HP))
    slope = jax.nn.sigmoid(query_scale) / softplus
    vectors = jnp.concatenate(
        [attn_gain, mlp_gain, b_rel, b_down, repeat, jnp.pad(slope, (0, width - HD))]
    ).reshape(6, width)

    far = dp // 2 if dp == 8 else 0
    matrices = (w_query, w_key, w_value, w_out.T, w_up, w_down.T)
    if not far:
        pair = [jnp.concatenate([w, swap(w, "tensor", tensor, 2)], axis=1) for w in matrices[3:]]
        half = gather_dp(jnp.concatenate(pair, axis=1)).reshape(width, 3, 2 * cols)
        both = jnp.concatenate([half, swap(half, "tensor", tensor, 1)], axis=2)
        full = gather_dp(jnp.concatenate(matrices[:3], axis=1))
        first = jnp.stack([pad_heads(full[:, i * cols : (i + 1) * cols]) for i in range(3)])
        matrices = (first,) + matrices[1:]
    qkv, normed_t, padded, attended, lse, got, pairs, wide = front(
        dp, far, tokens, vectors, block_ids, cols, matrices
    )
    if not far:
        wide = both[:, 0]
        pairs = both[:, 1:].reshape(width, 2, 4, cols).transpose(2, 0, 1, 3)
        pairs = pairs.reshape(4, width, 2 * cols)

    output, d_hidden, received, xk, xg, pb, early = middle(
        tokens, cotangent, got.reshape(4 * cols, rows), vectors, wide, pairs
    )
    depth = width // dp
    if far:
        xk, xg, pb = (v.reshape(far, 2, depth, 2 * cols) for v in (xk, xg, pb))
    d_tokens, s_q, s_k, s_v, s_out, s_up, s_down, sums = backward(
        dp, far, attended, lse, received, vectors, block_ids, xk, early,
        qkv, xg, pb, tokens, d_hidden, normed_t, padded,
    )
    if far:
        final = list(
            finish(
                cols, sums, vectors,
                (output, d_tokens, s_q, s_k, s_v, s_out, s_up, s_down),
            )
        )
        final[6] = final[6][:HD]
        final[7], final[11] = final[7].T, final[11].T
        return tuple(final)
    else:
        dots = lax.psum(jnp.sum(s_q * padded.astype(F32), axis=(0, 2)), ("dp", "tensor"))
        sums = lax.psum(sums, ("dp", "tensor"))
        s_qkv = scatter_dp(jnp.concatenate([trim_heads(g) for g in s_q], axis=1), dp)
        s_q, s_k, s_v = (s_qkv[:, i * cols : (i + 1) * cols] for i in range(3))
        both = xk.astype(F32) + swap(xg, "tensor", tensor, 2).astype(F32)
        both = scatter_dp(both, dp)
        s_up, s_down = both[:, :cols], both[:, cols:].T
        both = scatter_dp(pb.astype(F32), dp)
        s_out = (both[:, :cols] + swap(both[:, cols:], "tensor", tensor, 2)).T
    d_scale = sums[6, :HD] * slope
    return (
        output,
        d_tokens,
        dots / attn_gain,
        s_q,
        s_k,
        s_v,
        d_scale,
        s_out,
        sums[0],
        s_up,
        sums[2:6, :cols].reshape(4 * cols),
        s_down,
        sums[1],
    )


def solution(mesh):
    weight, turned, whole = P("dp", "tensor"), P("tensor", "dp"), P()
    positions = P(("dp", "tensor"), None)
    return jax.shard_map(
        lambda *args: body(mesh.shape["dp"], mesh.shape["tensor"], *args),
        mesh=mesh,
        in_specs=(positions, positions, P("dp", None), whole, weight, weight, weight, whole,
                  turned, whole, weight, whole, turned, whole),
        out_specs=(positions, positions, whole, weight, weight, weight, whole, turned, whole,
                   weight, whole, turned, whole),
        check_vma=False,
    )
```

```python
import math

import jax
import jax.numpy as jnp
from jax import lax
from jax.experimental import pallas as pl
from jax.experimental.pallas import tpu as pltpu
from jax.sharding import PartitionSpec as P

HD = 80
HP = 128
TILE = 256
BLOCK_MOST = 256
EPSILON = 1e-06
SCORE_BASE = 1.442695041
MASKED = -1e30
BF = jnp.bfloat16
F32 = jnp.float32


def mm(a, b, ca, cb):
    return lax.dot_general(a, b, (((ca,), (cb,)), ((), ())), preferred_element_type=F32)


def reach(tile, length):
    return min((tile + 1) * TILE + BLOCK_MOST, length)


MESH = pl.DeviceIdType.MESH
PARTNERS = (2, 1, 3)
SLOT = {0: 0, 2: 1, 1: 2, 3: 3}


def remote(src, dst, send, recv, where):
    return pltpu.make_async_remote_copy(
        src_ref=src, dst_ref=dst, send_sem=send, recv_sem=recv, device_id=where, device_id_type=MESH
    )


def greet(peers):
    barrier = pltpu.get_barrier_semaphore()
    for where in peers:
        pl.semaphore_signal(barrier, inc=1, device_id=where, device_id_type=MESH)
    pl.semaphore_wait(barrier, len(peers))


def front_kernel(
    dp, far, tok_ref, vec_ref, idr_ref, wq_ref, wk_ref, wv_ref, wo_ref, wu_ref, wd_ref,
    qkv_out, normt_out, wpad_out, att_out, lse_ref, got_out, both_out, wide_out,
    norm, normt, wpad, qkv, att, got, vt_ref, idc_ref, fac, w1_ref, w2_ref, z1, y1, x2, pair,
    sx, rx, sc, rc, sf, rf, sz1, rz1, sy1, ry1, sx2, rx2, sz2, rz2, sy2, ry2, sc2, rc2,
    sx3, rx3, sc3, rc3, st_, rt_, so,
):
    here, me = lax.axis_index("tensor"), lax.axis_index("dp")
    rows, width = tok_ref.shape
    length = norm.shape[0]
    tiles = length // TILE
    heads = qkv.shape[2] // HP
    cols = heads * HD
    depth = width // dp
    packed = depth // 2
    fused = far > 0
    major, minor = me // 2, me % 2

    def at(mask):
        return (me, here ^ mask)

    def xor(mask):
        return here ^ mask

    across = (me ^ 1, here)

    def along(step):
        return (lax.rem(major + step, far) * 2 + minor, here)

    def source(step):
        return lax.rem(major + far - step, far)

    peers = [at(mask) for mask in PARTNERS]
    if fused:
        peers += [across] + [along(step) for step in range(1, far)]
    greet(peers)

    def z_first(w, step):
        return remote(
            w1_ref.at[w], z1.at[step, w], sz1.at[step, w], rz1.at[step, w], along(step)
        )

    def y_first(w, step):
        src = w1_ref.at[w] if isinstance(step, int) and step == 0 else z1.at[step, w]
        return remote(src, y1.at[step, w], sy1.at[step, w], ry1.at[step, w], across)

    swap_two = remote(w2_ref, x2, sx2, rx2, at(2)) if fused else None
    if fused:
        for w, ref in enumerate((wq_ref, wk_ref, wv_ref)):
            w1_ref[w, :, :cols] = ref[:packed, :]
            w1_ref[w, :, cols:] = ref[packed:, :]
            for step in range(1, far):
                z_first(w, step).start()
            y_first(w, 0).start()
        pair[0, :, :cols] = wu_ref[...]
        pair[0, :, cols:] = wd_ref[...]
        pair[1, :, :cols] = wo_ref[...]
        w2_ref[:, :cols] = wo_ref[:packed, :]
        w2_ref[:, cols:] = wo_ref[packed:, :]
        swap_two.start()

    chunk = TILE
    count = rows // chunk

    @pl.loop(0, count)
    def _(c):
        low = pl.multiple_of(c * chunk, chunk)
        v = tok_ref[pl.ds(low, chunk), :].astype(F32)
        hat = v * lax.rsqrt(jnp.mean(v * v, axis=-1, keepdims=True) + EPSILON)
        norm[pl.ds(pl.multiple_of(here * rows + low, chunk), chunk), :] = (
            hat * vec_ref[0:1, :]
        ).astype(BF)

    def rows_of(mask, c):
        return norm.at[pl.ds(pl.multiple_of((here ^ mask) * rows + c * chunk, chunk), chunk), :]

    def send_x(c):
        return remote(rows_of(0, c), rows_of(0, c), sx.at[c], rx.at[c], at(2))

    def send_c(c):
        return remote(rows_of(0, c), rows_of(0, c), sc.at[c], rc.at[c], at(1))

    def forward(c):
        return remote(rows_of(2, c), rows_of(2, c), sf.at[c], rf.at[c], at(1))

    for c in range(count):
        send_x(c).start()
        send_c(c).start()
    idc_ref[...] = jnp.broadcast_to(idr_ref[...].astype(F32), (HP, length)).T.astype(jnp.int32)
    fac[...] = jnp.ones_like(fac)
    fac[0:1, :] = vec_ref[4:5, : heads * HP]

    def project(w, mask, c):
        low = pl.multiple_of(xor(mask) * rows + c * chunk, chunk)
        x = norm[pl.ds(low, chunk), :]
        y = mm(x, wpad[w], 1, 0)
        qkv[w, pl.ds(low, chunk), :] = (y * fac[pl.ds(w, 1), :]).astype(BF)

        @pl.when(w == 2)
        def _():
            normt[:, pl.ds(low, chunk)] = x.astype(F32).T.astype(BF)

    def rows_two(index):
        return pl.ds(pl.multiple_of(index * depth, 16), depth)

    def index_of(step, side):
        return source(step) * 2 + (minor if side == 0 else 1 - minor)

    def block_two(p, index):
        if p == 0:
            return both_out.at[0, rows_two(index), :]
        return wide_out.at[rows_two(index), pl.ds(0, 2 * cols)]

    def held_two(p, step, side):
        return pair.at[p] if step == 0 and side == 0 else block_two(p, index_of(step, side))

    def z_second(p, step):
        return remote(
            pair.at[p], block_two(p, me), sz2.at[p, step], rz2.at[p, step], along(step)
        )

    def y_second(p, step):
        return remote(
            held_two(p, step, 0), block_two(p, index_of(step, 0)),
            sy2.at[p, step], ry2.at[p, step], across,
        )

    def c_second(p, step, side):
        index = index_of(step, side)
        if p == 0:
            dst = both_out.at[2, rows_two(index), :]
        else:
            dst = wide_out.at[rows_two(index), pl.ds(2 * cols, 2 * cols)]
        return remote(
            held_two(p, step, side), dst, sc2.at[p, step, side], rc2.at[p, step, side], at(1)
        )

    def x_second(step, side):
        return remote(
            held_two(0, step, side), both_out.at[1, rows_two(index_of(step, side)), :],
            sx3.at[step, side], rx3.at[step, side], at(2),
        )

    def c_third(step, side):
        spot = rows_two(index_of(step, side))
        return remote(
            both_out.at[1, spot, :], both_out.at[3, spot, :],
            sc3.at[step, side], rc3.at[step, side], at(1),
        )

    def own_two(p):
        return pltpu.make_async_copy(pair.at[p], block_two(p, me), so.at[8 + p])

    def start_second(p):
        for step in range(1, far):
            z_second(p, step).start()
        y_second(p, 0).start()
        own_two(p).start()

    def spread(p, step, side):
        c_second(p, step, side).start()
        if p == 0:
            x_second(step, side).start()

    def after_z(p):
        for step in range(1, far):
            z_second(p, step).wait_recv()
            y_second(p, step).start()
            spread(p, step, 0)

    def after_y(p, step):
        y_second(p, step).wait_recv()
        spread(p, step, 1)

    if fused:
        start_second(0)
        spread(0, 0, 0)
        swap_two.wait_recv()
        for part in range(2):
            pair[1, part * packed : (part + 1) * packed, cols:] = x2[
                :, part * cols : (part + 1) * cols
            ]
        start_second(1)
        spread(1, 0, 0)

    if not fused:
        wpad[...] = wq_ref[...]
        for c in range(count):
            send_c(c).wait_recv()

        @pl.loop(0, 3)
        def _(w):
            @pl.loop(0, 2 * count)
            def _(j):
                project(w, j // count, lax.rem(j, count))

    else:
        wpad[...] = jnp.zeros_like(wpad)

        def unpack(w, block, device):
            for part in range(2):
                low = pl.multiple_of(device * depth + part * packed, 16)
                for h in range(heads):
                    lane = part * cols + h * HD
                    wpad[w, pl.ds(low, packed), h * HP : h * HP + HD] = block[:, lane : lane + HD]

        @pl.loop(0, 3)
        def _(w):
            unpack(w, w1_ref[w], me)

            @pl.loop(1, far)
            def _(step):
                z_first(w, step).wait_recv()
                y_first(w, step).start()
                unpack(w, z1[step, w], source(step) * 2 + minor)

            @pl.loop(0, far)
            def _(step):
                y_first(w, step).wait_recv()
                unpack(w, y1[step, w], source(step) * 2 + 1 - minor)

            @pl.when(w == 0)
            def _():
                for c in range(count):
                    send_c(c).wait_recv()

            @pl.loop(0, 2 * count)
            def _(j):
                project(w, j // count, lax.rem(j, count))

            @pl.when(w == 1)
            def _():
                after_y(0, 0)

        after_z(0)

    @pl.loop(0, count)
    def _(c):
        send_x(c).wait_recv()
        forward(c).start()

        @pl.loop(0, 3)
        def _(w):
            project(w, 2, c)

    @pl.loop(0, count)
    def _(c):
        forward(c).wait_recv()

        @pl.loop(0, 3)
        def _(w):
            project(w, 3, c)

    keep = [
        pltpu.make_async_copy(normt, normt_out, so.at[0]),
        pltpu.make_async_copy(wpad, wpad_out, so.at[1]),
        pltpu.make_async_copy(qkv, qkv_out, so.at[2]),
    ]
    for copy in keep:
        copy.start()

    def trade(h, mask):
        spot = pl.ds(pl.multiple_of((here ^ mask) * rows, HP), rows)
        return remote(
            att.at[h, :, spot], got.at[SLOT[mask], h], st_.at[mask, h], rt_.at[mask, h], at(mask)
        )

    sub = lax.broadcasted_iota(jnp.int32, (HP, length), 0)

    @pl.loop(0, heads)
    def _(h):
        lanes = pl.ds(pl.multiple_of(h * HP, HP), HP)
        vt_ref[...] = jnp.where(sub == HD, 1.0, qkv[2, :, lanes].astype(F32).T).astype(BF)

        def scores(t):
            seen, low = reach(t, length), t * TILE
            st = mm(qkv[1, :seen, lanes], qkv[0, low : low + TILE, lanes], 1, 1)
            visible = idc_ref[low:seen, 0:1] <= idr_ref[:, low : low + TILE]
            masked = jnp.where(visible, st[low:], MASKED)
            return jnp.concatenate([st[:low], masked], 0) if low else masked

        st = scores(0)
        for t in range(tiles):
            later = scores(t + 1) if t + 1 < tiles else None
            seen, low = st.shape[0], t * TILE
            group = jnp.max(st.reshape(seen // 64, 64, TILE), axis=0)
            highest = jnp.max(group, axis=0, keepdims=True)
            weights = jnp.exp(st - highest).astype(BF)
            ot = mm(vt_ref[:, :seen], weights, 1, 0)
            summed = ot[HD : HD + 1, :]
            att[h, :, low : low + TILE] = (ot[:HD] * (1.0 / summed)).astype(BF)
            lse_ref[h, :, low : low + TILE] = highest + jnp.log(summed)
            st = later
        for mask in PARTNERS:
            trade(h, mask).start()
        if fused:
            for n in range(heads):

                @pl.when(h == n)
                def _(n=n):
                    if n == 0:
                        after_y(0, 1)
                    if n == 1:
                        after_y(0, 2)
                        after_y(0, 3)
                    if n == 2:
                        after_z(1)
                        after_y(1, 0)

    got[0] = att[:, :, pl.ds(pl.multiple_of(here * rows, HP), rows)]
    keep.append(pltpu.make_async_copy(att, att_out, so.at[5]))
    keep[-1].start()
    if fused:
        for step in range(far):
            x_second(step, 0).wait_recv()
            c_third(step, 0).start()
        for step in range(1, far):
            after_y(1, step)
        for step in range(far):
            x_second(step, 1).wait_recv()
            c_third(step, 1).start()
    for h in range(heads):
        for mask in PARTNERS:
            trade(h, mask).wait_recv()
    keep.append(pltpu.make_async_copy(got, got_out, so.at[6]))
    keep[-1].start()

    for c in range(count):
        send_x(c).wait_send()
        send_c(c).wait_send()
        forward(c).wait_send()
    for h in range(heads):
        for mask in PARTNERS:
            trade(h, mask).wait_send()
    if fused:
        swap_two.wait_send()
        for w in range(3):
            for step in range(far):
                if step:
                    z_first(w, step).wait_send()
                y_first(w, step).wait_send()
        for p in range(2):
            own_two(p).wait()
            for step in range(far):
                if step:
                    z_second(p, step).wait_send()
                y_second(p, step).wait_send()
                for side in range(2):
                    c_second(p, step, side).wait()
                    if p == 0:
                        x_second(step, side).wait_send()
                        c_third(step, side).wait()
    for copy in keep:
        copy.wait()


def front(dp, far, tokens, vectors, idr, cols, matrices):
    rows, width = tokens.shape
    length = idr.shape[1]
    heads = cols // HD
    wide = heads * HP
    packed = width // dp // 2
    count = rows // TILE
    vmem = pl.BlockSpec(memory_space=pltpu.VMEM)
    hbm = pl.BlockSpec(memory_space=pl.ANY)
    sem = pltpu.SemaphoreType.DMA
    far_n = max(far, 1)
    fused = far > 0
    small = (packed, 2 * cols) if fused else (16, 128)
    return pl.pallas_call(
        lambda *refs: front_kernel(dp, far, *refs),
        out_shape=[
            jax.ShapeDtypeStruct((3, length, wide), BF),
            jax.ShapeDtypeStruct((width, length), BF),
            jax.ShapeDtypeStruct((3, width, wide), BF),
            jax.ShapeDtypeStruct((heads, HD, length), BF),
            jax.ShapeDtypeStruct((heads, 1, length), F32),
            jax.ShapeDtypeStruct((4, heads, HD, rows), BF),
            jax.ShapeDtypeStruct((4, width, 2 * cols) if fused else (16, 128), BF),
            jax.ShapeDtypeStruct((width, 4 * cols) if fused else (16, 128), BF),
        ],
        in_specs=[vmem] * 9,
        out_specs=[hbm] * 4 + [vmem] + [hbm] * 3,
        scratch_shapes=[
            pltpu.VMEM((length, width), BF),
            pltpu.VMEM((width, length), BF),
            pltpu.VMEM((3, width, wide), BF),
            pltpu.VMEM((3, length, wide), BF),
            pltpu.VMEM((heads, HD, length), BF),
            pltpu.VMEM((4, heads, HD, rows), BF),
            pltpu.VMEM((HP, length), BF),
            pltpu.VMEM((length, HP), jnp.int32),
            pltpu.VMEM((8, wide), F32),
            pltpu.VMEM((3,) + small, BF),
            pltpu.VMEM(small, BF),
            pltpu.VMEM((far_n, 3) + small, BF),
            pltpu.VMEM((far_n, 3) + small, BF),
            pltpu.VMEM(small, BF),
            pltpu.VMEM((2, 2 * packed, 2 * cols) if fused else (2, 16, 128), BF),
            sem((count,)), sem((count,)), sem((count,)), sem((count,)), sem((count,)), sem((count,)),
            sem((far_n, 3)), sem((far_n, 3)), sem((far_n, 3)), sem((far_n, 3)),
            sem, sem,
            sem((2, far_n)), sem((2, far_n)), sem((2, far_n)), sem((2, far_n)),
            sem((2, far_n, 2)), sem((2, far_n, 2)),
            sem((far_n, 2)), sem((far_n, 2)), sem((far_n, 2)), sem((far_n, 2)),
            sem((4, heads)), sem((4, heads)),
            sem((12,)),
        ],
        compiler_params=pltpu.CompilerParams(
            vmem_limit_bytes=60 << 20, collective_id=1, has_side_effects=True
        ),
    )(tokens, vectors, idr, *matrices)


def mid_kernel(
    tok_ref, cot_ref, got_ref, vec_ref, wide_ref, both_ref,
    out_ref, dhid_ref, drec_out, xk_out, xg_out, pb_out, early_ref,
    w, both, att, n2, act, dpre, branch, hid, give, grec, db, drec, kept, bs,
    ss, rs, sg, rg, so,
):
    here, me = lax.axis_index("tensor"), lax.axis_index("dp")
    rows, width = tok_ref.shape
    wide = w.shape[1]
    cols = wide // 4
    pair = 2 * cols
    chunk = TILE
    half = chunk // 2
    count = rows // chunk

    def at(mask):
        return (me, here ^ mask)

    loads = [
        pltpu.make_async_copy(both_ref, both, so.at[1]),
        pltpu.make_async_copy(wide_ref, w.at[0], so.at[0]),
    ]
    for copy in loads:
        copy.start()
    greet([at(mask) for mask in PARTNERS])
    att[...] = got_ref[...].astype(F32).T.astype(BF)
    early_ref[...] = jnp.zeros_like(early_ref)
    bs[...] = jnp.zeros_like(bs)
    loads[0].wait()

    @pl.loop(0, width // chunk)
    def _(j):
        spot = pl.ds(pl.multiple_of(j * chunk, chunk), chunk)
        for i in range(4):
            w[1, spot, i * cols : (i + 1) * cols] = both[i, spot, :cols]
            w[2, spot, i * cols : (i + 1) * cols] = both[i, spot, cols:]

    loads[1].wait()

    def trade(c, mask):
        return remote(
            db.at[c, SLOT[mask]], drec.at[c, SLOT[mask]],
            ss.at[c, mask], rs.at[c, mask], at(mask),
        )

    @pl.loop(0, count)
    def _(c):
        low = pl.multiple_of(c * chunk, chunk)
        spot = pl.ds(low, chunk)
        hidden = tok_ref[spot, :].astype(F32) + mm(att[spot, :], w[0], 1, 1)
        hid[spot, :] = hidden
        cot = cot_ref[spot, :]
        d_act = mm(cot, w[2], 1, 0)
        inverse = lax.rsqrt(jnp.mean(hidden * hidden, axis=-1, keepdims=True) + EPSILON)
        hat = hidden * inverse
        normed = (hat * vec_ref[1:2, :]).astype(BF)
        n2[spot, :] = normed
        pre = mm(normed, w[1], 1, 0) + vec_ref[2:3, :]
        sig = jax.nn.sigmoid(pre)
        act[spot, :] = (pre * sig).astype(BF)
        d_pre = (d_act * sig * (1.0 + pre * (1.0 - sig))).astype(BF)
        dpre[spot, :] = d_pre
        d_n2 = mm(d_pre, w[1], 1, 1)
        scaled = d_n2 * vec_ref[1:2, :]
        cot_f32 = cot.astype(F32)
        d_hidden = cot_f32 + inverse * (
            scaled - hat * jnp.mean(scaled * hat, axis=-1, keepdims=True)
        )
        dhid_ref[spot, :] = d_hidden
        br = d_hidden.astype(BF)
        branch[spot, :] = br
        d_att = mm(br, w[0], 1, 0).astype(BF)
        for i in range(4):
            for part in range(2):
                db[c, i, :, part * cols : (part + 1) * cols] = d_att[
                    part * half : (part + 1) * half, i * cols : (i + 1) * cols
                ]
        for mask in PARTNERS:
            trade(c, mask).start()
        drec[c, 0] = db[c, 0]
        early_ref[0:1, :] += jnp.sum(d_n2 * hat, axis=0, keepdims=True)
        early_ref[1:2, :] += jnp.sum(cot_f32, axis=0, keepdims=True)
        bs[0:1, :] += jnp.sum(d_pre.astype(F32), axis=0, keepdims=True)

    pieces = ((branch, att), (n2, dpre), (cot_ref, act))

    def hand(i):
        return remote(give.at[i], grec.at[i], sg.at[i], rg.at[i], at(1))

    for i in range(3):

        @pl.loop(0, width // chunk)
        def _(j):
            spot = pl.ds(pl.multiple_of(j * chunk, chunk), chunk)
            left, right = pieces[i]
            g = mm(left[:, spot], right[...], 0, 0).astype(BF)
            give[i, spot, :] = g[:, pair:]
            if i == 0:
                kept[2, spot, :] = g[:, :pair]
            else:
                lane = (i - 1) * cols
                kept[0, spot, lane : lane + cols] = g[:, :cols]
                kept[1, spot, lane : lane + cols] = g[:, cols:pair]

        hand(i).start()

    for i in range(4):
        place = here ^ (0, 2, 1, 3)[i]
        early_ref[pl.ds(2 + place, 1), 0:cols] = bs[0:1, i * cols : (i + 1) * cols]

    @pl.loop(0, count)
    def _(c):
        spot = pl.ds(pl.multiple_of(c * chunk, chunk), chunk)
        out_ref[spot, :] = (hid[spot, :] + mm(act[spot, :], w[2], 1, 1) + vec_ref[3:4, :]).astype(BF)

    for i in range(3):
        hand(i).wait_recv()

        @pl.loop(0, width // chunk)
        def _(j):
            spot = pl.ds(pl.multiple_of(j * chunk, chunk), chunk)
            came = grec[i, spot, :]
            if i == 0:
                kept[2, spot, :] += came
            else:
                lane = (i - 1) * cols
                kept[0, spot, lane : lane + cols] += came[:, :cols]
                kept[1, spot, lane : lane + cols] += came[:, cols:]

        if i == 0:
            keep = [pltpu.make_async_copy(kept.at[2], pb_out, so.at[3])]
            keep[0].start()
    keep.append(pltpu.make_async_copy(kept.at[0], xk_out, so.at[4]))
    keep.append(pltpu.make_async_copy(kept.at[1], xg_out, so.at[5]))
    for copy in keep[1:]:
        copy.start()
    for c in range(count):
        for mask in PARTNERS:
            trade(c, mask).wait_recv()
    keep.append(pltpu.make_async_copy(drec, drec_out, so.at[6]))
    keep[-1].start()
    for c in range(count):
        for mask in PARTNERS:
            trade(c, mask).wait_send()
    for i in range(3):
        hand(i).wait_send()
    for copy in keep:
        copy.wait()


def middle(tokens, cotangent, got, vectors, wide, both):
    rows, width = tokens.shape
    all_cols = wide.shape[1]
    cols = all_cols // 4
    count = rows // TILE
    vmem = pl.BlockSpec(memory_space=pltpu.VMEM)
    hbm = pl.BlockSpec(memory_space=pl.ANY)
    sem = pltpu.SemaphoreType.DMA
    blocks = (count, 4, TILE // 2, 2 * cols)
    halves = jax.ShapeDtypeStruct((width, 2 * cols), BF)
    return pl.pallas_call(
        mid_kernel,
        out_shape=[
            jax.ShapeDtypeStruct((rows, width), BF),
            jax.ShapeDtypeStruct((rows, width), F32),
            jax.ShapeDtypeStruct(blocks, BF),
            halves,
            halves,
            halves,
            jax.ShapeDtypeStruct((16, width), F32),
        ],
        in_specs=[vmem] * 4 + [hbm] * 2,
        out_specs=[vmem, vmem, hbm, hbm, hbm, hbm, vmem],
        scratch_shapes=[
            pltpu.VMEM((3, width, all_cols), BF),
            pltpu.VMEM((4, width, 2 * cols), BF),
            pltpu.VMEM((rows, all_cols), BF),
            pltpu.VMEM((rows, width), BF),
            pltpu.VMEM((rows, all_cols), BF),
            pltpu.VMEM((rows, all_cols), BF),
            pltpu.VMEM((rows, width), BF),
            pltpu.VMEM((rows, width), F32),
            pltpu.VMEM((3, width, 2 * cols), BF),
            pltpu.VMEM((3, width, 2 * cols), BF),
            pltpu.VMEM(blocks, BF),
            pltpu.VMEM(blocks, BF),
            pltpu.VMEM((3, width, 2 * cols), BF),
            pltpu.VMEM((8, all_cols), F32),
            sem((count, 4)), sem((count, 4)), sem((3,)), sem((3,)), sem((8,)),
        ],
        compiler_params=pltpu.CompilerParams(
            vmem_limit_bytes=60 << 20, collective_id=2, has_side_effects=True
        ),
    )(tokens, cotangent, got, vectors, wide, both)


def back_kernel(
    dp, far, o_ref, lse_ref, drec_ref, vec_ref, idr_ref, xk_ref, early_ref,
    qkv_hbm, xg_ref, pb_ref, tok_hbm, dhid_hbm, normt_hbm, wpad_hbm,
    dtok_ref, dq_out, dk_out, dv_out, dout_ref, dup_ref, ddown_ref, sums_ref,
    do, dka, dva, kt_ref, idc_ref, dqkv, tok, dhid, normt, wpad,
    xrec, pbown, yrec, zrec, last, lastsend, lastrec,
    gpay, gyrec, gzrec, ownsum, near, fo, crec, fs, frec, nrec, qsum, lvec, ar, arec, aorder, er, erec, eorder,
    so, sxa, rxa, sy, ry, sz, rz, sl, rl, sgy, rgy, sgz, rgz, sfo, rfo, sfs, rfs, sno, rno, sar, rar, ser, rer,
):
    here, me = lax.axis_index("tensor"), lax.axis_index("dp")
    heads, _, length = o_ref.shape
    rows, width = tok.shape
    cols = heads * HD
    tiles = length // TILE
    depth = width // dp
    packed = depth // 2
    fused = far > 0
    major, minor = me // 2, me % 2
    chunk = TILE
    count = rows // chunk

    def at(mask):
        return (me, here ^ mask)

    across = (me ^ 1, here)

    def along(step):
        return (lax.rem(major + step, far) * 2 + minor, here)

    def target(step):
        return lax.rem(major + step, far)

    loads = [
        pltpu.make_async_copy(src, dst, so.at[i])
        for i, (src, dst) in enumerate(
            ((wpad_hbm, wpad), (normt_hbm, normt), (tok_hbm, tok), (dhid_hbm, dhid))
        )
    ]
    load_qkv = pltpu.make_async_copy(qkv_hbm, dqkv, so.at[4])
    load_qkv.start()
    if fused:
        load_pb = pltpu.make_async_copy(pb_ref.at[:, minor], pbown, so.at[5])
        load_pb.start()
    for copy in loads:
        copy.start()
    peers = [at(2), at(1)]
    if fused:
        peers += [across] + [along(step) for step in range(1, far)]
    greet(peers)

    turn = list(range(1, far)) + [0]

    def x_send(step):
        spot = target(step)
        return remote(xg_ref.at[spot], xrec.at[spot], sxa.at[step], rxa.at[step], at(2))

    def y_send(p, step):
        spot = target(step)
        src = xrec.at[spot, 1 - minor] if p == 0 else pb_ref.at[spot, 1 - minor]
        return remote(src, yrec.at[p, spot], sy.at[p, step], ry.at[p, step], across)

    def z_send(p, step):
        return remote(
            yrec.at[p, target(step)], zrec.at[p, step - 1],
            sz.at[p, step], rz.at[p, step], along(step),
        )

    def after_x(step):
        x_send(step).wait_recv()
        spot = target(step)
        xrec[spot] = xk_ref[spot] + xrec[spot]
        y_send(0, step).start()

    def after_y(p, step):
        y_send(p, step).wait_recv()
        spot = target(step)
        mine = xrec[spot, minor] if p == 0 else pbown[spot]

        @pl.when(step != 0)
        def _():
            yrec[p, spot] = mine + yrec[p, spot]
            z_send(p, step).start()

        @pl.when(step == 0)
        def _():
            last[p] = mine.astype(F32) + yrec[p, spot].astype(F32)

    def after_z(p):
        for step in range(1, far):
            z_send(p, step).wait_recv()
            last[p] += zrec[p, step - 1].astype(F32)

    def e_hop(n, where):
        return remote(er.at[n], erec.at[n], ser.at[n], rer.at[n], where)

    def e_last():
        return remote(er.at[3], erec.at[2], ser.at[2], rer.at[2], at(2))

    def e_z(step):
        return remote(er.at[2], erec.at[3 + step], ser.at[3 + step], rer.at[3 + step], along(step))

    def early_hop(h):
        @pl.when(h == 0)
        def _():
            e_hop(0, at(1)).wait_recv()
            er[1] = er[0] + erec[0]
            e_hop(1, across).start()

        @pl.when(h == 1)
        def _():
            e_hop(1, across).wait_recv()
            er[2] = er[1] + erec[1]
            for step in range(1, far):
                e_z(step).start()

        @pl.when(h == 2)
        def _():
            eorder[major] = er[2]
            for step in range(1, far):
                e_z(step).wait_recv()
                eorder[lax.rem(major + far - step, far)] = erec[3 + step]
            er[3] = (eorder[0] + eorder[1]) + (eorder[2] + eorder[3])
            e_last().start()

    if fused:
        er[0] = early_ref[0:8, :]
        e_hop(0, at(1)).start()
        for step in turn:
            x_send(step).start()
            y_send(1, step).start()

    do[...] = jnp.zeros_like(do)
    half = chunk // 2
    for c in range(count):
        for i, mask in enumerate((0, 2, 1, 3)):
            block = drec_ref[c, i]
            for part in range(2):
                low = pl.multiple_of((here ^ mask) * rows + c * chunk + part * half, half)
                for h in range(heads):
                    lane = part * cols + h * HD
                    do[h, pl.ds(low, half), 0:HD] = block[:, lane : lane + HD]
    qsum[...] = jnp.zeros_like(qsum)
    if fused:
        gpay[...] = jnp.zeros_like(gpay)
    idc_ref[...] = jnp.broadcast_to(idr_ref[...].astype(F32), (HP, length)).T.astype(jnp.int32)

    load_qkv.wait()
    if fused:
        load_pb.wait()

    def one_head(h):
        lanes = pl.ds(pl.multiple_of(h * HP, HP), HP)
        kt_ref[...] = dqkv[1, :, lanes].astype(F32).T.astype(BF)
        dka[...] = jnp.zeros_like(dka)
        dva[...] = jnp.zeros_like(dva)
        scale_sum = jnp.zeros((1, HP), F32)
        for t in range(tiles):
            seen, low = reach(t, length), t * TILE
            spot = slice(low, low + TILE)
            qt = dqkv[0, spot, lanes]
            dot_ = do[h, spot, :]
            delta = jnp.sum(
                dot_.astype(F32).T[:HD] * o_ref[h, :, spot].astype(F32), axis=0, keepdims=True
            )
            st = mm(dqkv[1, :seen, lanes], qt, 1, 1)
            p = jnp.exp(st - lse_ref[h, :, spot])
            visible = idc_ref[low:seen, 0:1] <= idr_ref[:, spot]
            pm = jnp.where(visible, p[low:], 0.0)
            p = jnp.concatenate([p[:low], pm], 0) if low else pm
            d_p = mm(dqkv[2, :seen, lanes], dot_, 1, 1)
            ds = (p * (d_p - delta)).astype(BF)
            dva[:seen, :] += mm(p.astype(BF), dot_, 1, 0)
            dka[:seen, :] += mm(ds, qt, 1, 0)
            dq = mm(kt_ref[:, :seen], ds, 1, 0).T
            scale_sum = scale_sum + jnp.sum(dq * qt.astype(F32), axis=0, keepdims=True)
            dqkv[0, spot, lanes] = (dq * vec_ref[4:5, :HP]).astype(BF)
        dqkv[1, :, lanes] = dka[...].astype(BF)
        dqkv[2, :, lanes] = dva[...].astype(BF)
        qsum[0:1, :] += scale_sum

    group = 2 * HD

    def weight_blocks(n, step):
        spot = target(step)
        low = pl.multiple_of(spot * 2 * depth, 16)
        lanes = slice(n * 2 * HP, (n + 1) * 2 * HP)
        dots = jnp.zeros((2 * depth, 1), F32)
        for i in range(3):
            g = mm(normt[pl.ds(low, 2 * depth), :], dqkv[i, :, lanes], 1, 0)
            dots = dots + jnp.sum(
                g * wpad[i, pl.ds(low, 2 * depth), lanes].astype(F32), axis=1, keepdims=True
            )
            g = g.astype(BF)
            for side in range(2):
                for h in range(2):
                    lane = i * group + h * HD
                    gpay[n, spot, side, :, lane : lane + HD] = g[
                        side * depth : (side + 1) * depth, h * HP : h * HP + HD
                    ]
        flat = jnp.broadcast_to(dots, (2 * depth, HP)).T[0:1, :]
        lvec[n, pl.ds(spot * 2, 1), :] = flat[:, :depth]
        lvec[n, pl.ds(spot * 2 + 1, 1), :] = flat[:, depth:]

    def gy_send(n, step):
        spot = target(step)
        return remote(
            gpay.at[n, spot, 1 - minor], gyrec.at[n, spot], sgy.at[n, step], rgy.at[n, step], across
        )

    def gz_send(n, step):
        return remote(
            gyrec.at[n, target(step)], gzrec.at[n, step - 1],
            sgz.at[n, step], rgz.at[n, step], along(step),
        )

    def weight_pair(n):
        @pl.loop(0, far)
        def _(j):
            step = lax.rem(j + 1, far)
            weight_blocks(n, step)
            gy_send(n, step).start()

    def gz_start(n, step):
        gy_send(n, step).wait_recv()
        spot = target(step)
        mine = gpay[n, spot, minor]

        @pl.when(step != 0)
        def _():
            gyrec[n, spot] = mine + gyrec[n, spot]
            gz_send(n, step).start()

        @pl.when(step == 0)
        def _():
            ownsum[n] = mine.astype(F32) + gyrec[n, spot].astype(F32)

    @pl.loop(0, heads)
    def _(h):
        one_head(h)
        if fused:
            early_hop(h)
            after_x(lax.rem(h + 1, far))

            @pl.when(h < 2)
            def _():
                @pl.loop(0, 2)
                def _(k):
                    after_y(1, lax.rem(2 * h + k + 1, far))

            @pl.when(h == 1)
            def _():
                for copy in loads[:2]:
                    copy.wait()
                weight_pair(0)

            @pl.when(h > 0)
            def _():
                after_y(0, h)

    if not fused:
        for copy in loads[:2]:
            copy.wait()

    def part(mask, c):
        spot = pl.ds(pl.multiple_of((here ^ mask) * rows + c * chunk, chunk), chunk)
        total = mm(dqkv[0, spot, :], wpad[0], 1, 1)
        total = total + mm(dqkv[1, spot, :], wpad[1], 1, 1)
        return total + mm(dqkv[2, spot, :], wpad[2], 1, 1)

    def c_far(c):
        return remote(fo.at[c], crec.at[c], sfo.at[c], rfo.at[c], at(1))

    def x_far(c):
        return remote(fs.at[c], frec.at[c], sfs.at[c], rfs.at[c], at(2))

    def c_near(c):
        return remote(fo.at[c], nrec.at[c], sno.at[c], rno.at[c], at(1))

    def far_chunk(c):
        fo[c] = part(3, c).astype(BF)
        c_far(c).start()

    def far_sum(c):
        own = part(2, c)
        c_far(c).wait_recv()
        fs[c] = (own + crec[c].astype(F32)).astype(BF)

    def hop(n, where):
        return remote(ar.at[n], arec.at[n], sar.at[n], rar.at[n], where)

    def z_hop(step):
        return remote(ar.at[3], arec.at[3 + step], sar.at[3 + step], rar.at[3 + step], along(step))

    if fused:
        for c in range(count):
            far_chunk(c)
        far_sum(0)
        x_far(0).start()

        @pl.loop(0, far)
        def _(j):
            gz_start(0, lax.rem(j + 1, far))

        after_y(0, turn[far - 1])
        weight_pair(1)
        for index in range(dp):
            spot = slice(index * depth, (index + 1) * depth)
            ar[0, :, spot] = lvec[0, index : index + 1, :] + lvec[1, index : index + 1, :]
        ar[0, :, width:] = qsum[0:1, :]
        hop(0, at(1)).start()

        @pl.loop(1, 3)
        def _(step):
            gz_start(1, step)

        hop(0, at(1)).wait_recv()
        ar[1] = ar[0] + arec[0]
        hop(1, at(2)).start()
        for c in range(1, count):
            far_sum(c)
            x_far(c).start()
        after_z(1)
        for piece in range(2):
            last_half = last[1, piece * packed : (piece + 1) * packed, cols:]
            lastsend[:, piece * cols : (piece + 1) * cols] = last_half.astype(BF)
        cross = remote(lastsend, lastrec, sl, rl, at(2))
        cross.start()
    else:
        for c in range(count):
            far_chunk(c)
            far_sum(c)
            x_far(c).start()

        @pl.loop(0, 3)
        def _(i):
            for j in range(width // chunk):
                dq_out[i, j * chunk : (j + 1) * chunk, :] = mm(
                    normt[j * chunk : (j + 1) * chunk, :], dqkv[i], 1, 0
                )

    if not fused:
        sums_ref[...] = jnp.zeros_like(sums_ref)
        sums_ref[0:6, :] = early_ref[0:6, :]
        sums_ref[6:7, 0:HP] = qsum[0:1, :]

    @pl.loop(0, count)
    def _(c):
        c_far(c).wait_send()
        fo[c] = part(1, c).astype(BF)
        c_near(c).start()

    if fused:

        @pl.loop(0, 2)
        def _(j):
            gz_start(1, lax.rem(j + 3, far))

        hop(1, at(2)).wait_recv()
        ar[2] = ar[1] + arec[1]
        hop(2, across).start()
        after_z(0)
        dup_ref[...] = last[0, :, :cols]
        ddown_ref[...] = last[0, :, cols:]
    for copy in loads[2:]:
        copy.wait()

    @pl.loop(0, count)
    def _(c):
        near[c] = part(0, c)

    if fused:
        hop(2, across).wait_recv()
        ar[3] = ar[2] + arec[2]
        for step in range(1, far):
            z_hop(step).start()
        cross.wait_recv()
        arrived = jnp.concatenate([lastrec[:, :cols], lastrec[:, cols:]], axis=0)
        dout_ref[...] = last[1, :, :cols] + arrived.astype(F32)

    @pl.loop(0, count)
    def _(c):
        c_near(c).wait_recv()
        x_far(c).wait_recv()
        d_normed = near[c] + nrec[c].astype(F32) + frec[c].astype(F32)
        spot = pl.ds(pl.multiple_of(c * chunk, chunk), chunk)
        v = tok[spot, :].astype(F32)
        inverse = lax.rsqrt(jnp.mean(v * v, axis=-1, keepdims=True) + EPSILON)
        hat = v * inverse
        scaled = d_normed * vec_ref[0:1, :]
        dtok_ref[spot, :] = (
            dhid[spot, :]
            + inverse * (scaled - hat * jnp.mean(scaled * hat, axis=-1, keepdims=True))
        ).astype(BF)

    if fused:
        for n in range(2):
            for step in range(1, far):
                gz_send(n, step).wait_recv()
                ownsum[n] += gzrec[n, step - 1].astype(F32)
            for i, ref in enumerate((dq_out, dk_out, dv_out)):
                ref[:, n * group : (n + 1) * group] = ownsum[n, :, i * group : (i + 1) * group]
        aorder[major] = ar[3]
        for step in range(1, far):
            z_hop(step).wait_recv()
            aorder[lax.rem(major + far - step, far)] = arec[3 + step]
        total = (aorder[0] + aorder[1]) + (aorder[2] + aorder[3])
        e_last().wait_recv()
        sums_ref[...] = jnp.zeros_like(sums_ref)
        sums_ref[0:8, :] = er[3] + erec[2]
        sums_ref[6:7, 0:HP] = total[:, width:]
        sums_ref[7:8, :] = total[:, :width]
    else:
        dk_out[...] = jnp.zeros_like(dk_out)
        dv_out[...] = jnp.zeros_like(dv_out)
        dout_ref[...] = jnp.zeros_like(dout_ref)
        dup_ref[...] = jnp.zeros_like(dup_ref)
        ddown_ref[...] = jnp.zeros_like(ddown_ref)

    for c in range(count):
        x_far(c).wait_send()
        c_near(c).wait_send()
    if fused:
        for step in range(far):
            x_send(step).wait_send()
            for p in range(2):
                gy_send(p, step).wait_send()
                y_send(p, step).wait_send()
            if step:
                gz_send(0, step).wait_send()
                gz_send(1, step).wait_send()
                z_hop(step).wait_send()
                e_z(step).wait_send()
                for p in range(2):
                    z_send(p, step).wait_send()
        cross.wait_send()
        hop(0, at(1)).wait_send()
        hop(1, at(2)).wait_send()
        hop(2, across).wait_send()
        e_hop(0, at(1)).wait_send()
        e_hop(1, across).wait_send()
        e_last().wait_send()


def backward(dp, far, o, lse, drec, vectors, idr, xk, early, qkv, xg, pb,
             tokens, d_hidden, normt, wpad):
    heads, _, length = o.shape
    rows, width = tokens.shape
    cols, wide = heads * HD, heads * HP
    depth = width // dp
    packed = depth // 2
    count = rows // TILE
    fused = far > 0
    far_n = max(far, 1)
    vmem = pl.BlockSpec(memory_space=pltpu.VMEM)
    hbm = pl.BlockSpec(memory_space=pl.ANY)
    sem = pltpu.SemaphoreType.DMA
    tiny = jax.ShapeDtypeStruct((8, 128), F32)
    shard = jax.ShapeDtypeStruct((depth, cols), F32) if fused else tiny
    whole = shard if fused else jax.ShapeDtypeStruct((3, width, wide), F32)

    def buf(*shape, dtype=BF, only=True):
        return pltpu.VMEM(shape if fused or not only else (8, 128), dtype)

    pair = 2 * cols
    return pl.pallas_call(
        lambda *refs: back_kernel(dp, far, *refs),
        out_shape=[jax.ShapeDtypeStruct((rows, width), BF), whole, shard, shard, shard, shard,
                   shard, jax.ShapeDtypeStruct((16, width), F32)],
        in_specs=[vmem] * 7 + [hbm] * 7,
        out_specs=[vmem] * 8,
        scratch_shapes=[
            buf(heads, length, HP, only=False),
            buf(length, HP, dtype=F32, only=False),
            buf(length, HP, dtype=F32, only=False),
            buf(HP, length, only=False),
            buf(length, HP, dtype=jnp.int32, only=False),
            buf(3, length, wide, only=False),
            buf(rows, width, only=False),
            buf(rows, width, dtype=F32, only=False),
            buf(width, length, only=False),
            buf(3, width, wide, only=False),
            buf(far_n, 2, depth, pair),
            buf(far_n, depth, pair),
            buf(2, far_n, depth, pair),
            buf(2, far_n - 1, depth, pair),
            buf(2, depth, pair, dtype=F32),
            buf(packed, pair),
            buf(packed, pair),
            buf(2, far_n, 2, depth, 4 * HP),
            buf(2, far_n, depth, 4 * HP),
            buf(2, far_n - 1, depth, 4 * HP),
            buf(2, depth, 4 * HP, dtype=F32),
            buf(count, TILE, width, dtype=F32, only=False),
            buf(count, TILE, width, only=False),
            buf(count, TILE, width, only=False),
            buf(count, TILE, width, only=False),
            buf(count, TILE, width, only=False),
            buf(count, TILE, width, only=False),
            buf(8, HP, dtype=F32, only=False),
            buf(2, dp, depth, dtype=F32),
            buf(4, 1, width + HP, dtype=F32),
            buf(3 + far_n, 1, width + HP, dtype=F32),
            buf(far_n, 1, width + HP, dtype=F32),
            buf(4, 8, width, dtype=F32),
            buf(3 + far_n, 8, width, dtype=F32),
            buf(far_n, 8, width, dtype=F32),
            sem((6,)),
            sem((far_n,)), sem((far_n,)),
            sem((2, far_n)), sem((2, far_n)), sem((2, far_n)), sem((2, far_n)),
            sem, sem,
            sem((2, far_n)), sem((2, far_n)), sem((2, far_n)), sem((2, far_n)),
            sem((count,)), sem((count,)), sem((count,)), sem((count,)), sem((count,)), sem((count,)),
            sem((3 + far_n,)), sem((3 + far_n,)), sem((3 + far_n,)), sem((3 + far_n,)),
        ],
        compiler_params=pltpu.CompilerParams(
            vmem_limit_bytes=62 << 20, collective_id=3, has_side_effects=True
        ),
    )(o, lse, drec, vectors, idr, xk, early, qkv, xg, pb,
      tokens, d_hidden, normt, wpad)


def finish_kernel(cols, sums_ref, vec_ref, *refs):
    moves, outs, held = refs[:8], refs[8:21], refs[21:29]
    row, sem = refs[29:]
    width = vec_ref.shape[1]
    places = (0, 1, 3, 4, 5, 7, 9, 11)
    enter = [pltpu.make_async_copy(moves[i], held[i], sem.at[i]) for i in range(8)]
    leave = [pltpu.make_async_copy(held[i], outs[places[i]], sem.at[8 + i]) for i in range(8)]
    for copy in enter:
        copy.start()
    outs[6][...] = sums_ref[6, 0:HP] * vec_ref[5, 0:HP]
    outs[8][...] = sums_ref[0, :]
    outs[12][...] = sums_ref[1, :]
    row[...] = jnp.zeros_like(row)
    for i in range(width // cols):
        row[0:1, i * cols : (i + 1) * cols] = sums_ref[2 + i : 3 + i, :cols]
    row[1:2, :] = sums_ref[7:8, :] / vec_ref[0:1, :]
    outs[10][...] = row[0, :]
    outs[2][...] = row[1, :]
    for come, go in zip(enter, leave):
        come.wait()
        go.start()
    for copy in leave:
        copy.wait()


def finish(cols, sums, vectors, moves):
    width = vectors.shape[1]
    vmem = pl.BlockSpec(memory_space=pltpu.VMEM)
    hbm = pl.BlockSpec(memory_space=pl.ANY)
    row = jax.ShapeDtypeStruct((width,), F32)
    like = [jax.ShapeDtypeStruct(v.shape, v.dtype) for v in moves]
    shapes = like[:2] + [row] + like[2:5] + [jax.ShapeDtypeStruct((HP,), F32)]
    shapes += [like[5], row, like[6], row, like[7], row]
    small = (2, 6, 8, 10, 12)
    return pl.pallas_call(
        lambda *refs: finish_kernel(cols, *refs),
        out_shape=shapes,
        in_specs=[vmem] * 2 + [hbm] * 8,
        out_specs=[vmem if i in small else hbm for i in range(13)],
        scratch_shapes=[pltpu.VMEM(v.shape, v.dtype) for v in moves]
        + [pltpu.VMEM((8, width), F32), pltpu.SemaphoreType.DMA((16,))],
        compiler_params=pltpu.CompilerParams(vmem_limit_bytes=60 << 20),
    )(sums, vectors, *moves)


def swap(v, axis, size, mask):
    return lax.ppermute(v, axis, [(i, i ^ mask) for i in range(size)])


def gather_dp(shard):
    return lax.all_gather(shard, "dp", axis=0, tiled=True)


def scatter_dp(grad, size):
    return lax.psum_scatter(grad, "dp", scatter_dimension=0, tiled=True)


def pad_heads(w):
    rows, cols = w.shape
    w = w.reshape(rows, cols // HD, HD)
    return jnp.pad(w, ((0, 0), (0, 0), (0, HP - HD))).reshape(rows, cols // HD * HP)


def trim_heads(w):
    rows, cols = w.shape
    return w.reshape(rows, cols // HP, HP)[:, :, :HD].reshape(rows, cols // HP * HD)


def body(dp, tensor, tokens, cotangent, block_ids, attn_gain, w_query, w_key, w_value,
         query_scale, w_out, mlp_gain, w_up, b_up, w_down, b_down):
    assert tensor == 4
    here = lax.axis_index("tensor")
    rows, width = tokens.shape
    length = rows * tensor
    cols = w_query.shape[1]
    heads = cols // HD
    order = [here, here ^ 2, here ^ 1, here ^ 3]

    softplus = jnp.log1p(jnp.exp(query_scale))
    factor = jnp.pad(SCORE_BASE / math.sqrt(HD) * softplus, (0, HP - HD))
    b_rel = jnp.concatenate([lax.dynamic_slice(b_up, (at * cols,), (cols,)) for at in order])
    repeat = jnp.pad(jnp.tile(factor, heads), (0, width - heads * HP))
    slope = jax.nn.sigmoid(query_scale) / softplus
    vectors = jnp.concatenate(
        [attn_gain, mlp_gain, b_rel, b_down, repeat, jnp.pad(slope, (0, width - HD))]
    ).reshape(6, width)

    far = dp // 2 if dp == 8 else 0
    matrices = (w_query, w_key, w_value, w_out.T, w_up, w_down.T)
    if not far:
        pair = [jnp.concatenate([w, swap(w, "tensor", tensor, 2)], axis=1) for w in matrices[3:]]
        half = gather_dp(jnp.concatenate(pair, axis=1)).reshape(width, 3, 2 * cols)
        both = jnp.concatenate([half, swap(half, "tensor", tensor, 1)], axis=2)
        full = gather_dp(jnp.concatenate(matrices[:3], axis=1))
        first = jnp.stack([pad_heads(full[:, i * cols : (i + 1) * cols]) for i in range(3)])
        matrices = (first,) + matrices[1:]
    qkv, normed_t, padded, attended, lse, got, pairs, wide = front(
        dp, far, tokens, vectors, block_ids, cols, matrices
    )
    if not far:
        wide = both[:, 0]
        pairs = both[:, 1:].reshape(width, 2, 4, cols).transpose(2, 0, 1, 3)
        pairs = pairs.reshape(4, width, 2 * cols)

    output, d_hidden, received, xk, xg, pb, early = middle(
        tokens, cotangent, got.reshape(4 * cols, rows), vectors, wide, pairs
    )
    depth = width // dp
    if far:
        xk, xg, pb = (v.reshape(far, 2, depth, 2 * cols) for v in (xk, xg, pb))
    d_tokens, s_q, s_k, s_v, s_out, s_up, s_down, sums = backward(
        dp, far, attended, lse, received, vectors, block_ids, xk, early,
        qkv, xg, pb, tokens, d_hidden, normed_t, padded,
    )
    if far:
        final = list(
            finish(
                cols, sums, vectors,
                (output, d_tokens, s_q, s_k, s_v, s_out, s_up, s_down),
            )
        )
        final[6] = final[6][:HD]
        final[7], final[11] = final[7].T, final[11].T
        return tuple(final)
    else:
        dots = lax.psum(jnp.sum(s_q * padded.astype(F32), axis=(0, 2)), ("dp", "tensor"))
        sums = lax.psum(sums, ("dp", "tensor"))
        s_qkv = scatter_dp(jnp.concatenate([trim_heads(g) for g in s_q], axis=1), dp)
        s_q, s_k, s_v = (s_qkv[:, i * cols : (i + 1) * cols] for i in range(3))
        both = xk.astype(F32) + swap(xg, "tensor", tensor, 2).astype(F32)
        both = scatter_dp(both, dp)
        s_up, s_down = both[:, :cols], both[:, cols:].T
        both = scatter_dp(pb.astype(F32), dp)
        s_out = (both[:, :cols] + swap(both[:, cols:], "tensor", tensor, 2)).T
    d_scale = sums[6, :HD] * slope
    return (
        output,
        d_tokens,
        dots / attn_gain,
        s_q,
        s_k,
        s_v,
        d_scale,
        s_out,
        sums[0],
        s_up,
        sums[2:6, :cols].reshape(4 * cols),
        s_down,
        sums[1],
    )


def solution(mesh):
    weight, turned, whole = P("dp", "tensor"), P("tensor", "dp"), P()
    positions = P(("dp", "tensor"), None)
    return jax.shard_map(
        lambda *args: body(mesh.shape["dp"], mesh.shape["tensor"], *args),
        mesh=mesh,
        in_specs=(positions, positions, P("dp", None), whole, weight, weight, weight, whole,
                  turned, whole, weight, whole, turned, whole),
        out_specs=(positions, positions, whole, weight, weight, weight, whole, turned, whole,
                   weight, whole, turned, whole),
        check_vma=False,
    )
```
